256 devices in a mesh: lon: 16 (over z, x_hi), lat: 16 (over y, x_lo, core).
Axes of the slice: x: 4 (x_hi: 2, x_lo: 2; x = x_hi * 2 + x_lo), y: 4, z: 8, core: 2. Of those that a mesh axis runs over, the one named last changes fastest.
Arguments:
- tracers: float32 [2, 8, 2048, 4096], P(None, None, 'lat', 'lon'), may hold values from -6 to 6
- zonal_vel: float32 [8, 2048, 4096], P(None, 'lat', 'lon'), may hold values from -3 to 3
- merid_vel: float32 [8, 2048, 4096], P(None, 'lat', 'lon'), may hold values from -3 to 3
- thickness: float32 [8, 2048, 4096], P(None, 'lat', 'lon'), may hold values from 0.5 to 2
- land_sea: int32 [8, 2048, 4096], P(None, 'lat', 'lon'), may hold values from 0 to 1, as said below
- cell_dx: float32 [2048, 4096], P('lat', 'lon'), may hold values from 0.5 to 1.5
- cell_dy: float32 [2048, 4096], P('lat', 'lon'), may hold values from 0.5 to 1.5
- fold_partner: int32 [4096], P('lon'), may hold values from 0 to 4095, as said below
Outputs:
- new_tracers: float32 [2, 8, 2048, 4096], P(None, None, 'lat', 'lon')
The draws below stay inside these ranges and needn't reach their ends.
Inputs may be any that keep to these rules, and one draw needn't show every extreme that they name: In each column the ocean cells are the top levels: land_sea is 1 on levels above a column depth of 1 to 8 levels and 0 below it. fold_partner[i] = (4095 - i + p) mod 4096 with one pivot p of 1 to 255 for all i.
All inputs are finite; a program needn't handle non-finite values.
Results may differ from the reference program's by a relative error of at most 0.00002.
Values sent between devices are 32-bit elements; how exact they have to be, the bound alone decides.
No kernel may reach another device: no remote copies, remote signals or barrier semaphores. Data moves between devices by JAX's collectives and lax.ppermute only.
A program may use at most 128 MiB of HBM per device.

```python
import math
import jax
import jax.numpy as jnp

CI = 256
LEVELS = 8
NI = 4096
NJ = 2048


def draw_land_sea(key, part):
    key_coarse = jax.random.fold_in(key, 11)
    key_fine = jax.random.fold_in(key, 12)
    coarse = jax.random.randint(key_coarse, (NJ // 16 + 1, NI // 16 + 1), 1, LEVELS + 1)
    spread = jnp.repeat(jnp.repeat(coarse, 16, axis=0), 16, axis=1)[:NJ, :NI]
    depth = jnp.clip(spread + jax.random.randint(key_fine, (NJ, NI), -1, 2), 1, LEVELS)
    levels = jnp.arange(LEVELS, dtype=jnp.int32)[:, None, None]
    return (levels < depth[None]).astype(jnp.int32)


def draw_fold_partner(key, part):
    pivot = jax.random.randint(jax.random.fold_in(key, 21), (), 1, CI)
    columns = jnp.arange(NI, dtype=jnp.int32)
    return ((NI - 1 - columns + pivot) % NI).astype(jnp.int32)


def block_scale(rng, dims, cuts, least, high):
    def one(dim, shards_of):
        heights = jax.random.uniform(jax.random.fold_in(jax.random.fold_in(rng, 6), dim), (shards_of,), jnp.float32, least / len(cuts), high / len(cuts))
        return jnp.repeat(jnp.exp(heights), dims[dim] // shards_of).reshape((-1,) + (1,) * (len(dims) - dim - 1))

    loudness = one(*cuts[0])
    for cut in cuts[1:]:
        loudness = loudness * one(*cut)
    return loudness


def normal_values(key, dims, deviation, bound, shards=(), held_as=jnp.bfloat16):
    array = jax.random.normal(key, dims, jnp.float32) * deviation
    if len(shards) > 0:
        array = block_scale(key, dims, shards, -0.22, 0.18) * array
    return jnp.clip(array, min=-bound, max=bound).astype(held_as)


def setup_inputs(seed: int = 0) -> dict:
    key_list = jax.random.split(jax.random.key(seed), 9)
    tracers = normal_values(key_list[0], (2, LEVELS, NJ, NI), 1.0, 6.0, ((2, 16), (3, 16)), jnp.float32)
    zonal_vel = normal_values(key_list[1], (LEVELS, NJ, NI), 0.5, 3.0, ((1, 16), (2, 16)), jnp.float32)
    merid_vel = normal_values(key_list[2], (LEVELS, NJ, NI), 0.5, 3.0, ((1, 16), (2, 16)), jnp.float32)
    thickness = jnp.clip(jnp.exp(math.log(2.0) - 1.3862944 * jax.random.uniform(key_list[3], (LEVELS, NJ, NI), jnp.float32) ** block_scale(key_list[3], (LEVELS, NJ, NI), ((1, 16), (2, 16)), -0.2, 0.2)), 0.5, 2.0)
    land_sea = draw_land_sea(jax.random.fold_in(key_list[8], 71), 0)
    cell_dx = jnp.clip(1.0 + 0.1 * jax.random.normal(key_list[5], (NJ, NI), jnp.float32), 0.5, 1.5)
    cell_dy = jnp.clip(1.0 + 0.1 * jax.random.normal(key_list[6], (NJ, NI), jnp.float32), 0.5, 1.5)
    fold_partner = draw_fold_partner(jax.random.fold_in(key_list[8], 71), 0)
    return dict(tracers=tracers, zonal_vel=zonal_vel, merid_vel=merid_vel, thickness=thickness, land_sea=land_sea, cell_dx=cell_dx, cell_dy=cell_dy, fold_partner=fold_partner)


TIME_STEP = 0.2
DIFFUSIVITY = 0.25


def tendency(trac_lon, trac_lat, thick_lon, thick_lat, dx_lon, dx_lat, dy_lon, dy_lat, u_faces, v_faces, volume):
    dy_u = 0.5 * (dy_lon[:, :-1] + dy_lon[:, 1:])
    dx_u = 0.5 * (dx_lon[:, :-1] + dx_lon[:, 1:])
    thick_u = jnp.minimum(thick_lon[..., :-1], thick_lon[..., 1:])
    trans_u = u_faces * dy_u * thick_u
    diff_u = DIFFUSIVITY * dy_u * thick_u / dx_u
    flux_x = trans_u * 0.5 * (trac_lon[..., :-1] + trac_lon[..., 1:]) - diff_u * (trac_lon[..., 1:] - trac_lon[..., :-1])
    dx_v = 0.5 * (dx_lat[:-1, :] + dx_lat[1:, :])
    dy_v = 0.5 * (dy_lat[:-1, :] + dy_lat[1:, :])
    thick_v = jnp.minimum(thick_lat[..., :-1, :], thick_lat[..., 1:, :])
    trans_v = v_faces * dx_v * thick_v
    diff_v = DIFFUSIVITY * dx_v * thick_v / dy_v
    flux_y = trans_v * 0.5 * (trac_lat[..., :-1, :] + trac_lat[..., 1:, :]) - diff_v * (trac_lat[..., 1:, :] - trac_lat[..., :-1, :])
    divergence = (flux_x[..., 1:] - flux_x[..., :-1]) + (flux_y[..., 1:, :] - flux_y[..., :-1, :])
    return -divergence / volume


def lon_ext(field):
    return jnp.concatenate([field[..., -1:], field, field[..., :1]], axis=-1)


def lat_ext(field, partner):
    ghost_row = jnp.take(field[..., -1, :], partner, axis=-1)
    zero_row = jnp.zeros_like(field[..., :1, :])
    return jnp.concatenate([zero_row, field, ghost_row[..., None, :]], axis=-2)


def reference(tracers, zonal_vel, merid_vel, thickness, land_sea, cell_dx, cell_dy, fold_partner):
    sea_mask = land_sea.astype(jnp.float32)
    wet_thick = thickness * sea_mask
    volume = cell_dx * cell_dy * thickness
    u_faces = jnp.concatenate([zonal_vel[..., -1:], zonal_vel], axis=-1)
    v_faces = jnp.concatenate([jnp.zeros_like(merid_vel[:, :1, :]), merid_vel], axis=-2)
    geometry = (lon_ext(wet_thick), lat_ext(wet_thick, fold_partner), lon_ext(cell_dx), lat_ext(cell_dx, fold_partner), lon_ext(cell_dy), lat_ext(cell_dy, fold_partner))

    def operator(field):
        return tendency(lon_ext(field), lat_ext(field, fold_partner), geometry[0], geometry[1], geometry[2], geometry[3], geometry[4], geometry[5], u_faces, v_faces, volume)

    first = operator(tracers)
    section = tracers + TIME_STEP * first
    second = operator(section)
    return sea_mask * (tracers + 0.5 * TIME_STEP * (first + second))
```

```python
import functools
import jax
import jax.numpy as jnp
from jax import lax
from jax.experimental import pallas as pl
from jax.experimental.pallas import tpu as pltpu
from jax.sharding import PartitionSpec as P


STEP = 0.2
K = 8
SLABS = 9
C0, C1, WET, U, V, TH, D, F0, F1 = range(SLABS)
f32 = jnp.float32


def coefs(vel, wa, wb, la, lb, da, db):
    g = (0.5 * (la + lb)) * jnp.minimum(wa, wb)
    e = 0.5 / (da + db)
    h = 0.5 * vel
    return g * (h + e), g * (h - e)


def slab(x, s):
    return x[s * K : (s + 1) * K]


def join(*parts):
    return jnp.concatenate(parts, axis=0)


def row_message(t_ref, u_ref, v_ref, th_ref, sea_ref, dx_ref, dy_ref, near, far, face):
    def wet(r):
        return th_ref[:, r, :] * sea_ref[:, r, :].astype(f32)

    w1, w2 = wet(near), wet(far)
    dx1, dx2 = dx_ref[near : near + 1, :], dx_ref[far : far + 1, :]
    dy1, dy2 = dy_ref[near : near + 1, :], dy_ref[far : far + 1, :]
    p, q = coefs(v_ref[:, face, :], w1, w2, dx1, dx2, dy1, dy2)
    if near > far:
        p, q = coefs(v_ref[:, face, :], w2, w1, dx2, dx1, dy2, dy1)
        p, q = q, p
    near_c = [t_ref[n, :, near, :] for n in range(2)]
    inner = [p * near_c[n] + q * t_ref[n, :, far, :] for n in range(2)]
    pad = jnp.zeros((6, dx1.shape[1]), f32)
    return join(
        *near_c,
        w1,
        u_ref[:, near, :],
        v_ref[:, near, :],
        th_ref[:, near, :],
        join(dx1, dy1, pad),
        *inner,
    )


def rows_kernel(*refs):
    low, high, (x_ref, y_ref) = refs[:7], refs[7:14], refs[14:]
    bottom = row_message(*low, 0, 1, 0)
    top = row_message(*high, 7, 6, 6)
    even = lax.axis_index("lat") % 2 == 0

    @pl.when(even)
    def _():
        x_ref[...] = top
        y_ref[...] = bottom

    @pl.when(jnp.logical_not(even))
    def _():
        x_ref[...] = bottom
        y_ref[...] = top


def cols_kernel(t_ref, u_ref, v_ref, th_ref, sea_ref, dx_ref, dy_ref, w_ref, e_ref, accw, acce, flip):
    k = pl.program_id(0)
    rows = dx_ref.shape[0]
    lane = lax.broadcasted_iota(jnp.int32, (rows, 128), 1)
    pair = lane >> 1

    def put(value, slot):
        for acc, part, shift in ((accw, value[:, :128], 0), (acce, value[:, -128:], 2)):
            moved = pltpu.roll(part, (2 * slot + shift) % 128, 1)
            acc[...] = jnp.where(pair == slot, moved, acc[...])

    @pl.when(k == 0)
    def _():
        accw[...] = jnp.zeros_like(accw)
        acce[...] = jnp.zeros_like(acce)
        put(dx_ref[...], 48)
        put(dy_ref[...], 49)

    th = th_ref[0]
    wet = th * sea_ref[0].astype(f32)
    for q, value in enumerate((t_ref[0, 0], t_ref[1, 0], wet, u_ref[0], v_ref[0], th)):
        put(value, 8 * q + k)

    @pl.when(k == K - 1)
    def _():
        for acc, out, near, far in ((accw, w_ref, 0, 1), (acce, e_ref, 1, 0)):
            flip[...] = acc[...].T

            def get(q, c):
                return flip[pl.ds(16 * q + c, K, stride=2), :]

            d1 = flip[pl.ds(96 + near, 2, stride=2), :]
            d2 = flip[pl.ds(96 + far, 2, stride=2), :]
            first, second = (near, far) if near < far else (far, near)
            da, db = (d1, d2) if near < far else (d2, d1)
            p, q = coefs(
                get(U, first), get(WET, first), get(WET, second), da[1:2], db[1:2], da[0:1], db[0:1]
            )
            for s in (C0, C1, WET, U, V, TH):
                out[s * K : (s + 1) * K, :] = get(s, near)
            out[D * K : (D + 1) * K, :] = join(d1, jnp.zeros((6, rows), f32))
            for n in range(2):
                out[(F0 + n) * K : (F0 + n + 1) * K, :] = p * get(n, first) + q * get(n, second)


CORNER = (C0, C1, WET, U, V, D)


def corners_kernel(xr_ref, yr_ref, w_ref, e_ref, p_ref, q_ref):
    even_lat = lax.axis_index("lat") % 2 == 0
    even_lon = lax.axis_index("lon") % 2 == 0
    north = jnp.where(even_lat, xr_ref[...], yr_ref[...])
    south = jnp.where(even_lat, yr_ref[...], xr_ref[...])
    lane = lax.broadcasted_iota(jnp.int32, (K, 128), 1)

    def corner(col):
        out = jnp.zeros((K, 128), f32)
        for base, rows in ((0, south), (8, north)):
            for at, s in enumerate(CORNER):
                out = jnp.where(lane == base + at, slab(rows, s)[:, col : col + 1], out)
        return out

    n = SLABS * K
    west, east = corner(0), corner(255)

    @pl.when(even_lon)
    def _():
        p_ref[:n, :] = e_ref[...]
        p_ref[n:, :] = east
        q_ref[:n, :] = w_ref[...]
        q_ref[n:, :] = west

    @pl.when(jnp.logical_not(even_lon))
    def _():
        p_ref[:n, :] = w_ref[...]
        p_ref[n:, :] = west
        q_ref[:n, :] = e_ref[...]
        q_ref[n:, :] = east


def line_tendency(C, wet, th, d, along, across, vel, prev, nxt, prev_vel, side):
    n = wet.shape[1]
    lane = lax.broadcasted_iota(jnp.int32, (1, n), 1)

    def before(x, edge):
        return jnp.where(lane == 0, edge, pltpu.roll(x, 1, 1))

    def after(x, edge):
        return jnp.where(lane == n - 1, edge, pltpu.roll(x, n - 1, 1))

    def wide(x):
        return jnp.broadcast_to(x, (K, n))

    al, ac = wide(d[along : along + 1]), wide(d[across : across + 1])
    al_n, ac_n = after(al, nxt["d"][along : along + 1]), after(ac, nxt["d"][across : across + 1])
    al_p, ac_p = before(al, prev["d"][along : along + 1]), before(ac, prev["d"][across : across + 1])
    pn, qn = coefs(vel, wet, after(wet, nxt["w"]), ac, ac_n, al, al_n)
    pp, qp = coefs(before(vel, prev_vel), before(wet, prev["w"]), wet, ac_p, ac, al_p, al)
    out = []
    for t in range(2):
        ahead = pn * C[t] + qn * after(C[t], nxt["c"][t])
        behind = pp * before(C[t], prev["c"][t]) + qp * C[t]
        out.append(ahead - behind)
    return out


def face_fluxes(own, ghost, own_vel_is_low, vel, ghost_vel, along, across, own_line, ghost_line):
    d, g = slab(own, D), slab(ghost, D)

    def face(velocity):
        lo, hi = (own, ghost) if own_vel_is_low else (ghost, own)
        dl, dh = (d, g) if own_vel_is_low else (g, d)
        return coefs(
            velocity,
            slab(lo, WET),
            slab(hi, WET),
            dl[across : across + 1],
            dh[across : across + 1],
            dl[along : along + 1],
            dh[along : along + 1],
        )

    def through(pq, a, b):
        return pq[0] * a + pq[1] * b if own_vel_is_low else pq[0] * b + pq[1] * a

    pq = face(vel)
    pq_ghost = pq if ghost_vel is None else face(ghost_vel)
    vol_own = d[0:1] * d[1:2] * slab(own, TH)
    vol_ghost = g[0:1] * g[1:2] * slab(ghost, TH)
    one, two = [], []
    for t in range(2):
        a, b = slab(own, t), slab(ghost, t)
        f = through(pq, a, b)
        fg = f if ghost_vel is None else through(pq_ghost, a, b)
        if own_vel_is_low:
            own_div = own_line[t] + (f - slab(own, F0 + t))
            ghost_div = ghost_line[t] + (slab(ghost, F0 + t) - fg)
        else:
            own_div = own_line[t] + (slab(own, F0 + t) - f)
            ghost_div = ghost_line[t] + (fg - slab(ghost, F0 + t))
        a2 = a - STEP * own_div / vol_own
        b2 = b - STEP * ghost_div / vol_ghost
        one.append(f)
        two.append(through(pq, a2, b2))
    return one, two


def boundary(xs, ys, xr, yr, f2r, own_w, own_e, pr, qr, pivot, fy_ref, tt_ref, ghost_ref):
    lat, lon = lax.axis_index("lat"), lax.axis_index("lon")
    last = lax.axis_size("lat") - 1
    even_lat, even_lon = lat % 2 == 0, lon % 2 == 0
    n = SLABS * K
    top = jnp.where(even_lat, xs[...], ys[...])
    bottom = jnp.where(even_lat, ys[...], xs[...])
    south = jnp.where(even_lat, yr[...], xr[...])
    west_all = jnp.where(even_lon, qr[...], pr[...])
    east_all = jnp.where(even_lon, pr[...], qr[...])
    west, east = west_all[:n], east_all[:n]
    cw, ce = west_all[n:], east_all[n:]
    w_own, e_own = own_w[...], own_e[...]
    width = top.shape[1]
    height = w_own.shape[1]

    @pl.when(lat != last)
    def _():
        ghost_ref[:n, :width] = jnp.where(even_lat, xr[...], yr[...])
        ghost_ref[n:, :width] = slab(top, V)
        tile = jnp.zeros((K, 128), f32)
        lane = lax.broadcasted_iota(jnp.int32, (K, 128), 1)
        for at, s in enumerate(CORNER):
            ends = jnp.where(lane == 0, cw[:, 8 + at : 9 + at], tile)
            ends = jnp.where(lane == 1, ce[:, 8 + at : 9 + at], ends)
            ghost_ref[s * K : (s + 1) * K, width:] = ends

    @pl.when(lat == last)
    def _():
        p = pivot[0] - (lax.axis_size("lon") * width - 1) + lon * width
        p = jnp.where(p <= 0, p + lax.axis_size("lon") * width, p)
        mine = (2 * lon) % lax.axis_size("lon") == 0
        both = jnp.concatenate([yr[...], jnp.where(mine, ys[...], f2r[...])], axis=1)
        src = lax.broadcasted_iota(jnp.int32, (2 * width, width + 128), 0)
        dst = lax.broadcasted_iota(jnp.int32, (2 * width, width + 128), 1)
        dst = jnp.where(dst == width, -1, jnp.where(dst == width + 1, width, dst))
        pick = (src == (width - 1) - dst + p).astype(f32)
        win = jnp.dot(both, pick, preferred_element_type=f32, precision=lax.Precision.HIGHEST)
        for s in (C0, C1, WET, TH, D):
            ghost_ref[s * K : (s + 1) * K, :] = slab(win, s)
        u = slab(win, U)
        lane = lax.broadcasted_iota(jnp.int32, (K, width), 1)
        here = u[:, :width]
        ghost_ref[U * K : (U + 1) * K, :width] = -jnp.where(
            lane == width - 1, u[:, width + 1 : width + 2], pltpu.roll(here, width - 1, 1)
        )
        ghost_ref[U * K : (U + 1) * K, width:] = jnp.broadcast_to(-here[:, 0:1], (K, 128))
        for s in (F0, F1):
            ghost_ref[s * K : (s + 1) * K, :] = -slab(win, s)
        ghost_ref[n:, :width] = -slab(win, V)[:, :width]

    north = ghost_ref[:n, :width]
    north_vel = ghost_ref[n:, :width]

    def end(x, at):
        return dict(
            c=[slab(x, C0)[:, at : at + 1], slab(x, C1)[:, at : at + 1]],
            w=slab(x, WET)[:, at : at + 1],
            u=slab(x, U)[:, at : at + 1],
            v=slab(x, V)[:, at : at + 1],
            d=slab(x, D)[:, at : at + 1],
        )

    def corner(x, base):
        get = [x[:, base + at : base + at + 1] for at in range(len(CORNER))]
        return dict(c=get[:2], w=get[2], u=get[3], v=get[4], d=get[5])

    def ghost_end(at):
        x = {s: ghost_ref[s * K : (s + 1) * K, width:][:, at : at + 1] for s in (C0, C1, WET, U, D)}
        return dict(c=[x[C0], x[C1]], w=x[WET], u=x[U], d=x[D])

    def x_line(line, prev, nxt):
        c = [slab(line, C0), slab(line, C1)]
        return line_tendency(
            c, slab(line, WET), None, slab(line, D), 0, 1, slab(line, U), prev, nxt, prev["u"], 0
        )

    def y_line(line, prev, nxt):
        c = [slab(line, C0), slab(line, C1)]
        return line_tendency(
            c, slab(line, WET), None, slab(line, D), 1, 0, slab(line, V), prev, nxt, prev["v"], 0
        )

    nw, ne = ghost_end(0), ghost_end(1)
    line_n = x_line(north, nw, ne)
    line_s = x_line(south, corner(cw, 0), corner(ce, 0))
    line_top = x_line(top, end(west, height - 1), end(east, height - 1))
    line_bottom = x_line(bottom, end(west, 0), end(east, 0))
    n1, n2 = face_fluxes(top, north, True, slab(top, V), north_vel, 1, 0, line_top, line_n)
    s1, s2 = face_fluxes(bottom, south, False, slab(south, V), None, 1, 0, line_bottom, line_s)
    closed = lat == 0
    for i, value in enumerate((*s1, *s2)):
        fy_ref[i * K : (i + 1) * K, :] = jnp.where(closed, 0.0, value)
    for i, value in enumerate((*n1, *n2)):
        fy_ref[(4 + i) * K : (5 + i) * K, :] = value

    line_w = y_line(west, corner(cw, 0), nw)
    line_e = y_line(east, corner(ce, 0), ne)
    own_line_w = y_line(w_own, end(south, 0), end(north, 0))
    own_line_e = y_line(e_own, end(south, width - 1), end(north, width - 1))
    e1, e2 = face_fluxes(e_own, east, True, slab(e_own, U), None, 0, 1, own_line_e, line_e)
    w1, w2 = face_fluxes(w_own, west, False, slab(west, U), None, 0, 1, own_line_w, line_w)
    stack = join(*w1, *w2, *e1, *e2, jnp.zeros((128 - 8 * K, height), f32))
    tt_ref[...] = stack.T


def main_kernel(
    pivot, t_ref, u_ref, v_ref, th_ref, sea_ref, dx_ref, dy_ref, xs, ys, xr, yr, f2r, own_w, own_e, pr, qr,
    out_ref, fy_ref, tt_ref, ghost_ref, geo, coef, sec,
):
    k = pl.program_id(0)
    rows = dx_ref.shape[0]
    chunks = rows // 8
    lane = lax.broadcasted_iota(jnp.int32, (8, 128), 1)
    sub = lax.broadcasted_iota(jnp.int32, (8, 128), 0)
    tiles = (slice(0, 128), slice(128, 256))

    def at(c):
        return slice(8 * c, 8 * c + 8)

    def east_of(x):
        moved = [pltpu.roll(v, 127, 1) for v in x]
        return [jnp.where(lane == 127, moved[1], moved[0]), moved[1]]

    def north_of(x, nxt):
        return [jnp.where(sub == 7, pltpu.roll(b, 7, 0), pltpu.roll(a, 7, 0)) for a, b in zip(x, nxt)]

    def both(ref, c, *lead):
        return [ref[(*lead, at(c), t)] for t in tiles]

    @pl.when(k == 0)
    def _():
        boundary(xs, ys, xr, yr, f2r, own_w, own_e, pr, qr, pivot, fy_ref, tt_ref, ghost_ref)
        for c in range(chunks):
            n = min(c + 1, chunks - 1)
            dx, dy = both(dx_ref, c), both(dy_ref, c)
            dx_e, dy_e = east_of(dx), east_of(dy)
            dx_n, dy_n = north_of(dx, both(dx_ref, n)), north_of(dy, both(dy_ref, n))
            for i, t in enumerate(tiles):
                geo[0, at(c), t] = 0.5 * (dy[i] + dy_e[i])
                geo[1, at(c), t] = 0.5 / (dx[i] + dx_e[i])
                geo[2, at(c), t] = 0.5 * (dx[i] + dx_n[i])
                geo[3, at(c), t] = 0.5 / (dy[i] + dy_n[i])
                geo[4, at(c), t] = -1.0 / (dx[i] * dy[i])

    def wet(c):
        return [a * b.astype(f32) for a, b in zip(both(th_ref, c, 0), both(sea_ref, c, 0))]

    w = wet(0)
    for c in range(chunks):
        w_next = wet(c + 1) if c + 1 < chunks else w
        w_e, w_n = east_of(w), north_of(w, w_next)
        u, v, th = both(u_ref, c, 0), both(v_ref, c, 0), both(th_ref, c, 0)
        for i, t in enumerate(tiles):
            g = geo[0, at(c), t] * jnp.minimum(w[i], w_e[i])
            e, h = geo[1, at(c), t], 0.5 * u[i]
            coef[0, at(c), t] = g * (h + e)
            coef[1, at(c), t] = g * (h - e)
            g = geo[2, at(c), t] * jnp.minimum(w[i], w_n[i])
            e, h = geo[3, at(c), t], 0.5 * v[i]
            coef[2, at(c), t] = g * (h + e)
            coef[3, at(c), t] = g * (h - e)
            coef[4, at(c), t] = geo[4, at(c), t] / th[i]
        w = w_next

    def stage(load, n, s, write):
        def row(i):
            r = fy_ref[pl.ds((4 * i + 2 * s + n) * K + k, 1), :]
            return [jnp.broadcast_to(r[:, t], (8, 128)) for t in tiles]

        below = row(0)
        top = row(1)
        x = load(0)
        for c in range(chunks):
            x_next = load(c + 1) if c + 1 < chunks else x
            a, b, p, q, r = [both(coef, c, j) for j in range(5)]
            cols = pltpu.roll(tt_ref[at(c), :], (128 - k) % 128, 1)
            i_w, i_e = (2 * s + n) * K, (4 + 2 * s + n) * K
            f_w, f_e = cols[:, i_w : i_w + 1], cols[:, i_e : i_e + 1]
            x_e, x_n = east_of(x), north_of(x, x_next)
            fx = [a[i] * x[i] + b[i] * x_e[i] for i in range(2)]
            fx[1] = jnp.where(lane == 127, f_e, fx[1])
            moved = [pltpu.roll(f, 1, 1) for f in fx]
            fx_w = [jnp.where(lane == 0, f_w, moved[0]), jnp.where(lane == 0, moved[0], moved[1])]
            fy = [p[i] * x[i] + q[i] * x_n[i] for i in range(2)]
            if c == chunks - 1:
                fy = [jnp.where(sub == 7, top[i], fy[i]) for i in range(2)]
            up = [pltpu.roll(f, 1, 0) for f in fy]
            fy_s = [jnp.where(sub == 0, below[i], up[i]) for i in range(2)]
            below = up
            for i, t in enumerate(tiles):
                div = (fx[i] - fx_w[i]) + (fy[i] - fy_s[i])
                write(c, i, t, x[i], r[i] * div)
            x = x_next

    for n in range(2):

        def first(c, i, t, x, tend):
            sec[at(c), t] = x + STEP * tend
            out_ref[n, 0, at(c), t] = x + (0.5 * STEP) * tend

        def second(c, i, t, x, tend):
            sea = sea_ref[0, at(c), t].astype(f32)
            out_ref[n, 0, at(c), t] = sea * (out_ref[n, 0, at(c), t] + (0.5 * STEP) * tend)

        stage(lambda c: both(t_ref, c, n, 0), n, 0, first)
        stage(lambda c: both(sec, c), n, 1, second)


def pairs(count_lon, count_lat, partner):
    out = []
    for o in range(count_lon):
        for a in range(count_lat):
            to = partner(o, a)
            if to is not None:
                source, target = o * count_lat + a, (to[0] % count_lon) * count_lat + to[1]
                if source != target:
                    out.append((source, target))
    return out


def shards(nlon, nlat, tracers, zonal_vel, merid_vel, thickness, land_sea, cell_dx, cell_dy, fold_partner):
    rows, cols = cell_dx.shape
    axes = ("lon", "lat")
    end = nlat - 1

    def swap(x, partner):
        return lax.ppermute(x, axes, pairs(nlon, nlat, partner))

    def y_partner(o, a):
        if a == 0:
            return None
        if a == end:
            return (nlon - 1 - o, a)
        return (o, a + 1) if a % 2 else (o, a - 1)

    fields = (tracers, zonal_vel, merid_vel, thickness, land_sea, cell_dx, cell_dy)
    n = SLABS * K

    def edge(r):
        return [
            pl.BlockSpec((2, K, 8, cols), lambda i: (0, 0, r, 0)),
            *[pl.BlockSpec((K, 8, cols), lambda i: (0, r, 0))] * 4,
            *[pl.BlockSpec((8, cols), lambda i: (r, 0))] * 2,
        ]

    whole = pl.BlockSpec((n, cols), lambda i: (0, 0))
    line = jax.ShapeDtypeStruct((n, cols), f32)
    xs, ys = pl.pallas_call(
        rows_kernel,
        grid=(1,),
        in_specs=[*edge(0), *edge(rows // 8 - 1)],
        out_specs=[whole] * 2,
        out_shape=[line] * 2,
        name="edge_rows",
    )(*fields, *fields)
    yr = swap(ys, y_partner)
    xr = swap(xs, lambda o, a: (o, a ^ 1))
    f2r = swap(ys, lambda o, a: (nlon - o, a) if a == end else None)

    level = [
        pl.BlockSpec((2, 1, rows, cols), lambda k: (0, k, 0, 0)),
        *[pl.BlockSpec((1, rows, cols), lambda k: (k, 0, 0))] * 4,
        *[pl.BlockSpec((rows, cols), lambda k: (0, 0))] * 2,
    ]
    side = jax.ShapeDtypeStruct((n, rows), f32)
    own_w, own_e = pl.pallas_call(
        cols_kernel,
        grid=(K,),
        in_specs=level,
        out_specs=[pl.BlockSpec((n, rows), lambda k: (0, 0))] * 2,
        out_shape=[side] * 2,
        scratch_shapes=[pltpu.VMEM((rows, 128), f32)] * 2 + [pltpu.VMEM((128, rows), f32)],
        cost_estimate=pl.CostEstimate(flops=4_000_000, bytes_accessed=7_000_000, transcendentals=0),
        name="edge_cols",
    )(*fields)
    message = jax.ShapeDtypeStruct((n + K, rows), f32)
    ps, qs = pl.pallas_call(corners_kernel, out_shape=[message] * 2, name="corners")(xr, yr, own_w, own_e)
    qr = swap(qs, lambda o, a: (o + 1, a) if o % 2 else (o - 1, a))
    pr = swap(ps, lambda o, a: (o ^ 1, a))

    fixed = lambda shape: pl.BlockSpec(shape, lambda k: (0,) * len(shape))
    return pl.pallas_call(
        main_kernel,
        grid=(K,),
        in_specs=[pl.BlockSpec(memory_space=pltpu.SMEM), *level]
        + [fixed((n, cols))] * 5
        + [fixed((n, rows))] * 2
        + [fixed((n + K, rows))] * 2,
        out_specs=pl.BlockSpec((2, 1, rows, cols), lambda k: (0, k, 0, 0)),
        out_shape=jax.ShapeDtypeStruct(tracers.shape, f32),
        scratch_shapes=[
            pltpu.VMEM((8 * K, cols), f32),
            pltpu.VMEM((rows, 128), f32),
            pltpu.VMEM((n + K, cols + 128), f32),
            pltpu.VMEM((5, rows, cols), f32),
            pltpu.VMEM((5, rows, cols), f32),
            pltpu.VMEM((rows, cols), f32),
        ],
        name="stencil",
    )(fold_partner, *fields, xs, ys, xr, yr, f2r, own_w, own_e, pr, qr)


def solution(mesh):
    return jax.shard_map(
        functools.partial(shards, mesh.shape["lon"], mesh.shape["lat"]),
        mesh=mesh,
        in_specs=(
            P(None, None, "lat", "lon"),
            P(None, "lat", "lon"),
            P(None, "lat", "lon"),
            P(None, "lat", "lon"),
            P(None, "lat", "lon"),
            P("lat", "lon"),
            P("lat", "lon"),
            P("lon"),
        ),
        out_specs=P(None, None, "lat", "lon"),
        check_vma=False,
    )
```

```python
import functools
import jax
import jax.numpy as jnp
from jax import lax
from jax.experimental import pallas as pl
from jax.experimental.pallas import tpu as pltpu
from jax.sharding import PartitionSpec as P


STEP = 0.2
K = 8
SLABS = 9
C0, C1, WET, U, V, TH, D, F0, F1 = range(SLABS)
f32 = jnp.float32


def coefs(vel, wa, wb, la, lb, da, db):
    g = (0.5 * (la + lb)) * jnp.minimum(wa, wb)
    e = 0.5 / (da + db)
    h = 0.5 * vel
    return g * (h + e), g * (h - e)


def slab(x, s):
    return x[s * K : (s + 1) * K]


def join(*parts):
    return jnp.concatenate(parts, axis=0)


def row_message(t_ref, u_ref, v_ref, th_ref, sea_ref, dx_ref, dy_ref, near, far, face):
    def wet(r):
        return th_ref[:, r, :] * sea_ref[:, r, :].astype(f32)

    w1, w2 = wet(near), wet(far)
    dx1, dx2 = dx_ref[near : near + 1, :], dx_ref[far : far + 1, :]
    dy1, dy2 = dy_ref[near : near + 1, :], dy_ref[far : far + 1, :]
    p, q = coefs(v_ref[:, face, :], w1, w2, dx1, dx2, dy1, dy2)
    if near > far:
        p, q = coefs(v_ref[:, face, :], w2, w1, dx2, dx1, dy2, dy1)
        p, q = q, p
    near_c = [t_ref[n, :, near, :] for n in range(2)]
    inner = [p * near_c[n] + q * t_ref[n, :, far, :] for n in range(2)]
    pad = jnp.zeros((6, dx1.shape[1]), f32)
    return join(
        *near_c,
        w1,
        u_ref[:, near, :],
        v_ref[:, near, :],
        th_ref[:, near, :],
        join(dx1, dy1, pad),
        *inner,
    )


def rows_kernel(*refs):
    low, high, (x_ref, y_ref) = refs[:7], refs[7:14], refs[14:]
    bottom = row_message(*low, 0, 1, 0)
    top = row_message(*high, 7, 6, 6)
    even = lax.axis_index("lat") % 2 == 0

    @pl.when(even)
    def _():
        x_ref[...] = top
        y_ref[...] = bottom

    @pl.when(jnp.logical_not(even))
    def _():
        x_ref[...] = bottom
        y_ref[...] = top


def cols_kernel(t_ref, u_ref, v_ref, th_ref, sea_ref, dx_ref, dy_ref, w_ref, e_ref, accw, acce, flip):
    k = pl.program_id(0)
    rows = dx_ref.shape[0]
    lane = lax.broadcasted_iota(jnp.int32, (rows, 128), 1)
    pair = lane >> 1

    def put(value, slot):
        for acc, part, shift in ((accw, value[:, :128], 0), (acce, value[:, -128:], 2)):
            moved = pltpu.roll(part, (2 * slot + shift) % 128, 1)
            acc[...] = jnp.where(pair == slot, moved, acc[...])

    @pl.when(k == 0)
    def _():
        accw[...] = jnp.zeros_like(accw)
        acce[...] = jnp.zeros_like(acce)
        put(dx_ref[...], 48)
        put(dy_ref[...], 49)

    th = th_ref[0]
    wet = th * sea_ref[0].astype(f32)
    for q, value in enumerate((t_ref[0, 0], t_ref[1, 0], wet, u_ref[0], v_ref[0], th)):
        put(value, 8 * q + k)

    @pl.when(k == K - 1)
    def _():
        for acc, out, near, far in ((accw, w_ref, 0, 1), (acce, e_ref, 1, 0)):
            flip[...] = acc[...].T

            def get(q, c):
                return flip[pl.ds(16 * q + c, K, stride=2), :]

            d1 = flip[pl.ds(96 + near, 2, stride=2), :]
            d2 = flip[pl.ds(96 + far, 2, stride=2), :]
            first, second = (near, far) if near < far else (far, near)
            da, db = (d1, d2) if near < far else (d2, d1)
            p, q = coefs(
                get(U, first), get(WET, first), get(WET, second), da[1:2], db[1:2], da[0:1], db[0:1]
            )
            for s in (C0, C1, WET, U, V, TH):
                out[s * K : (s + 1) * K, :] = get(s, near)
            out[D * K : (D + 1) * K, :] = join(d1, jnp.zeros((6, rows), f32))
            for n in range(2):
                out[(F0 + n) * K : (F0 + n + 1) * K, :] = p * get(n, first) + q * get(n, second)


CORNER = (C0, C1, WET, U, V, D)


def corners_kernel(xr_ref, yr_ref, w_ref, e_ref, p_ref, q_ref):
    even_lat = lax.axis_index("lat") % 2 == 0
    even_lon = lax.axis_index("lon") % 2 == 0
    north = jnp.where(even_lat, xr_ref[...], yr_ref[...])
    south = jnp.where(even_lat, yr_ref[...], xr_ref[...])
    lane = lax.broadcasted_iota(jnp.int32, (K, 128), 1)

    def corner(col):
        out = jnp.zeros((K, 128), f32)
        for base, rows in ((0, south), (8, north)):
            for at, s in enumerate(CORNER):
                out = jnp.where(lane == base + at, slab(rows, s)[:, col : col + 1], out)
        return out

    n = SLABS * K
    west, east = corner(0), corner(255)

    @pl.when(even_lon)
    def _():
        p_ref[:n, :] = e_ref[...]
        p_ref[n:, :] = east
        q_ref[:n, :] = w_ref[...]
        q_ref[n:, :] = west

    @pl.when(jnp.logical_not(even_lon))
    def _():
        p_ref[:n, :] = w_ref[...]
        p_ref[n:, :] = west
        q_ref[:n, :] = e_ref[...]
        q_ref[n:, :] = east


def line_tendency(C, wet, th, d, along, across, vel, prev, nxt, prev_vel, side):
    n = wet.shape[1]
    lane = lax.broadcasted_iota(jnp.int32, (1, n), 1)

    def before(x, edge):
        return jnp.where(lane == 0, edge, pltpu.roll(x, 1, 1))

    def after(x, edge):
        return jnp.where(lane == n - 1, edge, pltpu.roll(x, n - 1, 1))

    def wide(x):
        return jnp.broadcast_to(x, (K, n))

    al, ac = wide(d[along : along + 1]), wide(d[across : across + 1])
    al_n, ac_n = after(al, nxt["d"][along : along + 1]), after(ac, nxt["d"][across : across + 1])
    al_p, ac_p = before(al, prev["d"][along : along + 1]), before(ac, prev["d"][across : across + 1])
    pn, qn = coefs(vel, wet, after(wet, nxt["w"]), ac, ac_n, al, al_n)
    pp, qp = coefs(before(vel, prev_vel), before(wet, prev["w"]), wet, ac_p, ac, al_p, al)
    out = []
    for t in range(2):
        ahead = pn * C[t] + qn * after(C[t], nxt["c"][t])
        behind = pp * before(C[t], prev["c"][t]) + qp * C[t]
        out.append(ahead - behind)
    return out


def face_fluxes(own, ghost, own_vel_is_low, vel, ghost_vel, along, across, own_line, ghost_line):
    d, g = slab(own, D), slab(ghost, D)

    def face(velocity):
        lo, hi = (own, ghost) if own_vel_is_low else (ghost, own)
        dl, dh = (d, g) if own_vel_is_low else (g, d)
        return coefs(
            velocity,
            slab(lo, WET),
            slab(hi, WET),
            dl[across : across + 1],
            dh[across : across + 1],
            dl[along : along + 1],
            dh[along : along + 1],
        )

    def through(pq, a, b):
        return pq[0] * a + pq[1] * b if own_vel_is_low else pq[0] * b + pq[1] * a

    pq = face(vel)
    pq_ghost = pq if ghost_vel is None else face(ghost_vel)
    vol_own = d[0:1] * d[1:2] * slab(own, TH)
    vol_ghost = g[0:1] * g[1:2] * slab(ghost, TH)
    one, two = [], []
    for t in range(2):
        a, b = slab(own, t), slab(ghost, t)
        f = through(pq, a, b)
        fg = f if ghost_vel is None else through(pq_ghost, a, b)
        if own_vel_is_low:
            own_div = own_line[t] + (f - slab(own, F0 + t))
            ghost_div = ghost_line[t] + (slab(ghost, F0 + t) - fg)
        else:
            own_div = own_line[t] + (slab(own, F0 + t) - f)
            ghost_div = ghost_line[t] + (fg - slab(ghost, F0 + t))
        a2 = a - STEP * own_div / vol_own
        b2 = b - STEP * ghost_div / vol_ghost
        one.append(f)
        two.append(through(pq, a2, b2))
    return one, two


def boundary(xs, ys, xr, yr, f2r, own_w, own_e, pr, qr, pivot, fy_ref, tt_ref, flip_ref, ghost_ref):
    lat, lon = lax.axis_index("lat"), lax.axis_index("lon")
    last = lax.axis_size("lat") - 1
    even_lat, even_lon = lat % 2 == 0, lon % 2 == 0
    n = SLABS * K
    top = jnp.where(even_lat, xs[...], ys[...])
    bottom = jnp.where(even_lat, ys[...], xs[...])
    south = jnp.where(even_lat, yr[...], xr[...])
    west_all = jnp.where(even_lon, qr[...], pr[...])
    east_all = jnp.where(even_lon, pr[...], qr[...])
    west, east = west_all[:n], east_all[:n]
    cw, ce = west_all[n:], east_all[n:]
    w_own, e_own = own_w[...], own_e[...]
    width = top.shape[1]
    height = w_own.shape[1]

    @pl.when(lat != last)
    def _():
        ghost_ref[:n, :width] = jnp.where(even_lat, xr[...], yr[...])
        ghost_ref[n:, :width] = slab(top, V)
        tile = jnp.zeros((K, 128), f32)
        lane = lax.broadcasted_iota(jnp.int32, (K, 128), 1)
        for at, s in enumerate(CORNER):
            ends = jnp.where(lane == 0, cw[:, 8 + at : 9 + at], tile)
            ends = jnp.where(lane == 1, ce[:, 8 + at : 9 + at], ends)
            ghost_ref[s * K : (s + 1) * K, width:] = ends

    @pl.when(lat == last)
    def _():
        p = pivot[0] - (lax.axis_size("lon") * width - 1) + lon * width
        p = jnp.where(p <= 0, p + lax.axis_size("lon") * width, p)
        mine = (2 * lon) % lax.axis_size("lon") == 0
        both = jnp.concatenate([yr[...], jnp.where(mine, ys[...], f2r[...])], axis=1)
        src = lax.broadcasted_iota(jnp.int32, (2 * width, width + 128), 0)
        dst = lax.broadcasted_iota(jnp.int32, (2 * width, width + 128), 1)
        dst = jnp.where(dst == width, -1, jnp.where(dst == width + 1, width, dst))
        pick = (src == (width - 1) - dst + p).astype(f32)
        win = jnp.dot(both, pick, preferred_element_type=f32, precision=lax.Precision.HIGHEST)
        for s in (C0, C1, WET, TH, D):
            ghost_ref[s * K : (s + 1) * K, :] = slab(win, s)
        u = slab(win, U)
        lane = lax.broadcasted_iota(jnp.int32, (K, width), 1)
        here = u[:, :width]
        ghost_ref[U * K : (U + 1) * K, :width] = -jnp.where(
            lane == width - 1, u[:, width + 1 : width + 2], pltpu.roll(here, width - 1, 1)
        )
        ghost_ref[U * K : (U + 1) * K, width:] = jnp.broadcast_to(-here[:, 0:1], (K, 128))
        for s in (F0, F1):
            ghost_ref[s * K : (s + 1) * K, :] = -slab(win, s)
        ghost_ref[n:, :width] = -slab(win, V)[:, :width]

    north = ghost_ref[:n, :width]
    north_vel = ghost_ref[n:, :width]

    def end(x, at):
        return dict(
            c=[slab(x, C0)[:, at : at + 1], slab(x, C1)[:, at : at + 1]],
            w=slab(x, WET)[:, at : at + 1],
            u=slab(x, U)[:, at : at + 1],
            v=slab(x, V)[:, at : at + 1],
            d=slab(x, D)[:, at : at + 1],
        )

    def corner(x, base):
        get = [x[:, base + at : base + at + 1] for at in range(len(CORNER))]
        return dict(c=get[:2], w=get[2], u=get[3], v=get[4], d=get[5])

    def ghost_end(at):
        x = {s: ghost_ref[s * K : (s + 1) * K, width:][:, at : at + 1] for s in (C0, C1, WET, U, D)}
        return dict(c=[x[C0], x[C1]], w=x[WET], u=x[U], d=x[D])

    def x_line(line, prev, nxt):
        c = [slab(line, C0), slab(line, C1)]
        return line_tendency(
            c, slab(line, WET), None, slab(line, D), 0, 1, slab(line, U), prev, nxt, prev["u"], 0
        )

    def y_line(line, prev, nxt):
        c = [slab(line, C0), slab(line, C1)]
        return line_tendency(
            c, slab(line, WET), None, slab(line, D), 1, 0, slab(line, V), prev, nxt, prev["v"], 0
        )

    nw, ne = ghost_end(0), ghost_end(1)
    line_n = x_line(north, nw, ne)
    line_s = x_line(south, corner(cw, 0), corner(ce, 0))
    line_top = x_line(top, end(west, height - 1), end(east, height - 1))
    line_bottom = x_line(bottom, end(west, 0), end(east, 0))
    n1, n2 = face_fluxes(top, north, True, slab(top, V), north_vel, 1, 0, line_top, line_n)
    s1, s2 = face_fluxes(bottom, south, False, slab(south, V), None, 1, 0, line_bottom, line_s)
    closed = lat == 0
    for i, value in enumerate((*s1, *s2)):
        fy_ref[i * K : (i + 1) * K, :] = jnp.where(closed, 0.0, value)
    for i, value in enumerate((*n1, *n2)):
        fy_ref[(4 + i) * K : (5 + i) * K, :] = value

    line_w = y_line(west, corner(cw, 0), nw)
    line_e = y_line(east, corner(ce, 0), ne)
    own_line_w = y_line(w_own, end(south, 0), end(north, 0))
    own_line_e = y_line(e_own, end(south, width - 1), end(north, width - 1))
    e1, e2 = face_fluxes(e_own, east, True, slab(e_own, U), None, 0, 1, own_line_e, line_e)
    w1, w2 = face_fluxes(w_own, west, False, slab(west, U), None, 0, 1, own_line_w, line_w)
    for j, (we, ea) in enumerate(zip((*w1, *w2), (*e1, *e2))):
        flip_ref[pl.ds(2 * K * j, K, stride=2), :] = ea
        flip_ref[pl.ds(2 * K * j + 1, K, stride=2), :] = we
    tt_ref[...] = flip_ref[...].T


def main_kernel(
    pivot, t_ref, u_ref, v_ref, th_ref, sea_ref, dx_ref, dy_ref, xs, ys, xr, yr, f2r, own_w, own_e, pr, qr,
    out_ref, fy_ref, tt_ref, flip_ref, ghost_ref, geo, coef, sec,
):
    k = pl.program_id(0)
    rows = dx_ref.shape[0]
    chunks = rows // 8
    lane = lax.broadcasted_iota(jnp.int32, (8, 128), 1)
    sub = lax.broadcasted_iota(jnp.int32, (8, 128), 0)
    tiles = (slice(0, 128), slice(128, 256))

    def at(c):
        return slice(8 * c, 8 * c + 8)

    def east_of(x):
        moved = [pltpu.roll(v, 127, 1) for v in x]
        return [jnp.where(lane == 127, moved[1], moved[0]), moved[1]]

    def north_of(x, nxt):
        return [jnp.where(sub == 7, pltpu.roll(b, 7, 0), pltpu.roll(a, 7, 0)) for a, b in zip(x, nxt)]

    def both(ref, c, *lead):
        return [ref[(*lead, at(c), t)] for t in tiles]

    @pl.when(k == 0)
    def _():
        boundary(xs, ys, xr, yr, f2r, own_w, own_e, pr, qr, pivot, fy_ref, tt_ref, flip_ref, ghost_ref)
        for c in range(chunks):
            n = min(c + 1, chunks - 1)
            dx, dy = both(dx_ref, c), both(dy_ref, c)
            dx_e, dy_e = east_of(dx), east_of(dy)
            dx_n, dy_n = north_of(dx, both(dx_ref, n)), north_of(dy, both(dy_ref, n))
            for i, t in enumerate(tiles):
                geo[0, at(c), t] = 0.5 * (dy[i] + dy_e[i])
                geo[1, at(c), t] = 0.5 / (dx[i] + dx_e[i])
                geo[2, at(c), t] = 0.5 * (dx[i] + dx_n[i])
                geo[3, at(c), t] = 0.5 / (dy[i] + dy_n[i])
                geo[4, at(c), t] = -1.0 / (dx[i] * dy[i])

    def wet(c):
        return [a * b.astype(f32) for a, b in zip(both(th_ref, c, 0), both(sea_ref, c, 0))]

    w = wet(0)
    for c in range(chunks):
        w_next = wet(c + 1) if c + 1 < chunks else w
        w_e, w_n = east_of(w), north_of(w, w_next)
        u, v, th = both(u_ref, c, 0), both(v_ref, c, 0), both(th_ref, c, 0)
        for i, t in enumerate(tiles):
            g = geo[0, at(c), t] * jnp.minimum(w[i], w_e[i])
            e, h = geo[1, at(c), t], 0.5 * u[i]
            coef[0, at(c), t] = g * (h + e)
            coef[1, at(c), t] = g * (h - e)
            g = geo[2, at(c), t] * jnp.minimum(w[i], w_n[i])
            e, h = geo[3, at(c), t], 0.5 * v[i]
            coef[2, at(c), t] = g * (h + e)
            coef[3, at(c), t] = g * (h - e)
            coef[4, at(c), t] = geo[4, at(c), t] / th[i]
        w = w_next

    def stage(load, n, s, write):
        def row(i):
            r = fy_ref[pl.ds((4 * i + 2 * s + n) * K + k, 1), :]
            return [jnp.broadcast_to(r[:, t], (8, 128)) for t in tiles]

        below = row(0)
        top = row(1)
        x = load(0)
        for c in range(chunks):
            x_next = load(c + 1) if c + 1 < chunks else x
            a, b, p, q, r = [both(coef, c, j) for j in range(5)]
            ends = pltpu.roll(tt_ref[at(c), :], 127 - 2 * ((2 * s + n) * K + k), 1)
            x_e, x_n = east_of(x), north_of(x, x_next)
            fx = [a[i] * x[i] + b[i] * x_e[i] for i in range(2)]
            fx[1] = jnp.where(lane == 127, ends, fx[1])
            moved = [pltpu.roll(f, 1, 1) for f in fx]
            fx_w = [jnp.where(lane == 0, ends, moved[0]), jnp.where(lane == 0, moved[0], moved[1])]
            fy = [p[i] * x[i] + q[i] * x_n[i] for i in range(2)]
            if c == chunks - 1:
                fy = [jnp.where(sub == 7, top[i], fy[i]) for i in range(2)]
            up = [pltpu.roll(f, 1, 0) for f in fy]
            fy_s = [jnp.where(sub == 0, below[i], up[i]) for i in range(2)]
            below = up
            for i, t in enumerate(tiles):
                div = (fx[i] - fx_w[i]) + (fy[i] - fy_s[i])
                write(c, i, t, x[i], r[i] * div)
            x = x_next

    for n in range(2):

        def first(c, i, t, x, tend):
            sec[at(c), t] = x + STEP * tend
            out_ref[n, 0, at(c), t] = x + (0.5 * STEP) * tend

        def second(c, i, t, x, tend):
            sea = sea_ref[0, at(c), t].astype(f32)
            out_ref[n, 0, at(c), t] = sea * (out_ref[n, 0, at(c), t] + (0.5 * STEP) * tend)

        stage(lambda c: both(t_ref, c, n, 0), n, 0, first)
        stage(lambda c: both(sec, c), n, 1, second)


def pairs(count_lon, count_lat, partner):
    out = []
    for o in range(count_lon):
        for a in range(count_lat):
            to = partner(o, a)
            if to is not None:
                source, target = o * count_lat + a, (to[0] % count_lon) * count_lat + to[1]
                if source != target:
                    out.append((source, target))
    return out


def shards(nlon, nlat, tracers, zonal_vel, merid_vel, thickness, land_sea, cell_dx, cell_dy, fold_partner):
    rows, cols = cell_dx.shape
    axes = ("lon", "lat")
    end = nlat - 1

    def swap(x, partner):
        return lax.ppermute(x, axes, pairs(nlon, nlat, partner))

    def y_partner(o, a):
        if a == 0:
            return None
        if a == end:
            return (nlon - 1 - o, a)
        return (o, a + 1) if a % 2 else (o, a - 1)

    fields = (tracers, zonal_vel, merid_vel, thickness, land_sea, cell_dx, cell_dy)
    n = SLABS * K

    def edge(r):
        return [
            pl.BlockSpec((2, K, 8, cols), lambda i: (0, 0, r, 0)),
            *[pl.BlockSpec((K, 8, cols), lambda i: (0, r, 0))] * 4,
            *[pl.BlockSpec((8, cols), lambda i: (r, 0))] * 2,
        ]

    whole = pl.BlockSpec((n, cols), lambda i: (0, 0))
    line = jax.ShapeDtypeStruct((n, cols), f32)
    xs, ys = pl.pallas_call(
        rows_kernel,
        grid=(1,),
        in_specs=[*edge(0), *edge(rows // 8 - 1)],
        out_specs=[whole] * 2,
        out_shape=[line] * 2,
        compiler_params=pltpu.CompilerParams(vmem_limit_bytes=8 << 20),
        name="edge_rows",
    )(*[pltpu.with_memory_space_constraint(x, pltpu.HBM) for x in (*fields, *fields)])
    yr = swap(ys, y_partner)
    xr = swap(xs, lambda o, a: (o, a ^ 1))
    f2r = swap(ys, lambda o, a: (nlon - o, a) if a == end else None)

    level = [
        pl.BlockSpec((2, 1, rows, cols), lambda k: (0, k, 0, 0)),
        *[pl.BlockSpec((1, rows, cols), lambda k: (k, 0, 0))] * 4,
        *[pl.BlockSpec((rows, cols), lambda k: (0, 0))] * 2,
    ]
    side = jax.ShapeDtypeStruct((n, rows), f32)
    own_w, own_e = pl.pallas_call(
        cols_kernel,
        grid=(K,),
        in_specs=level,
        out_specs=[pl.BlockSpec((n, rows), lambda k: (0, 0))] * 2,
        out_shape=[side] * 2,
        scratch_shapes=[pltpu.VMEM((rows, 128), f32)] * 2 + [pltpu.VMEM((128, rows), f32)],
        cost_estimate=pl.CostEstimate(flops=4_000_000, bytes_accessed=7_000_000, transcendentals=0),
        compiler_params=pltpu.CompilerParams(vmem_limit_bytes=8 << 20),
        name="edge_cols",
    )(*fields)
    message = jax.ShapeDtypeStruct((n + K, rows), f32)
    ps, qs = pl.pallas_call(
        corners_kernel,
        out_shape=[message] * 2,
        compiler_params=pltpu.CompilerParams(vmem_limit_bytes=8 << 20),
        name="corners",
    )(xr, yr, own_w, own_e)
    qr = swap(qs, lambda o, a: (o + 1, a) if o % 2 else (o - 1, a))
    pr = swap(ps, lambda o, a: (o ^ 1, a))

    fixed = lambda shape: pl.BlockSpec(shape, lambda k: (0,) * len(shape))
    return pl.pallas_call(
        main_kernel,
        grid=(K,),
        in_specs=[pl.BlockSpec(memory_space=pltpu.SMEM), *level]
        + [fixed((n, cols))] * 5
        + [fixed((n, rows))] * 2
        + [fixed((n + K, rows))] * 2,
        out_specs=pl.BlockSpec((2, 1, rows, cols), lambda k: (0, k, 0, 0)),
        out_shape=jax.ShapeDtypeStruct(tracers.shape, f32),
        scratch_shapes=[
            pltpu.VMEM((8 * K, cols), f32),
            pltpu.VMEM((rows, 128), f32),
            pltpu.VMEM((128, rows), f32),
            pltpu.VMEM((n + K, cols + 128), f32),
            pltpu.VMEM((5, rows, cols), f32),
            pltpu.VMEM((5, rows, cols), f32),
            pltpu.VMEM((rows, cols), f32),
        ],
        compiler_params=pltpu.CompilerParams(vmem_limit_bytes=16 << 20),
        name="stencil",
    )(fold_partner, *fields, xs, ys, xr, yr, f2r, own_w, own_e, pr, qr)


def solution(mesh):
    return jax.shard_map(
        functools.partial(shards, mesh.shape["lon"], mesh.shape["lat"]),
        mesh=mesh,
        in_specs=(
            P(None, None, "lat", "lon"),
            P(None, "lat", "lon"),
            P(None, "lat", "lon"),
            P(None, "lat", "lon"),
            P(None, "lat", "lon"),
            P("lat", "lon"),
            P("lat", "lon"),
            P("lon"),
        ),
        out_specs=P(None, None, "lat", "lon"),
        check_vma=False,
    )
```

```python
import functools
import jax
import jax.numpy as jnp
from jax import lax
from jax.experimental import pallas as pl
from jax.experimental.pallas import tpu as pltpu
from jax.sharding import PartitionSpec as P


STEP = 0.2
K = 8
SLABS = 9
C0, C1, WET, U, V, TH, D, F0, F1 = range(SLABS)
f32 = jnp.float32


def coefs(vel, wa, wb, la, lb, da, db):
    g = (0.5 * (la + lb)) * jnp.minimum(wa, wb)
    e = 0.5 / (da + db)
    h = 0.5 * vel
    return g * (h + e), g * (h - e)


def slab(x, s):
    return x[s * K : (s + 1) * K]


def join(*parts):
    return jnp.concatenate(parts, axis=0)


def row_message(t_ref, u_ref, v_ref, th_ref, sea_ref, dx_ref, dy_ref, near, far, face):
    def wet(r):
        return th_ref[:, r, :] * sea_ref[:, r, :].astype(f32)

    w1, w2 = wet(near), wet(far)
    dx1, dx2 = dx_ref[near : near + 1, :], dx_ref[far : far + 1, :]
    dy1, dy2 = dy_ref[near : near + 1, :], dy_ref[far : far + 1, :]
    p, q = coefs(v_ref[:, face, :], w1, w2, dx1, dx2, dy1, dy2)
    if near > far:
        p, q = coefs(v_ref[:, face, :], w2, w1, dx2, dx1, dy2, dy1)
        p, q = q, p
    near_c = [t_ref[n, :, near, :] for n in range(2)]
    inner = [p * near_c[n] + q * t_ref[n, :, far, :] for n in range(2)]
    pad = jnp.zeros((6, dx1.shape[1]), f32)
    return join(
        *near_c,
        w1,
        u_ref[:, near, :],
        v_ref[:, near, :],
        th_ref[:, near, :],
        join(dx1, dy1, pad),
        *inner,
    )


def rows_kernel(*refs):
    low, high, (x_ref, y_ref) = refs[:7], refs[7:14], refs[14:]
    bottom = row_message(*low, 0, 1, 0)
    top = row_message(*high, 7, 6, 6)
    even = lax.axis_index("lat") % 2 == 0

    @pl.when(even)
    def _():
        x_ref[...] = top
        y_ref[...] = bottom

    @pl.when(jnp.logical_not(even))
    def _():
        x_ref[...] = bottom
        y_ref[...] = top


def cols_kernel(t_ref, u_ref, v_ref, th_ref, sea_ref, dx_ref, dy_ref, w_ref, e_ref, accw, acce, flip):
    k = pl.program_id(0)
    rows = dx_ref.shape[0]
    lane = lax.broadcasted_iota(jnp.int32, (rows, 128), 1)
    pair = lane >> 1

    def put(value, slot):
        for acc, part, shift in ((accw, value[:, :128], 0), (acce, value[:, -128:], 2)):
            moved = pltpu.roll(part, (2 * slot + shift) % 128, 1)
            acc[...] = jnp.where(pair == slot, moved, acc[...])

    @pl.when(k == 0)
    def _():
        accw[...] = jnp.zeros_like(accw)
        acce[...] = jnp.zeros_like(acce)
        put(dx_ref[...], 48)
        put(dy_ref[...], 49)

    th = th_ref[0]
    wet = th * sea_ref[0].astype(f32)
    for q, value in enumerate((t_ref[0, 0], t_ref[1, 0], wet, u_ref[0], v_ref[0], th)):
        put(value, 8 * q + k)

    @pl.when(k == K - 1)
    def _():
        for acc, out, near, far in ((accw, w_ref, 0, 1), (acce, e_ref, 1, 0)):
            flip[...] = acc[...].T

            def get(q, c):
                return flip[pl.ds(16 * q + c, K, stride=2), :]

            d1 = flip[pl.ds(96 + near, 2, stride=2), :]
            d2 = flip[pl.ds(96 + far, 2, stride=2), :]
            first, second = (near, far) if near < far else (far, near)
            da, db = (d1, d2) if near < far else (d2, d1)
            p, q = coefs(
                get(U, first), get(WET, first), get(WET, second), da[1:2], db[1:2], da[0:1], db[0:1]
            )
            for s in (C0, C1, WET, U, V, TH):
                out[s * K : (s + 1) * K, :] = get(s, near)
            out[D * K : (D + 1) * K, :] = join(d1, jnp.zeros((6, rows), f32))
            for n in range(2):
                out[(F0 + n) * K : (F0 + n + 1) * K, :] = p * get(n, first) + q * get(n, second)


CORNER = (C0, C1, WET, U, V, D)


def move(x, at, to):
    tile = x[:, at // 128 * 128 : at // 128 * 128 + 128]
    shift = (to - at) % 128
    return pltpu.roll(tile, shift, 1) if shift else tile


def corners_kernel(xr_ref, yr_ref, ys_ref, w_ref, e_ref, p_ref, q_ref, f_ref):
    even_lat = lax.axis_index("lat") % 2 == 0
    even_lon = lax.axis_index("lon") % 2 == 0
    north = jnp.where(even_lat, xr_ref[...], yr_ref[...])
    south = jnp.where(even_lat, yr_ref[...], xr_ref[...])
    lane = lax.broadcasted_iota(jnp.int32, (K, 128), 1)

    def corner(col):
        out = jnp.zeros((K, 128), f32)
        for base, rows in ((0, south), (8, north)):
            for at, s in enumerate(CORNER):
                out = jnp.where(lane == base + at, move(slab(rows, s), col, base + at), out)
        return out

    n = SLABS * K
    west, east = corner(0), corner(xr_ref.shape[1] - 1)
    f_ref[...] = ys_ref[...]

    @pl.when(even_lon)
    def _():
        p_ref[:n, :] = e_ref[...]
        p_ref[n:, :] = east
        q_ref[:n, :] = w_ref[...]
        q_ref[n:, :] = west

    @pl.when(jnp.logical_not(even_lon))
    def _():
        p_ref[:n, :] = w_ref[...]
        p_ref[n:, :] = west
        q_ref[:n, :] = e_ref[...]
        q_ref[n:, :] = east


def line_tendency(line, along, across, velocity, prev, nxt):
    n = line.shape[1]
    lane = lax.broadcasted_iota(jnp.int32, (K, 128), 1)

    def before(x, edge):
        moved = pltpu.roll(x, 1, 1)
        first = jnp.where(lane == 0, edge, moved[:, :128])
        return first if n == 128 else jnp.concatenate([first, moved[:, 128:]], axis=1)

    def after(x, edge):
        moved = pltpu.roll(x, n - 1, 1)
        last = jnp.where(lane == 127, edge, moved[:, -128:])
        return last if n == 128 else jnp.concatenate([moved[:, :-128], last], axis=1)

    def wide(x, i):
        return jnp.broadcast_to(x[i : i + 1], x.shape)

    d, wet, vel = slab(line, D), slab(line, WET), slab(line, velocity)
    al, ac = wide(d, along), wide(d, across)
    al_n, ac_n = after(al, wide(nxt["d"], along)), after(ac, wide(nxt["d"], across))
    al_p, ac_p = before(al, wide(prev["d"], along)), before(ac, wide(prev["d"], across))
    pn, qn = coefs(vel, wet, after(wet, nxt["w"]), ac, ac_n, al, al_n)
    pp, qp = coefs(before(vel, prev["vel"]), before(wet, prev["w"]), wet, ac_p, ac, al_p, al)
    out = []
    for t in range(2):
        C = slab(line, t)
        ahead = pn * C + qn * after(C, nxt["c"][t])
        behind = pp * before(C, prev["c"][t]) + qp * C
        out.append(ahead - behind)
    return out


def face_fluxes(own, ghost, own_vel_is_low, vel, ghost_vel, along, across, own_line, ghost_line):
    d, g = slab(own, D), slab(ghost, D)

    def face(velocity):
        lo, hi = (own, ghost) if own_vel_is_low else (ghost, own)
        dl, dh = (d, g) if own_vel_is_low else (g, d)
        return coefs(
            velocity,
            slab(lo, WET),
            slab(hi, WET),
            dl[across : across + 1],
            dh[across : across + 1],
            dl[along : along + 1],
            dh[along : along + 1],
        )

    def through(pq, a, b):
        return pq[0] * a + pq[1] * b if own_vel_is_low else pq[0] * b + pq[1] * a

    pq = face(vel)
    pq_ghost = pq if ghost_vel is None else face(ghost_vel)
    vol_own = d[0:1] * d[1:2] * slab(own, TH)
    vol_ghost = g[0:1] * g[1:2] * slab(ghost, TH)
    one, two = [], []
    for t in range(2):
        a, b = slab(own, t), slab(ghost, t)
        f = through(pq, a, b)
        fg = f if ghost_vel is None else through(pq_ghost, a, b)
        if own_vel_is_low:
            own_div = own_line[t] + (f - slab(own, F0 + t))
            ghost_div = ghost_line[t] + (slab(ghost, F0 + t) - fg)
        else:
            own_div = own_line[t] + (slab(own, F0 + t) - f)
            ghost_div = ghost_line[t] + (fg - slab(ghost, F0 + t))
        a2 = a - STEP * own_div / vol_own
        b2 = b - STEP * ghost_div / vol_ghost
        one.append(f)
        two.append(through(pq, a2, b2))
    return one, two


def boundary(xs, ys, xr, yr, f2r, own_w, own_e, pr, qr, pivot, fy_ref, tt_ref, flip_ref, ghost_ref):
    lat, lon = lax.axis_index("lat"), lax.axis_index("lon")
    last = lax.axis_size("lat") - 1
    even_lat, even_lon = lat % 2 == 0, lon % 2 == 0
    n = SLABS * K
    top = jnp.where(even_lat, xs[...], ys[...])
    bottom = jnp.where(even_lat, ys[...], xs[...])
    south = jnp.where(even_lat, yr[...], xr[...])
    west_all = jnp.where(even_lon, qr[...], pr[...])
    east_all = jnp.where(even_lon, pr[...], qr[...])
    west, east = west_all[:n], east_all[:n]
    cw, ce = west_all[n:], east_all[n:]
    w_own, e_own = own_w[...], own_e[...]
    width = top.shape[1]
    height = w_own.shape[1]

    @pl.when(lat != last)
    def _():
        ghost_ref[:n, :width] = jnp.where(even_lat, xr[...], yr[...])
        ghost_ref[n:, :width] = slab(top, V)
        tile = jnp.zeros((K, 128), f32)
        lane = lax.broadcasted_iota(jnp.int32, (K, 128), 1)
        for at, s in enumerate(CORNER):
            ends = jnp.where(lane == 0, move(cw, 8 + at, 0), tile)
            ends = jnp.where(lane == 1, move(ce, 8 + at, 1), ends)
            ghost_ref[s * K : (s + 1) * K, width:] = ends

    @pl.when(lat == last)
    def _():
        p = pivot[0] - (lax.axis_size("lon") * width - 1) + lon * width
        p = jnp.where(p <= 0, p + lax.axis_size("lon") * width, p)
        mine = (2 * lon) % lax.axis_size("lon") == 0
        both = jnp.concatenate([yr[...], jnp.where(mine, ys[...], f2r[...])], axis=1)
        src = lax.broadcasted_iota(jnp.int32, (2 * width, width + 128), 0)
        dst = lax.broadcasted_iota(jnp.int32, (2 * width, width + 128), 1)
        dst = jnp.where(dst == width, -1, jnp.where(dst == width + 1, width, dst))
        pick = (src == (width - 1) - dst + p).astype(f32)
        win = jnp.dot(both, pick, preferred_element_type=f32, precision=lax.Precision.HIGHEST)
        for s in (C0, C1, WET, TH, D):
            ghost_ref[s * K : (s + 1) * K, :] = slab(win, s)
        u = slab(win, U)
        lane = lax.broadcasted_iota(jnp.int32, (K, 128), 1)
        here = pltpu.roll(u[:, :width], width - 1, 1)
        last_tile = jnp.where(lane == 127, move(u, width + 1, 127), here[:, -128:])
        ghost_ref[U * K : (U + 1) * K, :width] = -jnp.concatenate([here[:, :-128], last_tile], axis=1)
        ghost_ref[U * K : (U + 1) * K, width:] = -u[:, :128]
        for s in (F0, F1):
            ghost_ref[s * K : (s + 1) * K, :] = -slab(win, s)
        ghost_ref[n:, :width] = -slab(win, V)[:, :width]

    north = ghost_ref[:n, :width]
    north_vel = ghost_ref[n:, :width]

    def cell(get, vel, to):
        return dict(c=[get(C0, to), get(C1, to)], w=get(WET, to), d=get(D, to), vel=vel and get(vel, to))

    def end(x, at, vel, to):
        return cell(lambda s, to: move(slab(x, s), at, to), vel, to)

    def corner(x, base, vel, to):
        return cell(lambda s, to: move(x, base + CORNER.index(s), to), vel, to)

    def ghost_end(at, vel, to):
        return cell(lambda s, to: move(ghost_ref[s * K : (s + 1) * K, width:], at, to), vel, to)

    def x_line(line, prev, nxt):
        return line_tendency(line, 0, 1, U, prev, nxt)

    def y_line(line, prev, nxt):
        return line_tendency(line, 1, 0, V, prev, nxt)

    line_n = x_line(north, ghost_end(0, U, 0), ghost_end(1, None, 127))
    line_s = x_line(south, corner(cw, 0, U, 0), corner(ce, 0, None, 127))
    line_top = x_line(top, end(west, height - 1, U, 0), end(east, height - 1, None, 127))
    line_bottom = x_line(bottom, end(west, 0, U, 0), end(east, 0, None, 127))
    n1, n2 = face_fluxes(top, north, True, slab(top, V), north_vel, 1, 0, line_top, line_n)
    s1, s2 = face_fluxes(bottom, south, False, slab(south, V), None, 1, 0, line_bottom, line_s)
    closed = lat == 0
    for i, value in enumerate((*s1, *s2)):
        fy_ref[i * K : (i + 1) * K, :] = jnp.where(closed, 0.0, value)
    for i, value in enumerate((*n1, *n2)):
        fy_ref[(4 + i) * K : (5 + i) * K, :] = value

    line_w = y_line(west, corner(cw, 0, V, 0), ghost_end(0, None, 127))
    line_e = y_line(east, corner(ce, 0, V, 0), ghost_end(1, None, 127))
    own_line_w = y_line(w_own, end(south, 0, V, 0), end(north, 0, None, 127))
    own_line_e = y_line(e_own, end(south, width - 1, V, 0), end(north, width - 1, None, 127))
    e1, e2 = face_fluxes(e_own, east, True, slab(e_own, U), None, 0, 1, own_line_e, line_e)
    w1, w2 = face_fluxes(w_own, west, False, slab(west, U), None, 0, 1, own_line_w, line_w)
    for j, (we, ea) in enumerate(zip((*w1, *w2), (*e1, *e2))):
        flip_ref[pl.ds(2 * K * j, K, stride=2), :] = ea
        flip_ref[pl.ds(2 * K * j + 1, K, stride=2), :] = we
    tt_ref[...] = flip_ref[...].T


TILES = (slice(0, 128), slice(128, 256))


def chunk(c):
    return slice(8 * c, 8 * c + 8)


def both(ref, c, *lead):
    return [ref[(*lead, chunk(c), t)] for t in TILES]


def lanes():
    return lax.broadcasted_iota(jnp.int32, (8, 128), 1)


def subs():
    return lax.broadcasted_iota(jnp.int32, (8, 128), 0)


def east_of(x):
    moved = [pltpu.roll(v, 127, 1) for v in x]
    return [jnp.where(lanes() == 127, moved[1], moved[0]), moved[1]]


def west_of(x):
    moved = [pltpu.roll(v, 1, 1) for v in x]
    return [moved[0], jnp.where(lanes() == 0, moved[0], moved[1])]


def up_rolled(x):
    return [pltpu.roll(v, 7, 0) for v in x]


def down_rolled(x):
    return [pltpu.roll(v, 1, 0) for v in x]


def pick(mask, x, y):
    return [jnp.where(mask, a, b) for a, b in zip(x, y)]


def apply(load, m_ref, k, chunks, write):
    x = load(0)
    up = up_rolled(x)
    below = x
    for c in range(chunks):
        x_next = load(c + 1) if c + 1 < chunks else x
        up_next, down = up_rolled(x_next), down_rolled(x)
        x_n, x_s = pick(subs() == 7, up_next, up), pick(subs() == 0, below, down)
        x_e, x_w = east_of(x), west_of(x)
        m = [both(m_ref, c, j, k) for j in range(5)]
        for i, t in enumerate(TILES):
            tend = (m[0][i] * x[i] + m[1][i] * x_e[i]) + (m[2][i] * x_w[i] + m[3][i] * x_n[i]) + m[4][i] * x_s[i]
            write(c, i, t, x[i], tend)
        x, up, below = x_next, up_next, down


def inner_kernel(t_ref, u_ref, v_ref, th_ref, sea_ref, dx_ref, dy_ref, m_ref, sec_ref, geo):
    rows = dx_ref.shape[0]
    chunks = rows // 8
    for c in range(chunks):
        n = min(c + 1, chunks - 1)
        dx, dy = both(dx_ref, c), both(dy_ref, c)
        dx_e, dy_e = east_of(dx), east_of(dy)
        dx_n, dy_n = (pick(subs() == 7, up_rolled(both(r, n)), up_rolled(x)) for r, x in ((dx_ref, dx), (dy_ref, dy)))
        for i, t in enumerate(TILES):
            geo[0, chunk(c), t] = 0.5 * (dy[i] + dy_e[i])
            geo[1, chunk(c), t] = 0.5 / (dx[i] + dx_e[i])
            geo[2, chunk(c), t] = 0.5 * (dx[i] + dx_n[i])
            geo[3, chunk(c), t] = 0.5 / (dy[i] + dy_n[i])
            geo[4, chunk(c), t] = (-0.5 * STEP) / (dx[i] * dy[i])

    def level(k, carry):
        def wet(c):
            return [a * b.astype(f32) for a, b in zip(both(th_ref, c, k), both(sea_ref, c, k))]

        w = wet(0)
        up = up_rolled(w)
        zero = jnp.zeros((8, 128), f32)
        p_below, q_below = [zero, zero], [zero, zero]
        for c in range(chunks):
            w_next = wet(c + 1) if c + 1 < chunks else w
            up_next = up_rolled(w_next)
            w_e, w_n = east_of(w), pick(subs() == 7, up_next, up)
            u, v, th = both(u_ref, c, k), both(v_ref, c, k), both(th_ref, c, k)
            gx, ex, gy, ey, dd = [both(geo, c, j) for j in range(5)]
            a, b, p, q = [], [], [], []
            for i in range(2):
                g, h = gx[i] * jnp.minimum(w[i], w_e[i]), 0.5 * u[i]
                if i == 1:
                    g = jnp.where(lanes() == 127, 0.0, g)
                a.append(g * (h + ex[i]))
                b.append(g * (h - ex[i]))
                g, h = gy[i] * jnp.minimum(w[i], w_n[i]), 0.5 * v[i]
                if c == chunks - 1:
                    g = jnp.where(subs() == 7, 0.0, g)
                p.append(g * (h + ey[i]))
                q.append(g * (h - ey[i]))
            a_w, b_w = west_of(a), west_of(b)
            a_w[0], b_w[0] = (jnp.where(lanes() == 0, 0.0, y[0]) for y in (a_w, b_w))
            p_down, q_down = down_rolled(p), down_rolled(q)
            p_s, q_s = pick(subs() == 0, p_below, p_down), pick(subs() == 0, q_below, q_down)
            for i, t in enumerate(TILES):
                r = dd[i] / th[i]
                m_ref[0, k, chunk(c), t] = r * ((a[i] - b_w[i]) + (p[i] - q_s[i]))
                m_ref[1, k, chunk(c), t] = r * b[i]
                m_ref[2, k, chunk(c), t] = -r * a_w[i]
                m_ref[3, k, chunk(c), t] = r * q[i]
                m_ref[4, k, chunk(c), t] = -r * p_s[i]
                m_ref[5, k, chunk(c), t] = r
            w, up, p_below, q_below = w_next, up_next, p_down, q_down
        for n in range(2):

            def write(c, i, t, x, tend):
                sec_ref[n, k, chunk(c), t] = x + 2.0 * tend

            apply(lambda c: both(t_ref, c, n, k), m_ref, k, chunks, write)
        return carry

    lax.fori_loop(0, K, level, 0)


def final_kernel(
    pivot, t_ref, sea_ref, m_ref, sec_ref, xs, ys, xr, yr, f2r, own_w, own_e, pr, qr,
    out_ref, fy_ref, tt_ref, flip_ref, ghost_ref, sec, done, sems,
):
    rows = sea_ref.shape[1]
    chunks = rows // 8
    boundary(xs, ys, xr, yr, f2r, own_w, own_e, pr, qr, pivot, fy_ref, tt_ref, flip_ref, ghost_ref)
    lane, sub = lanes(), subs()

    def edges(n, s, k):
        def row(i):
            r = fy_ref[pl.ds((4 * i + 2 * s + n) * K + k, 1), :]
            return [jnp.broadcast_to(r[:, t], (8, 128)) for t in TILES]

        south, north = row(0), row(1)

        def at(c):
            ends = pltpu.roll(tt_ref[chunk(c), :], 127 - 2 * ((2 * s + n) * K + k), 1)
            out = [jnp.where(lane == 0, -ends, 0.0), jnp.where(lane == 127, ends, 0.0)]
            if c == 0:
                out = [o - jnp.where(sub == 0, f, 0.0) for o, f in zip(out, south)]
            if c == chunks - 1:
                out = [o + jnp.where(sub == 7, f, 0.0) for o, f in zip(out, north)]
            return out

        return at

    def copy(k):
        return pltpu.make_async_copy(done.at[:, pl.ds(k, 1)], out_ref.at[:, pl.ds(k, 1)], sems.at[k])

    def level(k, carry):
        for n in range(2):
            at = edges(n, 0, k)
            for c in range(chunks):
                add = at(c)
                r, x = both(m_ref, c, 5, k), both(sec_ref, c, n, k)
                for i, t in enumerate(TILES):
                    sec[n, chunk(c), t] = x[i] + 2.0 * (r[i] * add[i])
        for n in range(2):
            at = edges(n, 1, k)

            def write(c, i, t, x, tend):
                add = at(c)[i]
                total = 0.5 * (t_ref[n, k, chunk(c), t] + x) + (tend + m_ref[5, k, chunk(c), t] * add)
                done[n, k, chunk(c), t] = jnp.where(sea_ref[k, chunk(c), t] > 0, total, 0.0)

            apply(lambda c: both(sec, c, n), m_ref, k, chunks, write)
        copy(k).start()
        return carry

    lax.fori_loop(0, K, level, 0)
    for k in range(K):
        copy(k).wait()


def pairs(count_lon, count_lat, partner):
    out = []
    for o in range(count_lon):
        for a in range(count_lat):
            to = partner(o, a)
            if to is not None:
                source, target = o * count_lat + a, (to[0] % count_lon) * count_lat + to[1]
                if source != target:
                    out.append((source, target))
    return out


def shards(nlon, nlat, tracers, zonal_vel, merid_vel, thickness, land_sea, cell_dx, cell_dy, fold_partner):
    rows, cols = cell_dx.shape
    axes = ("lon", "lat")
    end = nlat - 1

    def swap(x, partner):
        return lax.ppermute(x, axes, pairs(nlon, nlat, partner))

    def y_partner(o, a):
        if a == 0:
            return None
        if a == end:
            return (nlon - 1 - o, a)
        return (o, a + 1) if a % 2 else (o, a - 1)

    fields = (tracers, zonal_vel, merid_vel, thickness, land_sea, cell_dx, cell_dy)
    n = SLABS * K

    def edge(r):
        return [
            pl.BlockSpec((2, K, 8, cols), lambda i: (0, 0, r, 0)),
            *[pl.BlockSpec((K, 8, cols), lambda i: (0, r, 0))] * 4,
            *[pl.BlockSpec((8, cols), lambda i: (r, 0))] * 2,
        ]

    whole = pl.BlockSpec((n, cols), lambda i: (0, 0))
    line = jax.ShapeDtypeStruct((n, cols), f32)
    xs, ys = pl.pallas_call(
        rows_kernel,
        grid=(1,),
        in_specs=[*edge(0), *edge(rows // 8 - 1)],
        out_specs=[whole] * 2,
        out_shape=[line] * 2,
        compiler_params=pltpu.CompilerParams(vmem_limit_bytes=8 << 20),
        name="edge_rows",
    )(*[pltpu.with_memory_space_constraint(x, pltpu.HBM) for x in (*fields, *fields)])
    xr = swap(xs, lambda o, a: (o, a ^ 1))
    yr = swap(ys, y_partner)

    level = [
        pl.BlockSpec((2, 1, rows, cols), lambda k: (0, k, 0, 0)),
        *[pl.BlockSpec((1, rows, cols), lambda k: (k, 0, 0))] * 4,
        *[pl.BlockSpec((rows, cols), lambda k: (0, 0))] * 2,
    ]
    side = jax.ShapeDtypeStruct((n, rows), f32)
    own_w, own_e = pl.pallas_call(
        cols_kernel,
        grid=(K,),
        in_specs=level,
        out_specs=[pl.BlockSpec((n, rows), lambda k: (0, 0))] * 2,
        out_shape=[side] * 2,
        scratch_shapes=[pltpu.VMEM((rows, 128), f32)] * 2 + [pltpu.VMEM((128, rows), f32)],
        cost_estimate=pl.CostEstimate(flops=4_000_000, bytes_accessed=7_000_000, transcendentals=0),
        compiler_params=pltpu.CompilerParams(vmem_limit_bytes=8 << 20),
        name="edge_cols",
    )(*fields)
    message = jax.ShapeDtypeStruct((n + K, rows), f32)
    ps, qs, fs = pl.pallas_call(
        corners_kernel,
        out_shape=[message, message, line],
        compiler_params=pltpu.CompilerParams(vmem_limit_bytes=8 << 20),
        name="corners",
    )(xr, yr, ys, own_w, own_e)
    qr = swap(qs, lambda o, a: (o + 1, a) if o % 2 else (o - 1, a))
    pr = swap(ps, lambda o, a: (o ^ 1, a))
    f2r = swap(fs, lambda o, a: (nlon - o, a) if a == end else None)

    vmem = pl.BlockSpec(memory_space=pltpu.VMEM)
    whole_field = (K, rows, cols)
    m, sec = pl.pallas_call(
        inner_kernel,
        in_specs=[vmem] * 7,
        out_specs=[vmem] * 2,
        out_shape=[
            jax.ShapeDtypeStruct((6, *whole_field), f32),
            jax.ShapeDtypeStruct((2, *whole_field), f32),
        ],
        scratch_shapes=[pltpu.VMEM((5, rows, cols), f32)],
        cost_estimate=pl.CostEstimate(flops=20_000_000, bytes_accessed=14_000_000, transcendentals=0),
        compiler_params=pltpu.CompilerParams(vmem_limit_bytes=18 << 20),
        name="inner",
    )(*fields)
    return pl.pallas_call(
        final_kernel,
        in_specs=[pl.BlockSpec(memory_space=pltpu.SMEM)] + [vmem] * 13,
        out_specs=pl.BlockSpec(memory_space=pl.ANY),
        out_shape=jax.ShapeDtypeStruct(tracers.shape, f32),
        scratch_shapes=[
            pltpu.VMEM((8 * K, cols), f32),
            pltpu.VMEM((rows, 128), f32),
            pltpu.VMEM((128, rows), f32),
            pltpu.VMEM((n + K, cols + 128), f32),
            pltpu.VMEM((2, rows, cols), f32),
            pltpu.VMEM((2, *whole_field), f32),
            pltpu.SemaphoreType.DMA((K,)),
        ],
        cost_estimate=pl.CostEstimate(flops=20_000_000, bytes_accessed=14_000_000, transcendentals=0),
        compiler_params=pltpu.CompilerParams(vmem_limit_bytes=18 << 20),
        name="final",
    )(fold_partner, tracers, land_sea, m, sec, xs, ys, xr, yr, f2r, own_w, own_e, pr, qr)


def solution(mesh):
    return jax.shard_map(
        functools.partial(shards, mesh.shape["lon"], mesh.shape["lat"]),
        mesh=mesh,
        in_specs=(
            P(None, None, "lat", "lon"),
            P(None, "lat", "lon"),
            P(None, "lat", "lon"),
            P(None, "lat", "lon"),
            P(None, "lat", "lon"),
            P("lat", "lon"),
            P("lat", "lon"),
            P("lon"),
        ),
        out_specs=P(None, None, "lat", "lon"),
        check_vma=False,
    )
```

```python
import functools
import jax
import jax.numpy as jnp
from jax import lax
from jax.experimental import pallas as pl
from jax.experimental.pallas import tpu as pltpu
from jax.sharding import PartitionSpec as P


STEP = 0.2
K = 8
SLABS = 9
C0, C1, WET, U, V, TH, D, F0, F1 = range(SLABS)
f32 = jnp.float32


def coefs(vel, wa, wb, la, lb, da, db):
    g = (0.5 * (la + lb)) * jnp.minimum(wa, wb)
    e = 0.5 / (da + db)
    h = 0.5 * vel
    return g * (h + e), g * (h - e)


def slab(x, s):
    return x[s * K : (s + 1) * K]


def join(*parts):
    return jnp.concatenate(parts, axis=0)


def row_message(t_ref, u_ref, v_ref, th_ref, sea_ref, dx_ref, dy_ref, near, far, face):
    def wet(r):
        return th_ref[:, r, :] * sea_ref[:, r, :].astype(f32)

    w1, w2 = wet(near), wet(far)
    dx1, dx2 = dx_ref[near : near + 1, :], dx_ref[far : far + 1, :]
    dy1, dy2 = dy_ref[near : near + 1, :], dy_ref[far : far + 1, :]
    p, q = coefs(v_ref[:, face, :], w1, w2, dx1, dx2, dy1, dy2)
    if near > far:
        p, q = coefs(v_ref[:, face, :], w2, w1, dx2, dx1, dy2, dy1)
        p, q = q, p
    near_c = [t_ref[n, :, near, :] for n in range(2)]
    inner = [p * near_c[n] + q * t_ref[n, :, far, :] for n in range(2)]
    pad = jnp.zeros((6, dx1.shape[1]), f32)
    return join(
        *near_c,
        w1,
        u_ref[:, near, :],
        v_ref[:, near, :],
        th_ref[:, near, :],
        join(dx1, dy1, pad),
        *inner,
    )


def rows_kernel(*refs):
    low, high, (x_ref, y_ref) = refs[:7], refs[7:14], refs[14:]
    bottom = row_message(*low, 0, 1, 0)
    top = row_message(*high, 7, 6, 6)
    even = lax.axis_index("lat") % 2 == 0

    @pl.when(even)
    def _():
        x_ref[...] = top
        y_ref[...] = bottom

    @pl.when(jnp.logical_not(even))
    def _():
        x_ref[...] = bottom
        y_ref[...] = top


def cols_kernel(t_ref, u_ref, v_ref, th_ref, sea_ref, dx_ref, dy_ref, w_ref, e_ref, accw, acce, flip):
    k = pl.program_id(0)
    rows = dx_ref.shape[0]
    lane = lax.broadcasted_iota(jnp.int32, (rows, 128), 1)
    pair = lane >> 1

    def put(value, slot):
        for acc, part, shift in ((accw, value[:, :128], 0), (acce, value[:, -128:], 2)):
            moved = pltpu.roll(part, (2 * slot + shift) % 128, 1)
            acc[...] = jnp.where(pair == slot, moved, acc[...])

    @pl.when(k == 0)
    def _():
        accw[...] = jnp.zeros_like(accw)
        acce[...] = jnp.zeros_like(acce)
        put(dx_ref[...], 48)
        put(dy_ref[...], 49)

    th = th_ref[0]
    wet = th * sea_ref[0].astype(f32)
    for q, value in enumerate((t_ref[0, 0], t_ref[1, 0], wet, u_ref[0], v_ref[0], th)):
        put(value, 8 * q + k)

    @pl.when(k == K - 1)
    def _():
        for acc, out, near, far in ((accw, w_ref, 0, 1), (acce, e_ref, 1, 0)):
            flip[...] = acc[...].T

            def get(q, c):
                return flip[pl.ds(16 * q + c, K, stride=2), :]

            d1 = flip[pl.ds(96 + near, 2, stride=2), :]
            d2 = flip[pl.ds(96 + far, 2, stride=2), :]
            first, second = (near, far) if near < far else (far, near)
            da, db = (d1, d2) if near < far else (d2, d1)
            p, q = coefs(
                get(U, first), get(WET, first), get(WET, second), da[1:2], db[1:2], da[0:1], db[0:1]
            )
            for s in (C0, C1, WET, U, V, TH):
                out[s * K : (s + 1) * K, :] = get(s, near)
            out[D * K : (D + 1) * K, :] = join(d1, jnp.zeros((6, rows), f32))
            for n in range(2):
                out[(F0 + n) * K : (F0 + n + 1) * K, :] = p * get(n, first) + q * get(n, second)


CORNER = (C0, C1, WET, U, V, D)


def move(x, at, to):
    tile = x[:, at // 128 * 128 : at // 128 * 128 + 128]
    shift = (to - at) % 128
    return pltpu.roll(tile, shift, 1) if shift else tile


def corners_kernel(xr_ref, yr_ref, w_ref, e_ref, p_ref, q_ref):
    even_lat = lax.axis_index("lat") % 2 == 0
    even_lon = lax.axis_index("lon") % 2 == 0
    north = jnp.where(even_lat, xr_ref[...], yr_ref[...])
    south = jnp.where(even_lat, yr_ref[...], xr_ref[...])
    lane = lax.broadcasted_iota(jnp.int32, (K, 128), 1)

    def corner(col):
        out = jnp.zeros((K, 128), f32)
        for base, rows in ((0, south), (8, north)):
            for at, s in enumerate(CORNER):
                out = jnp.where(lane == base + at, move(slab(rows, s), col, base + at), out)
        return out

    n = SLABS * K
    west, east = corner(0), corner(xr_ref.shape[1] - 1)
    for ref in (p_ref, q_ref):
        ref[n + K : 2 * n + K, :] = yr_ref[:, :128]
        ref[2 * n + K :, :] = yr_ref[:, 128:]

    @pl.when(even_lon)
    def _():
        p_ref[:n, :] = e_ref[...]
        p_ref[n : n + K, :] = east
        q_ref[:n, :] = w_ref[...]
        q_ref[n : n + K, :] = west

    @pl.when(jnp.logical_not(even_lon))
    def _():
        p_ref[:n, :] = w_ref[...]
        p_ref[n : n + K, :] = west
        q_ref[:n, :] = e_ref[...]
        q_ref[n : n + K, :] = east


def line_tendency(line, along, across, velocity, prev, nxt):
    n = line.shape[1]
    lane = lax.broadcasted_iota(jnp.int32, (K, 128), 1)

    def before(x, edge):
        moved = pltpu.roll(x, 1, 1)
        first = jnp.where(lane == 0, edge, moved[:, :128])
        return first if n == 128 else jnp.concatenate([first, moved[:, 128:]], axis=1)

    def after(x, edge):
        moved = pltpu.roll(x, n - 1, 1)
        last = jnp.where(lane == 127, edge, moved[:, -128:])
        return last if n == 128 else jnp.concatenate([moved[:, :-128], last], axis=1)

    def wide(x, i):
        return jnp.broadcast_to(x[i : i + 1], x.shape)

    d, wet, vel = slab(line, D), slab(line, WET), slab(line, velocity)
    al, ac = wide(d, along), wide(d, across)
    al_n, ac_n = after(al, wide(nxt["d"], along)), after(ac, wide(nxt["d"], across))
    al_p, ac_p = before(al, wide(prev["d"], along)), before(ac, wide(prev["d"], across))
    pn, qn = coefs(vel, wet, after(wet, nxt["w"]), ac, ac_n, al, al_n)
    pp, qp = coefs(before(vel, prev["vel"]), before(wet, prev["w"]), wet, ac_p, ac, al_p, al)
    out = []
    for t in range(2):
        C = slab(line, t)
        ahead = pn * C + qn * after(C, nxt["c"][t])
        behind = pp * before(C, prev["c"][t]) + qp * C
        out.append(ahead - behind)
    return out


def face_fluxes(own, ghost, own_vel_is_low, vel, ghost_vel, along, across, own_line, ghost_line):
    d, g = slab(own, D), slab(ghost, D)

    def face(velocity):
        lo, hi = (own, ghost) if own_vel_is_low else (ghost, own)
        dl, dh = (d, g) if own_vel_is_low else (g, d)
        return coefs(
            velocity,
            slab(lo, WET),
            slab(hi, WET),
            dl[across : across + 1],
            dh[across : across + 1],
            dl[along : along + 1],
            dh[along : along + 1],
        )

    def through(pq, a, b):
        return pq[0] * a + pq[1] * b if own_vel_is_low else pq[0] * b + pq[1] * a

    pq = face(vel)
    pq_ghost = pq if ghost_vel is None else face(ghost_vel)
    vol_own = d[0:1] * d[1:2] * slab(own, TH)
    vol_ghost = g[0:1] * g[1:2] * slab(ghost, TH)
    one, two = [], []
    for t in range(2):
        a, b = slab(own, t), slab(ghost, t)
        f = through(pq, a, b)
        fg = f if ghost_vel is None else through(pq_ghost, a, b)
        if own_vel_is_low:
            own_div = own_line[t] + (f - slab(own, F0 + t))
            ghost_div = ghost_line[t] + (slab(ghost, F0 + t) - fg)
        else:
            own_div = own_line[t] + (slab(own, F0 + t) - f)
            ghost_div = ghost_line[t] + (fg - slab(ghost, F0 + t))
        a2 = a - STEP * own_div / vol_own
        b2 = b - STEP * ghost_div / vol_ghost
        one.append(f)
        two.append(through(pq, a2, b2))
    return one, two


def boundary(xs, ys, xr, yr, own_w, own_e, pr, qr, pivot, fy_ref, tt_ref, flip_ref, ghost_ref):
    lat, lon = lax.axis_index("lat"), lax.axis_index("lon")
    last = lax.axis_size("lat") - 1
    even_lat, even_lon = lat % 2 == 0, lon % 2 == 0
    n = SLABS * K
    top = jnp.where(even_lat, xs[...], ys[...])
    bottom = jnp.where(even_lat, ys[...], xs[...])
    south = jnp.where(even_lat, yr[...], xr[...])
    west_all = jnp.where(even_lon, qr[...], pr[...])
    east_all = jnp.where(even_lon, pr[...], qr[...])
    west, east = west_all[:n], east_all[:n]
    cw, ce = west_all[n : n + K], east_all[n : n + K]
    w_own, e_own = own_w[...], own_e[...]
    width = top.shape[1]
    height = w_own.shape[1]

    @pl.when(lat != last)
    def _():
        ghost_ref[:n, :width] = jnp.where(even_lat, xr[...], yr[...])
        ghost_ref[n:, :width] = slab(top, V)
        tile = jnp.zeros((K, 128), f32)
        lane = lax.broadcasted_iota(jnp.int32, (K, 128), 1)
        for at, s in enumerate(CORNER):
            ends = jnp.where(lane == 0, move(cw, 8 + at, 0), tile)
            ends = jnp.where(lane == 1, move(ce, 8 + at, 1), ends)
            ghost_ref[s * K : (s + 1) * K, width:] = ends

    @pl.when(lat == last)
    def _():
        p = pivot[0] - (lax.axis_size("lon") * width - 1) + lon * width
        p = jnp.where(p <= 0, p + lax.axis_size("lon") * width, p)
        both = jnp.concatenate([yr[...], west_all[n + K : 2 * n + K], west_all[2 * n + K :]], axis=1)
        src = lax.broadcasted_iota(jnp.int32, (2 * width, width + 128), 0)
        dst = lax.broadcasted_iota(jnp.int32, (2 * width, width + 128), 1)
        dst = jnp.where(dst == width, -1, jnp.where(dst == width + 1, width, dst))
        pick = (src == (width - 1) - dst + p).astype(f32)
        win = jnp.dot(both, pick, preferred_element_type=f32, precision=lax.Precision.HIGHEST)
        for s in (C0, C1, WET, TH, D):
            ghost_ref[s * K : (s + 1) * K, :] = slab(win, s)
        u = slab(win, U)
        lane = lax.broadcasted_iota(jnp.int32, (K, 128), 1)
        here = pltpu.roll(u[:, :width], width - 1, 1)
        last_tile = jnp.where(lane == 127, move(u, width + 1, 127), here[:, -128:])
        ghost_ref[U * K : (U + 1) * K, :width] = -jnp.concatenate([here[:, :-128], last_tile], axis=1)
        ghost_ref[U * K : (U + 1) * K, width:] = -u[:, :128]
        for s in (F0, F1):
            ghost_ref[s * K : (s + 1) * K, :] = -slab(win, s)
        ghost_ref[n:, :width] = -slab(win, V)[:, :width]

    north = ghost_ref[:n, :width]
    north_vel = ghost_ref[n:, :width]

    def cell(get, vel, to):
        return dict(c=[get(C0, to), get(C1, to)], w=get(WET, to), d=get(D, to), vel=vel and get(vel, to))

    def end(x, at, vel, to):
        return cell(lambda s, to: move(slab(x, s), at, to), vel, to)

    def corner(x, base, vel, to):
        return cell(lambda s, to: move(x, base + CORNER.index(s), to), vel, to)

    def ghost_end(at, vel, to):
        return cell(lambda s, to: move(ghost_ref[s * K : (s + 1) * K, width:], at, to), vel, to)

    def x_line(line, prev, nxt):
        return line_tendency(line, 0, 1, U, prev, nxt)

    def y_line(line, prev, nxt):
        return line_tendency(line, 1, 0, V, prev, nxt)

    line_n = x_line(north, ghost_end(0, U, 0), ghost_end(1, None, 127))
    line_s = x_line(south, corner(cw, 0, U, 0), corner(ce, 0, None, 127))
    line_top = x_line(top, end(west, height - 1, U, 0), end(east, height - 1, None, 127))
    line_bottom = x_line(bottom, end(west, 0, U, 0), end(east, 0, None, 127))
    n1, n2 = face_fluxes(top, north, True, slab(top, V), north_vel, 1, 0, line_top, line_n)
    s1, s2 = face_fluxes(bottom, south, False, slab(south, V), None, 1, 0, line_bottom, line_s)
    closed = lat == 0
    for i, value in enumerate((*s1, *s2)):
        fy_ref[i * K : (i + 1) * K, :] = jnp.where(closed, 0.0, value)
    for i, value in enumerate((*n1, *n2)):
        fy_ref[(4 + i) * K : (5 + i) * K, :] = value

    line_w = y_line(west, corner(cw, 0, V, 0), ghost_end(0, None, 127))
    line_e = y_line(east, corner(ce, 0, V, 0), ghost_end(1, None, 127))
    own_line_w = y_line(w_own, end(south, 0, V, 0), end(north, 0, None, 127))
    own_line_e = y_line(e_own, end(south, width - 1, V, 0), end(north, width - 1, None, 127))
    e1, e2 = face_fluxes(e_own, east, True, slab(e_own, U), None, 0, 1, own_line_e, line_e)
    w1, w2 = face_fluxes(w_own, west, False, slab(west, U), None, 0, 1, own_line_w, line_w)
    for j, (we, ea) in enumerate(zip((*w1, *w2), (*e1, *e2))):
        flip_ref[pl.ds(2 * K * j, K, stride=2), :] = ea
        flip_ref[pl.ds(2 * K * j + 1, K, stride=2), :] = we
    tt_ref[...] = flip_ref[...].T


TILES = (slice(0, 128), slice(128, 256))


def chunk(c):
    return slice(8 * c, 8 * c + 8)


def both(ref, c, *lead):
    return [ref[(*lead, chunk(c), t)] for t in TILES]


def lanes():
    return lax.broadcasted_iota(jnp.int32, (8, 128), 1)


def subs():
    return lax.broadcasted_iota(jnp.int32, (8, 128), 0)


def east_of(x):
    moved = [pltpu.roll(v, 127, 1) for v in x]
    return [jnp.where(lanes() == 127, moved[1], moved[0]), moved[1]]


def west_of(x):
    moved = [pltpu.roll(v, 1, 1) for v in x]
    return [moved[0], jnp.where(lanes() == 0, moved[0], moved[1])]


def up_rolled(x):
    return [pltpu.roll(v, 7, 0) for v in x]


def down_rolled(x):
    return [pltpu.roll(v, 1, 0) for v in x]


def pick(mask, x, y):
    return [jnp.where(mask, a, b) for a, b in zip(x, y)]


def apply(load, m_ref, k, chunks, write):
    x = load(0)
    up = up_rolled(x)
    below = x
    for c in range(chunks):
        x_next = load(c + 1) if c + 1 < chunks else x
        up_next, down = up_rolled(x_next), down_rolled(x)
        x_n, x_s = pick(subs() == 7, up_next, up), pick(subs() == 0, below, down)
        x_e, x_w = east_of(x), west_of(x)
        m = [both(m_ref, c, j, k) for j in range(5)]
        for i, t in enumerate(TILES):
            tend = (m[0][i] * x[i] + m[1][i] * x_e[i]) + (m[2][i] * x_w[i] + m[3][i] * x_n[i]) + m[4][i] * x_s[i]
            write(c, i, t, x[i], tend)
        x, up, below = x_next, up_next, down


def inner_kernel(t_ref, u_ref, v_ref, th_ref, sea_ref, dx_ref, dy_ref, m_ref, sec_ref, geo):
    rows = dx_ref.shape[0]
    chunks = rows // 8
    for c in range(chunks):
        n = min(c + 1, chunks - 1)
        dx, dy = both(dx_ref, c), both(dy_ref, c)
        dx_e, dy_e = east_of(dx), east_of(dy)
        dx_n, dy_n = (pick(subs() == 7, up_rolled(both(r, n)), up_rolled(x)) for r, x in ((dx_ref, dx), (dy_ref, dy)))
        for i, t in enumerate(TILES):
            geo[0, chunk(c), t] = 0.5 * (dy[i] + dy_e[i])
            geo[1, chunk(c), t] = 0.5 / (dx[i] + dx_e[i])
            geo[2, chunk(c), t] = 0.5 * (dx[i] + dx_n[i])
            geo[3, chunk(c), t] = 0.5 / (dy[i] + dy_n[i])
            geo[4, chunk(c), t] = (-0.5 * STEP) / (dx[i] * dy[i])

    def level(k, carry):
        def wet(c):
            return [a * b.astype(f32) for a, b in zip(both(th_ref, c, k), both(sea_ref, c, k))]

        w = wet(0)
        up = up_rolled(w)
        zero = jnp.zeros((8, 128), f32)
        p_below, q_below = [zero, zero], [zero, zero]
        for c in range(chunks):
            w_next = wet(c + 1) if c + 1 < chunks else w
            up_next = up_rolled(w_next)
            w_e, w_n = east_of(w), pick(subs() == 7, up_next, up)
            u, v, th = both(u_ref, c, k), both(v_ref, c, k), both(th_ref, c, k)
            gx, ex, gy, ey, dd = [both(geo, c, j) for j in range(5)]
            a, b, p, q = [], [], [], []
            for i in range(2):
                g, h = gx[i] * jnp.minimum(w[i], w_e[i]), 0.5 * u[i]
                if i == 1:
                    g = jnp.where(lanes() == 127, 0.0, g)
                a.append(g * (h + ex[i]))
                b.append(g * (h - ex[i]))
                g, h = gy[i] * jnp.minimum(w[i], w_n[i]), 0.5 * v[i]
                if c == chunks - 1:
                    g = jnp.where(subs() == 7, 0.0, g)
                p.append(g * (h + ey[i]))
                q.append(g * (h - ey[i]))
            a_w, b_w = west_of(a), west_of(b)
            a_w[0], b_w[0] = (jnp.where(lanes() == 0, 0.0, y[0]) for y in (a_w, b_w))
            p_down, q_down = down_rolled(p), down_rolled(q)
            p_s, q_s = pick(subs() == 0, p_below, p_down), pick(subs() == 0, q_below, q_down)
            for i, t in enumerate(TILES):
                r = dd[i] / th[i]
                m_ref[0, k, chunk(c), t] = r * ((a[i] - b_w[i]) + (p[i] - q_s[i]))
                m_ref[1, k, chunk(c), t] = r * b[i]
                m_ref[2, k, chunk(c), t] = -r * a_w[i]
                m_ref[3, k, chunk(c), t] = r * q[i]
                m_ref[4, k, chunk(c), t] = -r * p_s[i]
                m_ref[5, k, chunk(c), t] = r
            w, up, p_below, q_below = w_next, up_next, p_down, q_down
        for n in range(2):

            def write(c, i, t, x, tend):
                sec_ref[n, k, chunk(c), t] = x + 2.0 * tend

            apply(lambda c: both(t_ref, c, n, k), m_ref, k, chunks, write)
        return carry

    lax.fori_loop(0, K, level, 0)


def final_kernel(
    pivot, t_ref, sea_ref, m_ref, sec_ref, xs, ys, xr, yr, own_w, own_e, pr, qr,
    out_ref, fy_ref, tt_ref, flip_ref, ghost_ref, sec, done, sems,
):
    rows = sea_ref.shape[1]
    chunks = rows // 8
    boundary(xs, ys, xr, yr, own_w, own_e, pr, qr, pivot, fy_ref, tt_ref, flip_ref, ghost_ref)
    lane, sub = lanes(), subs()

    def edges(n, s, k):
        def row(i):
            r = fy_ref[pl.ds((4 * i + 2 * s + n) * K + k, 1), :]
            return [jnp.broadcast_to(r[:, t], (8, 128)) for t in TILES]

        south, north = row(0), row(1)

        def at(c):
            ends = pltpu.roll(tt_ref[chunk(c), :], 127 - 2 * ((2 * s + n) * K + k), 1)
            out = [jnp.where(lane == 0, -ends, 0.0), jnp.where(lane == 127, ends, 0.0)]
            if c == 0:
                out = [o - jnp.where(sub == 0, f, 0.0) for o, f in zip(out, south)]
            if c == chunks - 1:
                out = [o + jnp.where(sub == 7, f, 0.0) for o, f in zip(out, north)]
            return out

        return at

    def copy(k):
        return pltpu.make_async_copy(done.at[:, pl.ds(k, 1)], out_ref.at[:, pl.ds(k, 1)], sems.at[k])

    def level(k, carry):
        for n in range(2):
            at = edges(n, 0, k)
            for c in range(chunks):
                add = at(c)
                r, x = both(m_ref, c, 5, k), both(sec_ref, c, n, k)
                for i, t in enumerate(TILES):
                    sec[n, chunk(c), t] = x[i] + 2.0 * (r[i] * add[i])
        for n in range(2):
            at = edges(n, 1, k)

            def write(c, i, t, x, tend):
                add = at(c)[i]
                total = 0.5 * (t_ref[n, k, chunk(c), t] + x) + (tend + m_ref[5, k, chunk(c), t] * add)
                done[n, k, chunk(c), t] = jnp.where(sea_ref[k, chunk(c), t] > 0, total, 0.0)

            apply(lambda c: both(sec, c, n), m_ref, k, chunks, write)
        copy(k).start()
        return carry

    lax.fori_loop(0, K, level, 0)
    for k in range(K):
        copy(k).wait()


def pairs(count_lon, count_lat, partner):
    out = []
    for o in range(count_lon):
        for a in range(count_lat):
            to = partner(o, a)
            if to is not None:
                source, target = o * count_lat + a, (to[0] % count_lon) * count_lat + to[1]
                if source != target:
                    out.append((source, target))
    return out


def shards(nlon, nlat, tracers, zonal_vel, merid_vel, thickness, land_sea, cell_dx, cell_dy, fold_partner):
    rows, cols = cell_dx.shape
    axes = ("lon", "lat")
    end = nlat - 1

    def swap(x, partner):
        return lax.ppermute(x, axes, pairs(nlon, nlat, partner))

    def y_partner(o, a):
        if a == 0:
            return None
        if a == end:
            return (nlon - 1 - o, a)
        return (o, a + 1) if a % 2 else (o, a - 1)

    fields = (tracers, zonal_vel, merid_vel, thickness, land_sea, cell_dx, cell_dy)
    n = SLABS * K

    def edge(r):
        return [
            pl.BlockSpec((2, K, 8, cols), lambda i: (0, 0, r, 0)),
            *[pl.BlockSpec((K, 8, cols), lambda i: (0, r, 0))] * 4,
            *[pl.BlockSpec((8, cols), lambda i: (r, 0))] * 2,
        ]

    whole = pl.BlockSpec((n, cols), lambda i: (0, 0))
    line = jax.ShapeDtypeStruct((n, cols), f32)
    xs, ys = pl.pallas_call(
        rows_kernel,
        grid=(1,),
        in_specs=[*edge(0), *edge(rows // 8 - 1)],
        out_specs=[whole] * 2,
        out_shape=[line] * 2,
        compiler_params=pltpu.CompilerParams(vmem_limit_bytes=8 << 20),
        name="edge_rows",
    )(*[pltpu.with_memory_space_constraint(x, pltpu.HBM) for x in (*fields, *fields)])
    xr = swap(xs, lambda o, a: (o, a ^ 1))
    yr = swap(ys, y_partner)

    level = [
        pl.BlockSpec((2, 1, rows, cols), lambda k: (0, k, 0, 0)),
        *[pl.BlockSpec((1, rows, cols), lambda k: (k, 0, 0))] * 4,
        *[pl.BlockSpec((rows, cols), lambda k: (0, 0))] * 2,
    ]
    side = jax.ShapeDtypeStruct((n, rows), f32)
    own_w, own_e = pl.pallas_call(
        cols_kernel,
        grid=(K,),
        in_specs=level,
        out_specs=[pl.BlockSpec((n, rows), lambda k: (0, 0))] * 2,
        out_shape=[side] * 2,
        scratch_shapes=[pltpu.VMEM((rows, 128), f32)] * 2 + [pltpu.VMEM((128, rows), f32)],
        cost_estimate=pl.CostEstimate(flops=4_000_000, bytes_accessed=7_000_000, transcendentals=0),
        compiler_params=pltpu.CompilerParams(vmem_limit_bytes=8 << 20),
        name="edge_cols",
    )(*fields)
    message = jax.ShapeDtypeStruct((n + K + 2 * n, 128), f32)
    ps, qs = pl.pallas_call(
        corners_kernel,
        out_shape=[message, message],
        compiler_params=pltpu.CompilerParams(vmem_limit_bytes=8 << 20),
        name="corners",
    )(xr, yr, own_w, own_e)
    qr = swap(qs, lambda o, a: (o + 1, a) if o % 2 else (o - 1, a))
    pr = swap(ps, lambda o, a: (o ^ 1, a))

    vmem = pl.BlockSpec(memory_space=pltpu.VMEM)
    whole_field = (K, rows, cols)
    m, sec = pl.pallas_call(
        inner_kernel,
        in_specs=[vmem] * 7,
        out_specs=[vmem] * 2,
        out_shape=[
            jax.ShapeDtypeStruct((6, *whole_field), f32),
            jax.ShapeDtypeStruct((2, *whole_field), f32),
        ],
        scratch_shapes=[pltpu.VMEM((5, rows, cols), f32)],
        cost_estimate=pl.CostEstimate(flops=20_000_000, bytes_accessed=14_000_000, transcendentals=0),
        compiler_params=pltpu.CompilerParams(vmem_limit_bytes=18 << 20),
        name="inner",
    )(*fields)
    return pl.pallas_call(
        final_kernel,
        in_specs=[pl.BlockSpec(memory_space=pltpu.SMEM)] + [vmem] * 12,
        out_specs=pl.BlockSpec(memory_space=pl.ANY),
        out_shape=jax.ShapeDtypeStruct(tracers.shape, f32),
        scratch_shapes=[
            pltpu.VMEM((8 * K, cols), f32),
            pltpu.VMEM((rows, 128), f32),
            pltpu.VMEM((128, rows), f32),
            pltpu.VMEM((n + K, cols + 128), f32),
            pltpu.VMEM((2, rows, cols), f32),
            pltpu.VMEM((2, *whole_field), f32),
            pltpu.SemaphoreType.DMA((K,)),
        ],
        cost_estimate=pl.CostEstimate(flops=20_000_000, bytes_accessed=14_000_000, transcendentals=0),
        compiler_params=pltpu.CompilerParams(vmem_limit_bytes=18 << 20),
        name="final",
    )(fold_partner, tracers, land_sea, m, sec, xs, ys, xr, yr, own_w, own_e, pr, qr)


def solution(mesh):
    return jax.shard_map(
        functools.partial(shards, mesh.shape["lon"], mesh.shape["lat"]),
        mesh=mesh,
        in_specs=(
            P(None, None, "lat", "lon"),
            P(None, "lat", "lon"),
            P(None, "lat", "lon"),
            P(None, "lat", "lon"),
            P(None, "lat", "lon"),
            P("lat", "lon"),
            P("lat", "lon"),
            P("lon"),
        ),
        out_specs=P(None, None, "lat", "lon"),
        check_vma=False,
    )
```

```python
import functools
import jax
import jax.numpy as jnp
from jax import lax
from jax.experimental import pallas as pl
from jax.experimental.pallas import tpu as pltpu
from jax.sharding import PartitionSpec as P


STEP = 0.2
K = 8
SLABS = 9
C0, C1, WET, U, V, TH, D, F0, F1 = range(SLABS)
SELF, BESIDE = SLABS, SLABS + 1
f32 = jnp.float32


def coefs(vel, wa, wb, la, lb, da, db):
    g = (0.5 * (la + lb)) * jnp.minimum(wa, wb)
    e = 0.5 / (da + db)
    h = 0.5 * vel
    return g * (h + e), g * (h - e)


def slab(x, s):
    return x[s * K : (s + 1) * K]


def join(*parts):
    return jnp.concatenate(parts, axis=0)


def row_message(t_ref, u_ref, v_ref, th_ref, sea_ref, dx_ref, dy_ref, near, far, face):
    def wet(r):
        return th_ref[:, r, :] * sea_ref[:, r, :].astype(f32)

    w1, w2 = wet(near), wet(far)
    dx1, dx2 = dx_ref[near : near + 1, :], dx_ref[far : far + 1, :]
    dy1, dy2 = dy_ref[near : near + 1, :], dy_ref[far : far + 1, :]
    p, q = coefs(v_ref[:, face, :], w1, w2, dx1, dx2, dy1, dy2)
    if near > far:
        p, q = coefs(v_ref[:, face, :], w2, w1, dx2, dx1, dy2, dy1)
        p, q = q, p
    near_c = [t_ref[n, :, near, :] for n in range(2)]
    inner = [p * near_c[n] + q * t_ref[n, :, far, :] for n in range(2)]
    pad = jnp.zeros((6, dx1.shape[1]), f32)
    return join(
        *near_c,
        w1,
        u_ref[:, near, :],
        v_ref[:, near, :],
        th_ref[:, near, :],
        join(dx1, dy1, pad),
        *inner,
    )


def rows_kernel(*refs):
    low, high, (x_ref, y_ref) = refs[:7], refs[7:14], refs[14:]
    bottom = row_message(*low, 0, 1, 0)
    top = row_message(*high, 7, 6, 6)
    even = lax.axis_index("lat") % 2 == 0

    @pl.when(even)
    def _():
        x_ref[...] = top
        y_ref[...] = bottom

    @pl.when(jnp.logical_not(even))
    def _():
        x_ref[...] = bottom
        y_ref[...] = top


CORNER = (C0, C1, WET, U, V, D)


def move(x, at, to):
    tile = x[:, at // 128 * 128 : at // 128 * 128 + 128]
    shift = (to - at) % 128
    return pltpu.roll(tile, shift, 1) if shift else tile


def corners_kernel(xr_ref, yr_ref, w_ref, e_ref, p_ref, q_ref):
    even_lat = lax.axis_index("lat") % 2 == 0
    even_lon = lax.axis_index("lon") % 2 == 0
    north = jnp.where(even_lat, xr_ref[...], yr_ref[...])
    south = jnp.where(even_lat, yr_ref[...], xr_ref[...])
    lane = lax.broadcasted_iota(jnp.int32, (K, 128), 1)

    def corner(col):
        out = jnp.zeros((K, 128), f32)
        for base, rows in ((0, south), (8, north)):
            for at, s in enumerate(CORNER):
                out = jnp.where(lane == base + at, move(slab(rows, s), col, base + at), out)
        return out

    n = SLABS * K
    west, east = corner(0), corner(xr_ref.shape[1] - 1)
    for ref in (p_ref, q_ref):
        ref[n + K : 2 * n + K, :] = yr_ref[:, :128]
        ref[2 * n + K :, :] = yr_ref[:, 128:]

    @pl.when(even_lon)
    def _():
        p_ref[:n, :] = e_ref[:n, :]
        p_ref[n : n + K, :] = east
        q_ref[:n, :] = w_ref[:n, :]
        q_ref[n : n + K, :] = west

    @pl.when(jnp.logical_not(even_lon))
    def _():
        p_ref[:n, :] = w_ref[:n, :]
        p_ref[n : n + K, :] = west
        q_ref[:n, :] = e_ref[:n, :]
        q_ref[n : n + K, :] = east


def line_tendency(line, along, across, velocity, prev, nxt):
    n = line.shape[1]
    lane = lax.broadcasted_iota(jnp.int32, (K, 128), 1)

    def before(x, edge):
        moved = pltpu.roll(x, 1, 1)
        first = jnp.where(lane == 0, edge, moved[:, :128])
        return first if n == 128 else jnp.concatenate([first, moved[:, 128:]], axis=1)

    def after(x, edge):
        moved = pltpu.roll(x, n - 1, 1)
        last = jnp.where(lane == 127, edge, moved[:, -128:])
        return last if n == 128 else jnp.concatenate([moved[:, :-128], last], axis=1)

    def wide(x, i):
        return jnp.broadcast_to(x[i : i + 1], x.shape)

    d, wet, vel = slab(line, D), slab(line, WET), slab(line, velocity)
    al, ac = wide(d, along), wide(d, across)
    al_n, ac_n = after(al, wide(nxt["d"], along)), after(ac, wide(nxt["d"], across))
    al_p, ac_p = before(al, wide(prev["d"], along)), before(ac, wide(prev["d"], across))
    pn, qn = coefs(vel, wet, after(wet, nxt["w"]), ac, ac_n, al, al_n)
    pp, qp = coefs(before(vel, prev["vel"]), before(wet, prev["w"]), wet, ac_p, ac, al_p, al)
    out = []
    for t in range(2):
        C = slab(line, t)
        ahead = pn * C + qn * after(C, nxt["c"][t])
        behind = pp * before(C, prev["c"][t]) + qp * C
        out.append(ahead - behind)
    return out, (pn, qn, pp, qp)


def face_fluxes(own, ghost, own_vel_is_low, vel, ghost_vel, along, across, own_line, ghost_line):
    d, g = slab(own, D), slab(ghost, D)

    def face(velocity):
        lo, hi = (own, ghost) if own_vel_is_low else (ghost, own)
        dl, dh = (d, g) if own_vel_is_low else (g, d)
        return coefs(
            velocity,
            slab(lo, WET),
            slab(hi, WET),
            dl[across : across + 1],
            dh[across : across + 1],
            dl[along : along + 1],
            dh[along : along + 1],
        )

    def through(pq, a, b):
        return pq[0] * a + pq[1] * b if own_vel_is_low else pq[0] * b + pq[1] * a

    pq = face(vel)
    pq_ghost = pq if ghost_vel is None else face(ghost_vel)
    vol_own = d[0:1] * d[1:2] * slab(own, TH)
    vol_ghost = g[0:1] * g[1:2] * slab(ghost, TH)
    one, two = [], []
    for t in range(2):
        a, b = slab(own, t), slab(ghost, t)
        f = through(pq, a, b)
        fg = f if ghost_vel is None else through(pq_ghost, a, b)
        if own_vel_is_low:
            own_div = own_line[t] + (f - slab(own, F0 + t))
            ghost_div = ghost_line[t] + (slab(ghost, F0 + t) - fg)
        else:
            own_div = own_line[t] + (slab(own, F0 + t) - f)
            ghost_div = ghost_line[t] + (fg - slab(ghost, F0 + t))
        a2 = a - STEP * own_div / vol_own
        b2 = b - STEP * ghost_div / vol_ghost
        one.append(f)
        two.append(through(pq, a2, b2))
    return one, two


def correction(own, face_coefs, first, second):
    pn, qn, pp, qp = face_coefs
    d = slab(own, D)
    r = (-0.5 * STEP) / (d[0:1] * d[1:2] * slab(own, TH))
    delta = (2.0 * r) * first
    n = delta.shape[1]
    out = r * (first + second) + (r * (slab(own, SELF) + pn - qp)) * delta
    out = out + (r * qn) * pltpu.roll(delta, n - 1, 1) - (r * pp) * pltpu.roll(delta, 1, 1)
    return jnp.where(slab(own, WET) > 0, out, 0.0), slab(own, BESIDE) * delta


def boundary(xs, ys, xr, yr, own_w, own_e, pr, qr, pivot, fy_ref, tt_ref, flip_ref, ghost_ref):
    lat, lon = lax.axis_index("lat"), lax.axis_index("lon")
    last = lax.axis_size("lat") - 1
    even_lat, even_lon = lat % 2 == 0, lon % 2 == 0
    n = SLABS * K
    top = jnp.where(even_lat, xs[...], ys[...])
    bottom = jnp.where(even_lat, ys[...], xs[...])
    south = jnp.where(even_lat, yr[...], xr[...])
    west_all = jnp.where(even_lon, qr[...], pr[...])
    east_all = jnp.where(even_lon, pr[...], qr[...])
    west, east = west_all[:n], east_all[:n]
    cw, ce = west_all[n : n + K], east_all[n : n + K]
    w_own, e_own = own_w[...], own_e[...]
    width = top.shape[1]
    height = w_own.shape[1]

    @pl.when(lat != last)
    def _():
        ghost_ref[:n, :width] = jnp.where(even_lat, xr[...], yr[...])
        ghost_ref[n:, :width] = slab(top, V)
        tile = jnp.zeros((K, 128), f32)
        lane = lax.broadcasted_iota(jnp.int32, (K, 128), 1)
        for at, s in enumerate(CORNER):
            ends = jnp.where(lane == 0, move(cw, 8 + at, 0), tile)
            ends = jnp.where(lane == 1, move(ce, 8 + at, 1), ends)
            ghost_ref[s * K : (s + 1) * K, width:] = ends

    @pl.when(lat == last)
    def _():
        p = pivot[0] - (lax.axis_size("lon") * width - 1) + lon * width
        p = jnp.where(p <= 0, p + lax.axis_size("lon") * width, p)
        both = jnp.concatenate([yr[...], west_all[n + K : 2 * n + K], west_all[2 * n + K :]], axis=1)
        src = lax.broadcasted_iota(jnp.int32, (2 * width, width + 128), 0)
        dst = lax.broadcasted_iota(jnp.int32, (2 * width, width + 128), 1)
        dst = jnp.where(dst == width, -1, jnp.where(dst == width + 1, width, dst))
        pick = (src == (width - 1) - dst + p).astype(f32)
        win = jnp.dot(both, pick, preferred_element_type=f32, precision=lax.Precision.HIGHEST)
        for s in (C0, C1, WET, TH, D):
            ghost_ref[s * K : (s + 1) * K, :] = slab(win, s)
        u = slab(win, U)
        lane = lax.broadcasted_iota(jnp.int32, (K, 128), 1)
        here = pltpu.roll(u[:, :width], width - 1, 1)
        last_tile = jnp.where(lane == 127, move(u, width + 1, 127), here[:, -128:])
        ghost_ref[U * K : (U + 1) * K, :width] = -jnp.concatenate([here[:, :-128], last_tile], axis=1)
        ghost_ref[U * K : (U + 1) * K, width:] = -u[:, :128]
        for s in (F0, F1):
            ghost_ref[s * K : (s + 1) * K, :] = -slab(win, s)
        ghost_ref[n:, :width] = -slab(win, V)[:, :width]

    north = ghost_ref[:n, :width]
    north_vel = ghost_ref[n:, :width]

    def cell(get, vel, to):
        return dict(c=[get(C0, to), get(C1, to)], w=get(WET, to), d=get(D, to), vel=vel and get(vel, to))

    def end(x, at, vel, to):
        return cell(lambda s, to: move(slab(x, s), at, to), vel, to)

    def corner(x, base, vel, to):
        return cell(lambda s, to: move(x, base + CORNER.index(s), to), vel, to)

    def ghost_end(at, vel, to):
        return cell(lambda s, to: move(ghost_ref[s * K : (s + 1) * K, width:], at, to), vel, to)

    def x_line(line, prev, nxt):
        return line_tendency(line, 0, 1, U, prev, nxt)[0]

    def y_line(line, prev, nxt):
        return line_tendency(line, 1, 0, V, prev, nxt)

    line_n = x_line(north, ghost_end(0, U, 0), ghost_end(1, None, 127))
    line_s = x_line(south, corner(cw, 0, U, 0), corner(ce, 0, None, 127))
    line_top = x_line(top, end(west, height - 1, U, 0), end(east, height - 1, None, 127))
    line_bottom = x_line(bottom, end(west, 0, U, 0), end(east, 0, None, 127))
    n1, n2 = face_fluxes(top, north, True, slab(top, V), north_vel, 1, 0, line_top, line_n)
    s1, s2 = face_fluxes(bottom, south, False, slab(south, V), None, 1, 0, line_bottom, line_s)
    closed = lat == 0
    for i, value in enumerate((*s1, *s2)):
        fy_ref[i * K : (i + 1) * K, :] = jnp.where(closed, 0.0, value)
    for i, value in enumerate((*n1, *n2)):
        fy_ref[(4 + i) * K : (5 + i) * K, :] = value

    line_w, _ = y_line(west, corner(cw, 0, V, 0), ghost_end(0, None, 127))
    line_e, _ = y_line(east, corner(ce, 0, V, 0), ghost_end(1, None, 127))
    own_line_w, coef_w = y_line(w_own, end(south, 0, V, 0), end(north, 0, None, 127))
    own_line_e, coef_e = y_line(e_own, end(south, width - 1, V, 0), end(north, width - 1, None, 127))
    e1, e2 = face_fluxes(e_own, east, True, slab(e_own, U), None, 0, 1, own_line_e, line_e)
    w1, w2 = face_fluxes(w_own, west, False, slab(west, U), None, 0, 1, own_line_w, line_w)
    for n in range(2):
        west_out, west_in = correction(w_own, coef_w, -w1[n], -w2[n])
        east_out, east_in = correction(e_own, coef_e, e1[n], e2[n])
        for at, value in enumerate((east_in, east_out, west_out, west_in)):
            flip_ref[pl.ds(4 * K * n + at, K, stride=4), :] = value
    for j, (ea, we) in enumerate(zip((*e1, *e2), (*w1, *w2))):
        flip_ref[pl.ds(64 + 2 * K * j, K, stride=2), :] = ea
        flip_ref[pl.ds(65 + 2 * K * j, K, stride=2), :] = we
    tt_ref[...] = flip_ref[...].T


TILES = (slice(0, 128), slice(128, 256))


def chunk(c):
    return slice(8 * c, 8 * c + 8)


def both(ref, c, *lead):
    return [ref[(*lead, chunk(c), t)] for t in TILES]


def lanes():
    return lax.broadcasted_iota(jnp.int32, (8, 128), 1)


def subs():
    return lax.broadcasted_iota(jnp.int32, (8, 128), 0)


def east_of(x):
    moved = [pltpu.roll(v, 127, 1) for v in x]
    return [jnp.where(lanes() == 127, moved[1], moved[0]), moved[1]]


def west_of(x):
    moved = [pltpu.roll(v, 1, 1) for v in x]
    return [moved[0], jnp.where(lanes() == 0, moved[0], moved[1])]


def up_rolled(x):
    return [pltpu.roll(v, 7, 0) for v in x]


def down_rolled(x):
    return [pltpu.roll(v, 1, 0) for v in x]


def pick(mask, x, y):
    return [jnp.where(mask, a, b) for a, b in zip(x, y)]


def tendency(x, x_n, x_s, m):
    x_e, x_w = east_of(x), west_of(x)
    return [
        (m[0][i] * x[i] + m[1][i] * x_e[i]) + (m[2][i] * x_w[i] + m[3][i] * x_n[i]) + m[4][i] * x_s[i]
        for i in range(2)
    ]


def apply(load, m_ref, k, chunks, write):
    x = load(0)
    up = up_rolled(x)
    below = x
    for c in range(chunks):
        x_next = load(c + 1) if c + 1 < chunks else x
        up_next, down = up_rolled(x_next), down_rolled(x)
        x_n, x_s = pick(subs() == 7, up_next, up), pick(subs() == 0, below, down)
        tend = tendency(x, x_n, x_s, [both(m_ref, c, j, k) for j in range(5)])
        for i, t in enumerate(TILES):
            write(c, i, t, x[i], tend[i])
        x, up, below = x_next, up_next, down


def prep_kernel(
    t_ref, u_ref, v_ref, th_ref, sea_ref, dx_ref, dy_ref, w_ref, e_ref, m_ref, geo, acc0, acc1, flip0, flip1
):
    rows = dx_ref.shape[0]
    chunks = rows // 8

    def columns(c, carry):
        at = pl.ds(pl.multiple_of(8 * c, 8), 8)
        lane = lanes()

        def put(acc, slot, left, right):
            moved = pltpu.roll(jnp.where(lane < 64, left, right), (4 * slot + 2) % 128, 1)
            return moved if acc is None else jnp.where(lane >> 2 == slot, moved, acc)

        def ends(ref, *lead):
            return ref[(*lead, at, TILES[0])], ref[(*lead, at, TILES[-1])]

        one = two = None
        for k in range(K):
            th = ends(th_ref, k)
            wet = [a * b.astype(f32) for a, b in zip(th, ends(sea_ref, k))]
            for q, value in enumerate((ends(t_ref, 0, k), ends(t_ref, 1, k), wet, ends(u_ref, k))):
                one = put(one, q * K + k, *value)
            for q, value in enumerate((ends(v_ref, k), th)):
                two = put(two, q * K + k, *value)
        two = put(two, 2 * K, *ends(dx_ref))
        two = put(two, 2 * K + 1, *ends(dy_ref))
        acc0[at, :] = one
        acc1[at, :] = two
        return carry

    lax.fori_loop(0, chunks, columns, 0, unroll=8)
    flip0[...] = acc0[...].T
    flip1[...] = acc1[...].T
    places = {C0: (flip0, 0), C1: (flip0, 1), WET: (flip0, 2), U: (flip0, 3), V: (flip1, 0), TH: (flip1, 1)}
    for out, near, far in ((w_ref, 2, 3), (e_ref, 1, 0)):

        def get(s, at):
            ref, q = places[s]
            return ref[pl.ds(4 * K * q + at, K, stride=4), :]

        d1 = flip1[pl.ds(8 * K + near, 2, stride=4), :]
        d2 = flip1[pl.ds(8 * K + far, 2, stride=4), :]
        low, high = min(near, far), max(near, far)
        da, db = (d1, d2) if near < far else (d2, d1)
        p, q = coefs(get(U, low), get(WET, low), get(WET, high), da[1:2], db[1:2], da[0:1], db[0:1])
        for s in (C0, C1, WET, U, V, TH):
            out[s * K : (s + 1) * K, :] = get(s, near)
        out[D * K : (D + 1) * K, :] = join(d1, jnp.zeros((6, rows), f32))
        for n in range(2):
            out[(F0 + n) * K : (F0 + n + 1) * K, :] = p * get(n, low) + q * get(n, high)
        mine = p if near < far else -q
        r = (-0.5 * STEP) / (d2[0:1] * d2[1:2] * get(TH, far))
        out[SELF * K : (SELF + 1) * K, :] = mine
        out[BESIDE * K : (BESIDE + 1) * K, :] = jnp.where(get(WET, far) > 0, -r * mine, 0.0)

    for c in range(chunks):
        n = min(c + 1, chunks - 1)
        dx, dy = both(dx_ref, c), both(dy_ref, c)
        dx_e, dy_e = east_of(dx), east_of(dy)
        dx_n, dy_n = (pick(subs() == 7, up_rolled(both(r, n)), up_rolled(x)) for r, x in ((dx_ref, dx), (dy_ref, dy)))
        for i, t in enumerate(TILES):
            geo[0, chunk(c), t] = 0.5 * (dy[i] + dy_e[i])
            geo[1, chunk(c), t] = 0.5 / (dx[i] + dx_e[i])
            geo[2, chunk(c), t] = 0.5 * (dx[i] + dx_n[i])
            geo[3, chunk(c), t] = 0.5 / (dy[i] + dy_n[i])
            geo[4, chunk(c), t] = (-0.5 * STEP) / (dx[i] * dy[i])

    def level(k, carry):
        def wet(c):
            return [a * b.astype(f32) for a, b in zip(both(th_ref, c, k), both(sea_ref, c, k))]

        w = wet(0)
        up = up_rolled(w)
        zero = jnp.zeros((8, 128), f32)
        p_below, q_below = [zero, zero], [zero, zero]
        for c in range(chunks):
            w_next = wet(c + 1) if c + 1 < chunks else w
            up_next = up_rolled(w_next)
            w_e, w_n = east_of(w), pick(subs() == 7, up_next, up)
            u, v, th = both(u_ref, c, k), both(v_ref, c, k), both(th_ref, c, k)
            gx, ex, gy, ey, dd = [both(geo, c, j) for j in range(5)]
            a, b, p, q = [], [], [], []
            for i in range(2):
                g, h = gx[i] * jnp.minimum(w[i], w_e[i]), 0.5 * u[i]
                if i == 1:
                    g = jnp.where(lanes() == 127, 0.0, g)
                a.append(g * (h + ex[i]))
                b.append(g * (h - ex[i]))
                g, h = gy[i] * jnp.minimum(w[i], w_n[i]), 0.5 * v[i]
                if c == chunks - 1:
                    g = jnp.where(subs() == 7, 0.0, g)
                p.append(g * (h + ey[i]))
                q.append(g * (h - ey[i]))
            a_w, b_w = west_of(a), west_of(b)
            a_w[0], b_w[0] = (jnp.where(lanes() == 0, 0.0, y[0]) for y in (a_w, b_w))
            p_down, q_down = down_rolled(p), down_rolled(q)
            p_s, q_s = pick(subs() == 0, p_below, p_down), pick(subs() == 0, q_below, q_down)
            for i, t in enumerate(TILES):
                r = dd[i] / th[i]
                m_ref[0, k, chunk(c), t] = r * ((a[i] - b_w[i]) + (p[i] - q_s[i]))
                m_ref[1, k, chunk(c), t] = r * b[i]
                m_ref[2, k, chunk(c), t] = -r * a_w[i]
                m_ref[3, k, chunk(c), t] = r * q[i]
                m_ref[4, k, chunk(c), t] = -r * p_s[i]
                m_ref[5, k, chunk(c), t] = r
            w, up, p_below, q_below = w_next, up_next, p_down, q_down
        return carry

    lax.fori_loop(0, K, level, 0)


def stages_kernel(t_ref, sea_ref, m_ref, sec_ref, res_ref):
    chunks = sea_ref.shape[1] // 8

    def level(k, carry):
        for n in range(2):

            def write(c, i, t, x, tend):
                sec_ref[n, k, chunk(c), t] = x + 2.0 * tend

            apply(lambda c: both(t_ref, c, n, k), m_ref, k, chunks, write)
        for n in range(2):

            def write(c, i, t, x, tend):
                total = 0.5 * (t_ref[n, k, chunk(c), t] + x) + tend
                res_ref[n, k, chunk(c), t] = jnp.where(sea_ref[k, chunk(c), t] > 0, total, 0.0)

            apply(lambda c: both(sec_ref, c, n, k), m_ref, k, chunks, write)
        return carry

    lax.fori_loop(0, K, level, 0)


def final_kernel(
    pivot, t_ref, sea_ref, m_ref, sec_ref, res_ref, xs, ys, xr, yr, own_w, own_e, pr, qr,
    out_ref, fy_ref, tt_ref, flip_ref, ghost_ref, done, sems,
):
    rows = sea_ref.shape[1]
    chunks = rows // 8
    boundary(xs, ys, xr, yr, own_w, own_e, pr, qr, pivot, fy_ref, tt_ref, flip_ref, ghost_ref)
    lane, sub = lanes(), subs()

    def edges(n, s, k, c):
        def row(i):
            r = fy_ref[pl.ds((4 * i + 2 * s + n) * K + k, 1), :]
            return [jnp.broadcast_to(r[:, t], (8, 128)) for t in TILES]

        ends = pltpu.roll(tt_ref[chunk(c), :], 63 - 2 * ((2 * s + n) * K + k), 1)
        out = [jnp.where(lane == 0, -ends, 0.0), jnp.where(lane == 127, ends, 0.0)]
        if c == 0:
            out = [o - jnp.where(sub == 0, f, 0.0) for o, f in zip(out, row(0))]
        if c == chunks - 1:
            out = [o + jnp.where(sub == 7, f, 0.0) for o, f in zip(out, row(1))]
        return out

    def copy(k):
        return pltpu.make_async_copy(done.at[:, pl.ds(k, 1)], out_ref.at[:, pl.ds(k, 1)], sems.at[k])

    def level(k, carry):
        for n in range(2):

            def section(c):
                r, x, add = both(m_ref, c, 5, k), both(sec_ref, c, n, k), edges(n, 0, k, c)
                return [x[i] + 2.0 * (r[i] * add[i]) for i in range(2)]

            for c, beside in ((0, 1), (chunks - 1, chunks - 2)):
                x, y = section(c), section(beside)
                x_n, x_s = up_rolled(x), down_rolled(x)
                if c == 0:
                    x_n = pick(sub == 7, up_rolled(y), x_n)
                else:
                    x_s = pick(sub == 0, down_rolled(y), x_s)
                tend = tendency(x, x_n, x_s, [both(m_ref, c, j, k) for j in range(5)])
                add, r = edges(n, 1, k, c), both(m_ref, c, 5, k)
                for i, t in enumerate(TILES):
                    total = 0.5 * (t_ref[n, k, chunk(c), t] + x[i]) + (tend[i] + r[i] * add[i])
                    done[n, k, chunk(c), t] = jnp.where(sea_ref[k, chunk(c), t] > 0, total, 0.0)
            for c in range(1, chunks - 1):
                ends = pltpu.roll(tt_ref[chunk(c), :], 126 - 4 * (n * K + k), 1)
                left, right = TILES
                done[n, k, chunk(c), left] = res_ref[n, k, chunk(c), left] + jnp.where(lane < 2, ends, 0.0)
                done[n, k, chunk(c), right] = res_ref[n, k, chunk(c), right] + jnp.where(lane > 125, ends, 0.0)
        copy(k).start()
        return carry

    lax.fori_loop(0, K, level, 0)
    for k in range(K):
        copy(k).wait()


def pairs(count_lon, count_lat, partner):
    out = []
    for o in range(count_lon):
        for a in range(count_lat):
            to = partner(o, a)
            if to is not None:
                source, target = o * count_lat + a, (to[0] % count_lon) * count_lat + to[1]
                if source != target:
                    out.append((source, target))
    return out


def shards(nlon, nlat, tracers, zonal_vel, merid_vel, thickness, land_sea, cell_dx, cell_dy, fold_partner):
    rows, cols = cell_dx.shape
    axes = ("lon", "lat")
    end = nlat - 1

    def swap(x, partner):
        return lax.ppermute(x, axes, pairs(nlon, nlat, partner))

    def y_partner(o, a):
        if a == 0:
            return None
        if a == end:
            return (nlon - 1 - o, a)
        return (o, a + 1) if a % 2 else (o, a - 1)

    fields = (tracers, zonal_vel, merid_vel, thickness, land_sea, cell_dx, cell_dy)
    n = SLABS * K

    def edge(r):
        return [
            pl.BlockSpec((2, K, 8, cols), lambda i: (0, 0, r, 0)),
            *[pl.BlockSpec((K, 8, cols), lambda i: (0, r, 0))] * 4,
            *[pl.BlockSpec((8, cols), lambda i: (r, 0))] * 2,
        ]

    whole = pl.BlockSpec((n, cols), lambda i: (0, 0))
    line = jax.ShapeDtypeStruct((n, cols), f32)
    xs, ys = pl.pallas_call(
        rows_kernel,
        grid=(1,),
        in_specs=[*edge(0), *edge(rows // 8 - 1)],
        out_specs=[whole] * 2,
        out_shape=[line] * 2,
        compiler_params=pltpu.CompilerParams(vmem_limit_bytes=8 << 20),
        name="edge_rows",
    )(*[pltpu.with_memory_space_constraint(x, pltpu.HBM) for x in (*fields, *fields)])
    xr = swap(xs, lambda o, a: (o, a ^ 1))
    yr = swap(ys, y_partner)

    vmem = pl.BlockSpec(memory_space=pltpu.VMEM)
    whole_field = (K, rows, cols)
    side = jax.ShapeDtypeStruct((n + 2 * K, rows), f32)
    own_w, own_e, m = pl.pallas_call(
        prep_kernel,
        in_specs=[vmem] * 7,
        out_specs=[vmem] * 3,
        out_shape=[side, side, jax.ShapeDtypeStruct((6, *whole_field), f32)],
        scratch_shapes=[pltpu.VMEM((5, rows, cols), f32)] + [pltpu.VMEM((rows, 128), f32)] * 2 + [pltpu.VMEM((128, rows), f32)] * 2,
        cost_estimate=pl.CostEstimate(flops=10_000_000, bytes_accessed=10_000_000, transcendentals=0),
        compiler_params=pltpu.CompilerParams(vmem_limit_bytes=18 << 20),
        name="prep",
    )(*fields)
    message = jax.ShapeDtypeStruct((n + K + 2 * n, 128), f32)
    ps, qs = pl.pallas_call(
        corners_kernel,
        out_shape=[message, message],
        compiler_params=pltpu.CompilerParams(vmem_limit_bytes=8 << 20),
        name="corners",
    )(xr, yr, own_w, own_e)
    qr = swap(qs, lambda o, a: (o + 1, a) if o % 2 else (o - 1, a))
    pr = swap(ps, lambda o, a: (o ^ 1, a))

    field = jax.ShapeDtypeStruct((2, *whole_field), f32)
    sec, res = pl.pallas_call(
        stages_kernel,
        in_specs=[vmem] * 3,
        out_specs=[vmem] * 2,
        out_shape=[field, field],
        cost_estimate=pl.CostEstimate(flops=20_000_000, bytes_accessed=14_000_000, transcendentals=0),
        compiler_params=pltpu.CompilerParams(vmem_limit_bytes=18 << 20),
        name="stages",
    )(tracers, land_sea, m)
    return pl.pallas_call(
        final_kernel,
        in_specs=[pl.BlockSpec(memory_space=pltpu.SMEM)] + [vmem] * 13,
        out_specs=pl.BlockSpec(memory_space=pl.ANY),
        out_shape=jax.ShapeDtypeStruct(tracers.shape, f32),
        scratch_shapes=[
            pltpu.VMEM((8 * K, cols), f32),
            pltpu.VMEM((rows, 128), f32),
            pltpu.VMEM((128, rows), f32),
            pltpu.VMEM((n + K, cols + 128), f32),
            pltpu.VMEM((2, *whole_field), f32),
            pltpu.SemaphoreType.DMA((K,)),
        ],
        cost_estimate=pl.CostEstimate(flops=20_000_000, bytes_accessed=14_000_000, transcendentals=0),
        compiler_params=pltpu.CompilerParams(vmem_limit_bytes=18 << 20),
        name="final",
    )(fold_partner, tracers, land_sea, m, sec, res, xs, ys, xr, yr, own_w, own_e, pr, qr)


def solution(mesh):
    return jax.shard_map(
        functools.partial(shards, mesh.shape["lon"], mesh.shape["lat"]),
        mesh=mesh,
        in_specs=(
            P(None, None, "lat", "lon"),
            P(None, "lat", "lon"),
            P(None, "lat", "lon"),
            P(None, "lat", "lon"),
            P(None, "lat", "lon"),
            P("lat", "lon"),
            P("lat", "lon"),
            P("lon"),
        ),
        out_specs=P(None, None, "lat", "lon"),
        check_vma=False,
    )
```

```python
import functools
import jax
import jax.numpy as jnp
from jax import lax
from jax.experimental import pallas as pl
from jax.experimental.pallas import tpu as pltpu
from jax.sharding import PartitionSpec as P


STEP = 0.2
K = 8
SLABS = 9
C0, C1, WET, U, V, TH, D, F0, F1 = range(SLABS)
SELF, BESIDE = SLABS, SLABS + 1
f32 = jnp.float32


def coefs(vel, wa, wb, la, lb, da, db):
    g = (0.5 * (la + lb)) * jnp.minimum(wa, wb)
    e = 0.5 / (da + db)
    h = 0.5 * vel
    return g * (h + e), g * (h - e)


def slab(x, s):
    return x[s * K : (s + 1) * K]


def join(*parts):
    return jnp.concatenate(parts, axis=0)


def row_message(t_ref, u_ref, v_ref, th_ref, sea_ref, dx_ref, dy_ref, near, far, face):
    def wet(r):
        return th_ref[:, r, :] * sea_ref[:, r, :].astype(f32)

    w1, w2 = wet(near), wet(far)
    dx1, dx2 = dx_ref[near : near + 1, :], dx_ref[far : far + 1, :]
    dy1, dy2 = dy_ref[near : near + 1, :], dy_ref[far : far + 1, :]
    p, q = coefs(v_ref[:, face, :], w1, w2, dx1, dx2, dy1, dy2)
    if near > far:
        p, q = coefs(v_ref[:, face, :], w2, w1, dx2, dx1, dy2, dy1)
        p, q = q, p
    near_c = [t_ref[n, :, near, :] for n in range(2)]
    inner = [p * near_c[n] + q * t_ref[n, :, far, :] for n in range(2)]
    pad = jnp.zeros((6, dx1.shape[1]), f32)
    return join(
        *near_c,
        w1,
        u_ref[:, near, :],
        v_ref[:, near, :],
        th_ref[:, near, :],
        join(dx1, dy1, pad),
        *inner,
    )


def rows_kernel(*refs):
    low, high, (x_ref, y_ref) = refs[:7], refs[7:14], refs[14:]
    bottom = row_message(*low, 0, 1, 0)
    top = row_message(*high, 7, 6, 6)
    even = lax.axis_index("lat") % 2 == 0

    @pl.when(even)
    def _():
        x_ref[...] = top
        y_ref[...] = bottom

    @pl.when(jnp.logical_not(even))
    def _():
        x_ref[...] = bottom
        y_ref[...] = top


CORNER = (C0, C1, WET, U, V, D)


def move(x, at, to):
    tile = x[:, at // 128 * 128 : at // 128 * 128 + 128]
    shift = (to - at) % 128
    return pltpu.roll(tile, shift, 1) if shift else tile


def corners_kernel(xr_ref, yr_ref, w_ref, e_ref, p_ref, q_ref):
    even_lat = lax.axis_index("lat") % 2 == 0
    even_lon = lax.axis_index("lon") % 2 == 0
    north = jnp.where(even_lat, xr_ref[...], yr_ref[...])
    south = jnp.where(even_lat, yr_ref[...], xr_ref[...])
    lane = lax.broadcasted_iota(jnp.int32, (K, 128), 1)

    def corner(col):
        out = jnp.zeros((K, 128), f32)
        for base, rows in ((0, south), (8, north)):
            for at, s in enumerate(CORNER):
                out = jnp.where(lane == base + at, move(slab(rows, s), col, base + at), out)
        return out

    n = SLABS * K
    west, east = corner(0), corner(xr_ref.shape[1] - 1)
    for ref in (p_ref, q_ref):
        ref[n + K : 2 * n + K, :] = yr_ref[:, :128]
        ref[2 * n + K :, :] = yr_ref[:, 128:]

    @pl.when(even_lon)
    def _():
        p_ref[:n, :] = e_ref[:n, :]
        p_ref[n : n + K, :] = east
        q_ref[:n, :] = w_ref[:n, :]
        q_ref[n : n + K, :] = west

    @pl.when(jnp.logical_not(even_lon))
    def _():
        p_ref[:n, :] = w_ref[:n, :]
        p_ref[n : n + K, :] = west
        q_ref[:n, :] = e_ref[:n, :]
        q_ref[n : n + K, :] = east


def line_tendency(line, along, across, velocity, prev, nxt):
    n = line.shape[1]
    lane = lax.broadcasted_iota(jnp.int32, (K, 128), 1)

    def before(x, edge):
        moved = pltpu.roll(x, 1, 1)
        first = jnp.where(lane == 0, edge, moved[:, :128])
        return first if n == 128 else jnp.concatenate([first, moved[:, 128:]], axis=1)

    def after(x, edge):
        moved = pltpu.roll(x, n - 1, 1)
        last = jnp.where(lane == 127, edge, moved[:, -128:])
        return last if n == 128 else jnp.concatenate([moved[:, :-128], last], axis=1)

    def wide(x, i):
        return jnp.broadcast_to(x[i : i + 1], x.shape)

    d, wet, vel = slab(line, D), slab(line, WET), slab(line, velocity)
    al, ac = wide(d, along), wide(d, across)
    al_n, ac_n = after(al, wide(nxt["d"], along)), after(ac, wide(nxt["d"], across))
    al_p, ac_p = before(al, wide(prev["d"], along)), before(ac, wide(prev["d"], across))
    pn, qn = coefs(vel, wet, after(wet, nxt["w"]), ac, ac_n, al, al_n)
    pp, qp = coefs(before(vel, prev["vel"]), before(wet, prev["w"]), wet, ac_p, ac, al_p, al)
    out = []
    for t in range(2):
        C = slab(line, t)
        ahead = pn * C + qn * after(C, nxt["c"][t])
        behind = pp * before(C, prev["c"][t]) + qp * C
        out.append(ahead - behind)
    return out, (pn, qn, pp, qp)


def face_fluxes(own, ghost, own_vel_is_low, vel, ghost_vel, along, across, own_line, ghost_line):
    d, g = slab(own, D), slab(ghost, D)

    def face(velocity):
        lo, hi = (own, ghost) if own_vel_is_low else (ghost, own)
        dl, dh = (d, g) if own_vel_is_low else (g, d)
        return coefs(
            velocity,
            slab(lo, WET),
            slab(hi, WET),
            dl[across : across + 1],
            dh[across : across + 1],
            dl[along : along + 1],
            dh[along : along + 1],
        )

    def through(pq, a, b):
        return pq[0] * a + pq[1] * b if own_vel_is_low else pq[0] * b + pq[1] * a

    pq = face(vel)
    pq_ghost = pq if ghost_vel is None else face(ghost_vel)
    vol_own = d[0:1] * d[1:2] * slab(own, TH)
    vol_ghost = g[0:1] * g[1:2] * slab(ghost, TH)
    one, two = [], []
    for t in range(2):
        a, b = slab(own, t), slab(ghost, t)
        f = through(pq, a, b)
        fg = f if ghost_vel is None else through(pq_ghost, a, b)
        if own_vel_is_low:
            own_div = own_line[t] + (f - slab(own, F0 + t))
            ghost_div = ghost_line[t] + (slab(ghost, F0 + t) - fg)
        else:
            own_div = own_line[t] + (slab(own, F0 + t) - f)
            ghost_div = ghost_line[t] + (fg - slab(ghost, F0 + t))
        a2 = a - STEP * own_div / vol_own
        b2 = b - STEP * ghost_div / vol_ghost
        one.append(f)
        two.append(through(pq, a2, b2))
    return one, two


def correction(own, face_coefs, first, second):
    pn, qn, pp, qp = face_coefs
    d = slab(own, D)
    r = (-0.5 * STEP) / (d[0:1] * d[1:2] * slab(own, TH))
    delta = (2.0 * r) * first
    n = delta.shape[1]
    out = r * (first + second) + (r * (slab(own, SELF) + pn - qp)) * delta
    out = out + (r * qn) * pltpu.roll(delta, n - 1, 1) - (r * pp) * pltpu.roll(delta, 1, 1)
    return jnp.where(slab(own, WET) > 0, out, 0.0), slab(own, BESIDE) * delta


def boundary(xs, ys, xr, yr, own_w, own_e, pr, qr, partner, fy_ref, tt_ref, flip_ref, ghost_ref):
    lat, lon = lax.axis_index("lat"), lax.axis_index("lon")
    last = lax.axis_size("lat") - 1
    even_lat, even_lon = lat % 2 == 0, lon % 2 == 0
    n = SLABS * K
    top = jnp.where(even_lat, xs[...], ys[...])
    bottom = jnp.where(even_lat, ys[...], xs[...])
    south = jnp.where(even_lat, yr[...], xr[...])
    west_all = jnp.where(even_lon, qr[...], pr[...])
    east_all = jnp.where(even_lon, pr[...], qr[...])
    west, east = west_all[:n], east_all[:n]
    cw, ce = west_all[n : n + K], east_all[n : n + K]
    w_own, e_own = own_w[...], own_e[...]
    width = top.shape[1]
    height = w_own.shape[1]

    @pl.when(lat != last)
    def _():
        ghost_ref[:n, :width] = jnp.where(even_lat, xr[...], yr[...])
        ghost_ref[n:, :width] = slab(top, V)
        tile = jnp.zeros((K, 128), f32)
        lane = lax.broadcasted_iota(jnp.int32, (K, 128), 1)
        for at, s in enumerate(CORNER):
            ends = jnp.where(lane == 0, move(cw, 8 + at, 0), tile)
            ends = jnp.where(lane == 1, move(ce, 8 + at, 1), ends)
            ghost_ref[s * K : (s + 1) * K, width:] = ends

    @pl.when(lat == last)
    def _():
        total = lax.axis_size("lon") * width
        off = jnp.broadcast_to(partner[...], (K, width)) - (total - (lon + 1) * width)
        off = jnp.where(off < 0, off + total, off)
        first = lax.broadcasted_iota(jnp.int32, (K, 128), 1) == 0
        ends = jnp.where(first, off[:, :128] + 1, pltpu.roll(off[:, -128:], 2, 1) - 1)
        off = jnp.concatenate([off, ends], axis=1)[:1]
        both = jnp.concatenate([yr[...], west_all[n + K : 2 * n + K], west_all[2 * n + K :]], axis=1)
        src = lax.broadcasted_iota(jnp.int32, (2 * width, width + 128), 0)
        chosen = (src == off).astype(f32).astype(jnp.bfloat16)
        win = None
        for _ in range(3):
            part = both.astype(jnp.bfloat16)
            both = both - part.astype(f32)
            more = jnp.dot(part, chosen, preferred_element_type=f32)
            win = more if win is None else win + more
        for s in (C0, C1, WET, TH, D):
            ghost_ref[s * K : (s + 1) * K, :] = slab(win, s)
        u = slab(win, U)
        lane = lax.broadcasted_iota(jnp.int32, (K, 128), 1)
        here = pltpu.roll(u[:, :width], width - 1, 1)
        last_tile = jnp.where(lane == 127, move(u, width + 1, 127), here[:, -128:])
        ghost_ref[U * K : (U + 1) * K, :width] = -jnp.concatenate([here[:, :-128], last_tile], axis=1)
        ghost_ref[U * K : (U + 1) * K, width:] = -u[:, :128]
        for s in (F0, F1):
            ghost_ref[s * K : (s + 1) * K, :] = -slab(win, s)
        ghost_ref[n:, :width] = -slab(win, V)[:, :width]

    north = ghost_ref[:n, :width]
    north_vel = ghost_ref[n:, :width]

    def cell(get, vel, to):
        return dict(c=[get(C0, to), get(C1, to)], w=get(WET, to), d=get(D, to), vel=vel and get(vel, to))

    def end(x, at, vel, to):
        return cell(lambda s, to: move(slab(x, s), at, to), vel, to)

    def corner(x, base, vel, to):
        return cell(lambda s, to: move(x, base + CORNER.index(s), to), vel, to)

    def ghost_end(at, vel, to):
        return cell(lambda s, to: move(ghost_ref[s * K : (s + 1) * K, width:], at, to), vel, to)

    def x_line(line, prev, nxt):
        return line_tendency(line, 0, 1, U, prev, nxt)[0]

    def y_line(line, prev, nxt):
        return line_tendency(line, 1, 0, V, prev, nxt)

    line_n = x_line(north, ghost_end(0, U, 0), ghost_end(1, None, 127))
    line_s = x_line(south, corner(cw, 0, U, 0), corner(ce, 0, None, 127))
    line_top = x_line(top, end(west, height - 1, U, 0), end(east, height - 1, None, 127))
    line_bottom = x_line(bottom, end(west, 0, U, 0), end(east, 0, None, 127))
    n1, n2 = face_fluxes(top, north, True, slab(top, V), north_vel, 1, 0, line_top, line_n)
    s1, s2 = face_fluxes(bottom, south, False, slab(south, V), None, 1, 0, line_bottom, line_s)
    closed = lat == 0
    for i, value in enumerate((*s1, *s2)):
        fy_ref[i * K : (i + 1) * K, :] = jnp.where(closed, 0.0, value)
    for i, value in enumerate((*n1, *n2)):
        fy_ref[(4 + i) * K : (5 + i) * K, :] = value

    line_w, _ = y_line(west, corner(cw, 0, V, 0), ghost_end(0, None, 127))
    line_e, _ = y_line(east, corner(ce, 0, V, 0), ghost_end(1, None, 127))
    own_line_w, coef_w = y_line(w_own, end(south, 0, V, 0), end(north, 0, None, 127))
    own_line_e, coef_e = y_line(e_own, end(south, width - 1, V, 0), end(north, width - 1, None, 127))
    e1, e2 = face_fluxes(e_own, east, True, slab(e_own, U), None, 0, 1, own_line_e, line_e)
    w1, w2 = face_fluxes(w_own, west, False, slab(west, U), None, 0, 1, own_line_w, line_w)
    for n in range(2):
        west_out, west_in = correction(w_own, coef_w, -w1[n], -w2[n])
        east_out, east_in = correction(e_own, coef_e, e1[n], e2[n])
        for at, value in enumerate((east_in, east_out, west_out, west_in)):
            flip_ref[pl.ds(4 * K * n + at, K, stride=4), :] = value
    for j, (ea, we) in enumerate(zip((*e1, *e2), (*w1, *w2))):
        flip_ref[pl.ds(64 + 2 * K * j, K, stride=2), :] = ea
        flip_ref[pl.ds(65 + 2 * K * j, K, stride=2), :] = we
    tt_ref[...] = flip_ref[...].T


TILES = (slice(0, 128), slice(128, 256))


def chunk(c):
    return slice(8 * c, 8 * c + 8)


def both(ref, c, *lead):
    return [ref[(*lead, chunk(c), t)] for t in TILES]


def lanes():
    return lax.broadcasted_iota(jnp.int32, (8, 128), 1)


def subs():
    return lax.broadcasted_iota(jnp.int32, (8, 128), 0)


def east_of(x):
    moved = [pltpu.roll(v, 127, 1) for v in x]
    return [jnp.where(lanes() == 127, moved[1], moved[0]), moved[1]]


def west_of(x):
    moved = [pltpu.roll(v, 1, 1) for v in x]
    return [moved[0], jnp.where(lanes() == 0, moved[0], moved[1])]


def up_rolled(x):
    return [pltpu.roll(v, 7, 0) for v in x]


def down_rolled(x):
    return [pltpu.roll(v, 1, 0) for v in x]


def pick(mask, x, y):
    return [jnp.where(mask, a, b) for a, b in zip(x, y)]


def tendency(x, x_n, x_s, m):
    x_e, x_w = east_of(x), west_of(x)
    return [
        (m[0][i] * x[i] + m[1][i] * x_e[i]) + (m[2][i] * x_w[i] + m[3][i] * x_n[i]) + m[4][i] * x_s[i]
        for i in range(2)
    ]


def apply(load, m_ref, k, chunks, write):
    x = load(0)
    up = up_rolled(x)
    below = x
    for c in range(chunks):
        x_next = load(c + 1) if c + 1 < chunks else x
        up_next, down = up_rolled(x_next), down_rolled(x)
        x_n, x_s = pick(subs() == 7, up_next, up), pick(subs() == 0, below, down)
        tend = tendency(x, x_n, x_s, [both(m_ref, c, j, k) for j in range(5)])
        for i, t in enumerate(TILES):
            write(c, i, t, x[i], tend[i])
        x, up, below = x_next, up_next, down


def prep_kernel(
    t_ref, u_ref, v_ref, th_ref, sea_ref, dx_ref, dy_ref, w_ref, e_ref, m_ref, geo, acc0, acc1, flip0, flip1
):
    rows = dx_ref.shape[0]
    chunks = rows // 8

    def columns(c, carry):
        at = pl.ds(pl.multiple_of(8 * c, 8), 8)
        lane = lanes()

        def put(acc, slot, left, right):
            moved = pltpu.roll(jnp.where(lane < 64, left, right), (4 * slot + 2) % 128, 1)
            return moved if acc is None else jnp.where(lane >> 2 == slot, moved, acc)

        def ends(ref, *lead):
            return ref[(*lead, at, TILES[0])], ref[(*lead, at, TILES[-1])]

        one = two = None
        for k in range(K):
            th = ends(th_ref, k)
            wet = [a * b.astype(f32) for a, b in zip(th, ends(sea_ref, k))]
            for q, value in enumerate((ends(t_ref, 0, k), ends(t_ref, 1, k), wet, ends(u_ref, k))):
                one = put(one, q * K + k, *value)
            for q, value in enumerate((ends(v_ref, k), th)):
                two = put(two, q * K + k, *value)
        two = put(two, 2 * K, *ends(dx_ref))
        two = put(two, 2 * K + 1, *ends(dy_ref))
        acc0[at, :] = one
        acc1[at, :] = two
        return carry

    lax.fori_loop(0, chunks, columns, 0, unroll=8)
    flip0[...] = acc0[...].T
    flip1[...] = acc1[...].T
    places = {C0: (flip0, 0), C1: (flip0, 1), WET: (flip0, 2), U: (flip0, 3), V: (flip1, 0), TH: (flip1, 1)}
    for out, near, far in ((w_ref, 2, 3), (e_ref, 1, 0)):

        def get(s, at):
            ref, q = places[s]
            return ref[pl.ds(4 * K * q + at, K, stride=4), :]

        d1 = flip1[pl.ds(8 * K + near, 2, stride=4), :]
        d2 = flip1[pl.ds(8 * K + far, 2, stride=4), :]
        low, high = min(near, far), max(near, far)
        da, db = (d1, d2) if near < far else (d2, d1)
        p, q = coefs(get(U, low), get(WET, low), get(WET, high), da[1:2], db[1:2], da[0:1], db[0:1])
        for s in (C0, C1, WET, U, V, TH):
            out[s * K : (s + 1) * K, :] = get(s, near)
        out[D * K : (D + 1) * K, :] = join(d1, jnp.zeros((6, rows), f32))
        for n in range(2):
            out[(F0 + n) * K : (F0 + n + 1) * K, :] = p * get(n, low) + q * get(n, high)
        mine = p if near < far else -q
        r = (-0.5 * STEP) / (d2[0:1] * d2[1:2] * get(TH, far))
        out[SELF * K : (SELF + 1) * K, :] = mine
        out[BESIDE * K : (BESIDE + 1) * K, :] = jnp.where(get(WET, far) > 0, -r * mine, 0.0)

    for c in range(chunks):
        n = min(c + 1, chunks - 1)
        dx, dy = both(dx_ref, c), both(dy_ref, c)
        dx_e, dy_e = east_of(dx), east_of(dy)
        dx_n, dy_n = (pick(subs() == 7, up_rolled(both(r, n)), up_rolled(x)) for r, x in ((dx_ref, dx), (dy_ref, dy)))
        for i, t in enumerate(TILES):
            geo[0, chunk(c), t] = 0.5 * (dy[i] + dy_e[i])
            geo[1, chunk(c), t] = 0.5 / (dx[i] + dx_e[i])
            geo[2, chunk(c), t] = 0.5 * (dx[i] + dx_n[i])
            geo[3, chunk(c), t] = 0.5 / (dy[i] + dy_n[i])
            geo[4, chunk(c), t] = (-0.5 * STEP) / (dx[i] * dy[i])

    def level(k, carry):
        def wet(c):
            return [a * b.astype(f32) for a, b in zip(both(th_ref, c, k), both(sea_ref, c, k))]

        w = wet(0)
        up = up_rolled(w)
        zero = jnp.zeros((8, 128), f32)
        p_below, q_below = [zero, zero], [zero, zero]
        for c in range(chunks):
            w_next = wet(c + 1) if c + 1 < chunks else w
            up_next = up_rolled(w_next)
            w_e, w_n = east_of(w), pick(subs() == 7, up_next, up)
            u, v, th = both(u_ref, c, k), both(v_ref, c, k), both(th_ref, c, k)
            gx, ex, gy, ey, dd = [both(geo, c, j) for j in range(5)]
            a, b, p, q = [], [], [], []
            for i in range(2):
                g, h = gx[i] * jnp.minimum(w[i], w_e[i]), 0.5 * u[i]
                if i == 1:
                    g = jnp.where(lanes() == 127, 0.0, g)
                a.append(g * (h + ex[i]))
                b.append(g * (h - ex[i]))
                g, h = gy[i] * jnp.minimum(w[i], w_n[i]), 0.5 * v[i]
                if c == chunks - 1:
                    g = jnp.where(subs() == 7, 0.0, g)
                p.append(g * (h + ey[i]))
                q.append(g * (h - ey[i]))
            a_w, b_w = west_of(a), west_of(b)
            a_w[0], b_w[0] = (jnp.where(lanes() == 0, 0.0, y[0]) for y in (a_w, b_w))
            p_down, q_down = down_rolled(p), down_rolled(q)
            p_s, q_s = pick(subs() == 0, p_below, p_down), pick(subs() == 0, q_below, q_down)
            for i, t in enumerate(TILES):
                r = dd[i] / th[i]
                m_ref[0, k, chunk(c), t] = r * ((a[i] - b_w[i]) + (p[i] - q_s[i]))
                m_ref[1, k, chunk(c), t] = r * b[i]
                m_ref[2, k, chunk(c), t] = -r * a_w[i]
                m_ref[3, k, chunk(c), t] = r * q[i]
                m_ref[4, k, chunk(c), t] = -r * p_s[i]
                m_ref[5, k, chunk(c), t] = r
            w, up, p_below, q_below = w_next, up_next, p_down, q_down
        return carry

    lax.fori_loop(0, K, level, 0)


def stages_kernel(t_ref, sea_ref, m_ref, sec_ref, res_ref):
    chunks = sea_ref.shape[1] // 8

    def level(k, carry):
        for n in range(2):

            def write(c, i, t, x, tend):
                sec_ref[n, k, chunk(c), t] = x + 2.0 * tend

            apply(lambda c: both(t_ref, c, n, k), m_ref, k, chunks, write)
        for n in range(2):

            def write(c, i, t, x, tend):
                total = 0.5 * (t_ref[n, k, chunk(c), t] + x) + tend
                res_ref[n, k, chunk(c), t] = jnp.where(sea_ref[k, chunk(c), t] > 0, total, 0.0)

            apply(lambda c: both(sec_ref, c, n, k), m_ref, k, chunks, write)
        return carry

    lax.fori_loop(0, K, level, 0, unroll=2)


def final_kernel(
    partner, t_ref, sea_ref, m_ref, sec_ref, res_ref, xs, ys, xr, yr, own_w, own_e, pr, qr,
    out_ref, fy_ref, tt_ref, flip_ref, ghost_ref, done, sems,
):
    rows = sea_ref.shape[1]
    chunks = rows // 8
    boundary(xs, ys, xr, yr, own_w, own_e, pr, qr, partner, fy_ref, tt_ref, flip_ref, ghost_ref)
    lane, sub = lanes(), subs()

    def edges(n, s, k, c):
        def row(i):
            r = fy_ref[pl.ds((4 * i + 2 * s + n) * K + k, 1), :]
            return [jnp.broadcast_to(r[:, t], (8, 128)) for t in TILES]

        ends = pltpu.roll(tt_ref[chunk(c), :], 63 - 2 * ((2 * s + n) * K + k), 1)
        out = [jnp.where(lane == 0, -ends, 0.0), jnp.where(lane == 127, ends, 0.0)]
        if c == 0:
            out = [o - jnp.where(sub == 0, f, 0.0) for o, f in zip(out, row(0))]
        if c == chunks - 1:
            out = [o + jnp.where(sub == 7, f, 0.0) for o, f in zip(out, row(1))]
        return out

    def copy(k):
        return pltpu.make_async_copy(done.at[:, pl.ds(k, 1)], out_ref.at[:, pl.ds(k, 1)], sems.at[k])

    def level(k, carry):
        for n in range(2):

            def section(c):
                r, x, add = both(m_ref, c, 5, k), both(sec_ref, c, n, k), edges(n, 0, k, c)
                return [x[i] + 2.0 * (r[i] * add[i]) for i in range(2)]

            for c, beside in ((0, 1), (chunks - 1, chunks - 2)):
                x, y = section(c), section(beside)
                x_n, x_s = up_rolled(x), down_rolled(x)
                if c == 0:
                    x_n = pick(sub == 7, up_rolled(y), x_n)
                else:
                    x_s = pick(sub == 0, down_rolled(y), x_s)
                tend = tendency(x, x_n, x_s, [both(m_ref, c, j, k) for j in range(5)])
                add, r = edges(n, 1, k, c), both(m_ref, c, 5, k)
                for i, t in enumerate(TILES):
                    total = 0.5 * (t_ref[n, k, chunk(c), t] + x[i]) + (tend[i] + r[i] * add[i])
                    done[n, k, chunk(c), t] = jnp.where(sea_ref[k, chunk(c), t] > 0, total, 0.0)
            for c in range(1, chunks - 1):
                ends = pltpu.roll(tt_ref[chunk(c), :], 126 - 4 * (n * K + k), 1)
                left, right = TILES
                done[n, k, chunk(c), left] = res_ref[n, k, chunk(c), left] + jnp.where(lane < 2, ends, 0.0)
                done[n, k, chunk(c), right] = res_ref[n, k, chunk(c), right] + jnp.where(lane > 125, ends, 0.0)
        copy(k).start()
        return carry

    lax.fori_loop(0, K, level, 0, unroll=2)
    for k in range(K):
        copy(k).wait()


def pairs(count_lon, count_lat, partner):
    out = []
    for o in range(count_lon):
        for a in range(count_lat):
            to = partner(o, a)
            if to is not None:
                source, target = o * count_lat + a, (to[0] % count_lon) * count_lat + to[1]
                if source != target:
                    out.append((source, target))
    return out


def shards(nlon, nlat, tracers, zonal_vel, merid_vel, thickness, land_sea, cell_dx, cell_dy, fold_partner):
    rows, cols = cell_dx.shape
    axes = ("lon", "lat")
    end = nlat - 1

    def swap(x, partner):
        return lax.ppermute(x, axes, pairs(nlon, nlat, partner))

    def y_partner(o, a):
        if a == 0:
            return None
        if a == end:
            return (nlon - 1 - o, a)
        return (o, a + 1) if a % 2 else (o, a - 1)

    fields = (tracers, zonal_vel, merid_vel, thickness, land_sea, cell_dx, cell_dy)
    n = SLABS * K

    vmem = pl.BlockSpec(memory_space=pltpu.VMEM)

    def edge(r):
        return [
            pl.BlockSpec((2, K, 8, cols), lambda i: (0, 0, r, 0)),
            *[pl.BlockSpec((K, 8, cols), lambda i: (0, r, 0))] * 4,
            *[pl.BlockSpec((8, cols), lambda i: (r, 0))] * 2,
        ]

    whole = pl.BlockSpec((n, cols), lambda i: (0, 0))
    line = jax.ShapeDtypeStruct((n, cols), f32)
    xs, ys = pl.pallas_call(
        rows_kernel,
        grid=(1,),
        in_specs=[*edge(0), *edge(rows // 8 - 1)],
        out_specs=[whole] * 2,
        out_shape=[line] * 2,
        compiler_params=pltpu.CompilerParams(vmem_limit_bytes=8 << 20),
        name="edge_rows",
    )(*[pltpu.with_memory_space_constraint(x, pltpu.HBM) for x in (*fields, *fields)])
    xr = swap(xs, lambda o, a: (o, a ^ 1))
    yr = swap(ys, y_partner)

    whole_field = (K, rows, cols)
    side = jax.ShapeDtypeStruct((n + 2 * K, rows), f32)
    own_w, own_e, m = pl.pallas_call(
        prep_kernel,
        in_specs=[vmem] * 7,
        out_specs=[vmem] * 3,
        out_shape=[side, side, jax.ShapeDtypeStruct((6, *whole_field), f32)],
        scratch_shapes=[pltpu.VMEM((5, rows, cols), f32)] + [pltpu.VMEM((rows, 128), f32)] * 2 + [pltpu.VMEM((128, rows), f32)] * 2,
        cost_estimate=pl.CostEstimate(flops=10_000_000, bytes_accessed=10_000_000, transcendentals=0),
        compiler_params=pltpu.CompilerParams(vmem_limit_bytes=18 << 20),
        name="prep",
    )(*fields)
    message = jax.ShapeDtypeStruct((n + K + 2 * n, 128), f32)
    ps, qs = pl.pallas_call(
        corners_kernel,
        out_shape=[message, message],
        compiler_params=pltpu.CompilerParams(vmem_limit_bytes=8 << 20),
        name="corners",
    )(xr, yr, own_w, own_e)
    qr = swap(qs, lambda o, a: (o + 1, a) if o % 2 else (o - 1, a))
    pr = swap(ps, lambda o, a: (o ^ 1, a))

    field = jax.ShapeDtypeStruct((2, *whole_field), f32)
    sec, res = pl.pallas_call(
        stages_kernel,
        in_specs=[vmem] * 3,
        out_specs=[vmem] * 2,
        out_shape=[field, field],
        cost_estimate=pl.CostEstimate(flops=20_000_000, bytes_accessed=14_000_000, transcendentals=0),
        compiler_params=pltpu.CompilerParams(vmem_limit_bytes=18 << 20),
        name="stages",
    )(tracers, land_sea, m)
    return pl.pallas_call(
        final_kernel,
        in_specs=[vmem] * 14,
        out_specs=pl.BlockSpec(memory_space=pl.ANY),
        out_shape=jax.ShapeDtypeStruct(tracers.shape, f32),
        scratch_shapes=[
            pltpu.VMEM((8 * K, cols), f32),
            pltpu.VMEM((rows, 128), f32),
            pltpu.VMEM((128, rows), f32),
            pltpu.VMEM((n + K, cols + 128), f32),
            pltpu.VMEM((2, *whole_field), f32),
            pltpu.SemaphoreType.DMA((K,)),
        ],
        cost_estimate=pl.CostEstimate(flops=20_000_000, bytes_accessed=14_000_000, transcendentals=0),
        compiler_params=pltpu.CompilerParams(vmem_limit_bytes=18 << 20),
        name="final",
    )(fold_partner.reshape(1, cols), tracers, land_sea, m, sec, res, xs, ys, xr, yr, own_w, own_e, pr, qr)


def solution(mesh):
    return jax.shard_map(
        functools.partial(shards, mesh.shape["lon"], mesh.shape["lat"]),
        mesh=mesh,
        in_specs=(
            P(None, None, "lat", "lon"),
            P(None, "lat", "lon"),
            P(None, "lat", "lon"),
            P(None, "lat", "lon"),
            P(None, "lat", "lon"),
            P("lat", "lon"),
            P("lat", "lon"),
            P("lon"),
        ),
        out_specs=P(None, None, "lat", "lon"),
        check_vma=False,
    )
```

```python
import functools
import jax
import jax.numpy as jnp
from jax import lax
from jax.experimental import pallas as pl
from jax.experimental.pallas import tpu as pltpu
from jax.sharding import PartitionSpec as P


STEP = 0.2
K = 8
SLABS = 9
C0, C1, WET, U, V, TH, D, F0, F1 = range(SLABS)
SELF, BESIDE = SLABS, SLABS + 1
f32 = jnp.float32


def coefs(vel, wa, wb, la, lb, da, db):
    g = (0.5 * (la + lb)) * jnp.minimum(wa, wb)
    e = 0.5 / (da + db)
    h = 0.5 * vel
    return g * (h + e), g * (h - e)


def slab(x, s):
    return x[s * K : (s + 1) * K]


def join(*parts):
    return jnp.concatenate(parts, axis=0)


def row_message(t_ref, u_ref, v_ref, th_ref, sea_ref, dx_ref, dy_ref, near, far, face):
    def wet(r):
        return th_ref[:, r, :] * sea_ref[:, r, :].astype(f32)

    w1, w2 = wet(near), wet(far)
    dx1, dx2 = dx_ref[near : near + 1, :], dx_ref[far : far + 1, :]
    dy1, dy2 = dy_ref[near : near + 1, :], dy_ref[far : far + 1, :]
    p, q = coefs(v_ref[:, face, :], w1, w2, dx1, dx2, dy1, dy2)
    if near > far:
        p, q = coefs(v_ref[:, face, :], w2, w1, dx2, dx1, dy2, dy1)
        p, q = q, p
    near_c = [t_ref[n, :, near, :] for n in range(2)]
    inner = [p * near_c[n] + q * t_ref[n, :, far, :] for n in range(2)]
    pad = jnp.zeros((6, dx1.shape[1]), f32)
    return join(
        *near_c,
        w1,
        u_ref[:, near, :],
        v_ref[:, near, :],
        th_ref[:, near, :],
        join(dx1, dy1, pad),
        *inner,
    )


def rows_kernel(*refs):
    low, high, (x_ref, y_ref) = refs[:7], refs[7:14], refs[14:]
    bottom = row_message(*low, 0, 1, 0)
    top = row_message(*high, 7, 6, 6)
    even = lax.axis_index("lat") % 2 == 0

    @pl.when(even)
    def _():
        x_ref[...] = top
        y_ref[...] = bottom

    @pl.when(jnp.logical_not(even))
    def _():
        x_ref[...] = bottom
        y_ref[...] = top


CORNER = (C0, C1, WET, U, V, D)


def move(x, at, to):
    tile = x[:, at // 128 * 128 : at // 128 * 128 + 128]
    shift = (to - at) % 128
    return pltpu.roll(tile, shift, 1) if shift else tile


def corners_kernel(xr_ref, yr_ref, w_ref, e_ref, p_ref, q_ref):
    even_lat = lax.axis_index("lat") % 2 == 0
    even_lon = lax.axis_index("lon") % 2 == 0
    north = jnp.where(even_lat, xr_ref[...], yr_ref[...])
    south = jnp.where(even_lat, yr_ref[...], xr_ref[...])
    lane = lax.broadcasted_iota(jnp.int32, (K, 128), 1)

    def corner(col):
        out = jnp.zeros((K, 128), f32)
        for base, rows in ((0, south), (8, north)):
            for at, s in enumerate(CORNER):
                out = jnp.where(lane == base + at, move(slab(rows, s), col, base + at), out)
        return out

    n = SLABS * K
    west, east = corner(0), corner(xr_ref.shape[1] - 1)

    @pl.when(even_lon)
    def _():
        p_ref[:n, :] = e_ref[:n, :]
        p_ref[n : n + K, :] = east
        q_ref[:n, :] = w_ref[:n, :]
        q_ref[n : n + K, :] = west

    @pl.when(jnp.logical_not(even_lon))
    def _():
        p_ref[:n, :] = w_ref[:n, :]
        p_ref[n : n + K, :] = west
        q_ref[:n, :] = e_ref[:n, :]
        q_ref[n : n + K, :] = east

    d = D * K
    for ref in (p_ref, q_ref):
        for half in range(2):
            t = slice(128 * half, 128 * half + 128)
            base = n + K + half * (n - K)
            ref[base : base + d, :] = yr_ref[:d, t]
            ref[base + d : base + n - K, :] = yr_ref[d + K :, t]
            ref[d + 2 + 2 * half : d + 4 + 2 * half, :] = yr_ref[d : d + 2, t]


def line_tendency(line, along, across, velocity, prev, nxt):
    n = line.shape[1]
    lane = lax.broadcasted_iota(jnp.int32, (K, 128), 1)

    def before(x, edge):
        moved = pltpu.roll(x, 1, 1)
        first = jnp.where(lane == 0, edge, moved[:, :128])
        return first if n == 128 else jnp.concatenate([first, moved[:, 128:]], axis=1)

    def after(x, edge):
        moved = pltpu.roll(x, n - 1, 1)
        last = jnp.where(lane == 127, edge, moved[:, -128:])
        return last if n == 128 else jnp.concatenate([moved[:, :-128], last], axis=1)

    def wide(x, i):
        return jnp.broadcast_to(x[i : i + 1], x.shape)

    d, wet, vel = slab(line, D), slab(line, WET), slab(line, velocity)
    al, ac = wide(d, along), wide(d, across)
    al_n, ac_n = after(al, wide(nxt["d"], along)), after(ac, wide(nxt["d"], across))
    al_p, ac_p = before(al, wide(prev["d"], along)), before(ac, wide(prev["d"], across))
    pn, qn = coefs(vel, wet, after(wet, nxt["w"]), ac, ac_n, al, al_n)
    pp, qp = coefs(before(vel, prev["vel"]), before(wet, prev["w"]), wet, ac_p, ac, al_p, al)
    out = []
    for t in range(2):
        C = slab(line, t)
        ahead = pn * C + qn * after(C, nxt["c"][t])
        behind = pp * before(C, prev["c"][t]) + qp * C
        out.append(ahead - behind)
    return out, (pn, qn, pp, qp)


def face_fluxes(own, ghost, own_vel_is_low, vel, ghost_vel, along, across, own_line, ghost_line):
    d, g = slab(own, D), slab(ghost, D)

    def face(velocity):
        lo, hi = (own, ghost) if own_vel_is_low else (ghost, own)
        dl, dh = (d, g) if own_vel_is_low else (g, d)
        return coefs(
            velocity,
            slab(lo, WET),
            slab(hi, WET),
            dl[across : across + 1],
            dh[across : across + 1],
            dl[along : along + 1],
            dh[along : along + 1],
        )

    def through(pq, a, b):
        return pq[0] * a + pq[1] * b if own_vel_is_low else pq[0] * b + pq[1] * a

    pq = face(vel)
    pq_ghost = pq if ghost_vel is None else face(ghost_vel)
    vol_own = d[0:1] * d[1:2] * slab(own, TH)
    vol_ghost = g[0:1] * g[1:2] * slab(ghost, TH)
    one, two = [], []
    for t in range(2):
        a, b = slab(own, t), slab(ghost, t)
        f = through(pq, a, b)
        fg = f if ghost_vel is None else through(pq_ghost, a, b)
        if own_vel_is_low:
            own_div = own_line[t] + (f - slab(own, F0 + t))
            ghost_div = ghost_line[t] + (slab(ghost, F0 + t) - fg)
        else:
            own_div = own_line[t] + (slab(own, F0 + t) - f)
            ghost_div = ghost_line[t] + (fg - slab(ghost, F0 + t))
        a2 = a - STEP * own_div / vol_own
        b2 = b - STEP * ghost_div / vol_ghost
        one.append(f)
        two.append(through(pq, a2, b2))
    return one, two


def correction(own, face_coefs, first, second):
    pn, qn, pp, qp = face_coefs
    d = slab(own, D)
    r = (-0.5 * STEP) / (d[0:1] * d[1:2] * slab(own, TH))
    delta = (2.0 * r) * first
    n = delta.shape[1]
    out = r * (first + second) + (r * (slab(own, SELF) + pn - qp)) * delta
    out = out + (r * qn) * pltpu.roll(delta, n - 1, 1) - (r * pp) * pltpu.roll(delta, 1, 1)
    return jnp.where(slab(own, WET) > 0, out, 0.0), slab(own, BESIDE) * delta


def window(rows, partner, first):
    width = rows.shape[1]
    lon, total = lax.axis_index("lon"), lax.axis_size("lon") * width
    off = jnp.broadcast_to(partner[...], (K, width)) - (total - (lon + 1) * width)
    off = jnp.where(off < 0, off + total, off)
    before = lax.broadcasted_iota(jnp.int32, (K, 128), 1) == 0
    ends = jnp.where(before, off[:, :128] + 1, pltpu.roll(off[:, -128:], 2, 1) - 1)
    off = jnp.concatenate([off, ends], axis=1)[:1] - first
    src = lax.broadcasted_iota(jnp.int32, (width, width + 128), 0)
    chosen = (src == off).astype(f32).astype(jnp.bfloat16)
    win = None
    for _ in range(3):
        part = rows.astype(jnp.bfloat16)
        rows = rows - part.astype(f32)
        more = jnp.dot(part, chosen, preferred_element_type=f32)
        win = more if win is None else win + more
    return win


def boundary(xs, ys, xr, yr, own_w, own_e, pr, qr, partner, win_ref, fy_ref, tt_ref, flip_ref, ghost_ref):
    lat, lon = lax.axis_index("lat"), lax.axis_index("lon")
    last = lax.axis_size("lat") - 1
    even_lat, even_lon = lat % 2 == 0, lon % 2 == 0
    n = SLABS * K
    top = jnp.where(even_lat, xs[...], ys[...])
    bottom = jnp.where(even_lat, ys[...], xs[...])
    south = jnp.where(even_lat, yr[...], xr[...])
    west_all = jnp.where(even_lon, qr[...], pr[...])
    east_all = jnp.where(even_lon, pr[...], qr[...])
    west, east = west_all[:n], east_all[:n]
    cw, ce = west_all[n : n + K], east_all[n : n + K]
    w_own, e_own = own_w[...], own_e[...]
    width = top.shape[1]
    height = w_own.shape[1]

    @pl.when(lat != last)
    def _():
        ghost_ref[:n, :width] = jnp.where(even_lat, xr[...], yr[...])
        ghost_ref[n:, :width] = slab(top, V)
        tile = jnp.zeros((K, 128), f32)
        lane = lax.broadcasted_iota(jnp.int32, (K, 128), 1)
        for at, s in enumerate(CORNER):
            ends = jnp.where(lane == 0, move(cw, 8 + at, 0), tile)
            ends = jnp.where(lane == 1, move(ce, 8 + at, 1), ends)
            ghost_ref[s * K : (s + 1) * K, width:] = ends

    @pl.when(lat == last)
    def _():
        parts = []
        for half in range(2):
            base, d = n + K + half * (n - K), D * K
            dxdy = west_all[d + 2 + 2 * half : d + 4 + 2 * half]
            parts.append(
                join(west_all[base : base + d], dxdy, jnp.zeros((6, 128), f32), west_all[base + d : base + n - K])
            )
        passed_on = jnp.concatenate(parts, axis=1)
        win = win_ref[...] + window(passed_on, partner, width)
        for s in (C0, C1, WET, TH, D):
            ghost_ref[s * K : (s + 1) * K, :] = slab(win, s)
        u = slab(win, U)
        lane = lax.broadcasted_iota(jnp.int32, (K, 128), 1)
        here = pltpu.roll(u[:, :width], width - 1, 1)
        last_tile = jnp.where(lane == 127, move(u, width + 1, 127), here[:, -128:])
        ghost_ref[U * K : (U + 1) * K, :width] = -jnp.concatenate([here[:, :-128], last_tile], axis=1)
        ghost_ref[U * K : (U + 1) * K, width:] = -u[:, :128]
        for s in (F0, F1):
            ghost_ref[s * K : (s + 1) * K, :] = -slab(win, s)
        ghost_ref[n:, :width] = -slab(win, V)[:, :width]

    north = ghost_ref[:n, :width]
    north_vel = ghost_ref[n:, :width]

    def cell(get, vel, to):
        return dict(c=[get(C0, to), get(C1, to)], w=get(WET, to), d=get(D, to), vel=vel and get(vel, to))

    def end(x, at, vel, to):
        return cell(lambda s, to: move(slab(x, s), at, to), vel, to)

    def corner(x, base, vel, to):
        return cell(lambda s, to: move(x, base + CORNER.index(s), to), vel, to)

    def ghost_end(at, vel, to):
        return cell(lambda s, to: move(ghost_ref[s * K : (s + 1) * K, width:], at, to), vel, to)

    def x_line(line, prev, nxt):
        return line_tendency(line, 0, 1, U, prev, nxt)[0]

    def y_line(line, prev, nxt):
        return line_tendency(line, 1, 0, V, prev, nxt)

    line_n = x_line(north, ghost_end(0, U, 0), ghost_end(1, None, 127))
    line_s = x_line(south, corner(cw, 0, U, 0), corner(ce, 0, None, 127))
    line_top = x_line(top, end(west, height - 1, U, 0), end(east, height - 1, None, 127))
    line_bottom = x_line(bottom, end(west, 0, U, 0), end(east, 0, None, 127))
    n1, n2 = face_fluxes(top, north, True, slab(top, V), north_vel, 1, 0, line_top, line_n)
    s1, s2 = face_fluxes(bottom, south, False, slab(south, V), None, 1, 0, line_bottom, line_s)
    closed = lat == 0
    for i, value in enumerate((*s1, *s2)):
        fy_ref[i * K : (i + 1) * K, :] = jnp.where(closed, 0.0, value)
    for i, value in enumerate((*n1, *n2)):
        fy_ref[(4 + i) * K : (5 + i) * K, :] = value

    line_w, _ = y_line(west, corner(cw, 0, V, 0), ghost_end(0, None, 127))
    line_e, _ = y_line(east, corner(ce, 0, V, 0), ghost_end(1, None, 127))
    own_line_w, coef_w = y_line(w_own, end(south, 0, V, 0), end(north, 0, None, 127))
    own_line_e, coef_e = y_line(e_own, end(south, width - 1, V, 0), end(north, width - 1, None, 127))
    e1, e2 = face_fluxes(e_own, east, True, slab(e_own, U), None, 0, 1, own_line_e, line_e)
    w1, w2 = face_fluxes(w_own, west, False, slab(west, U), None, 0, 1, own_line_w, line_w)
    for n in range(2):
        west_out, west_in = correction(w_own, coef_w, -w1[n], -w2[n])
        east_out, east_in = correction(e_own, coef_e, e1[n], e2[n])
        for at, value in enumerate((east_in, east_out, west_out, west_in)):
            flip_ref[pl.ds(4 * K * n + at, K, stride=4), :] = value
    for j, (ea, we) in enumerate(zip((*e1, *e2), (*w1, *w2))):
        flip_ref[pl.ds(64 + 2 * K * j, K, stride=2), :] = ea
        flip_ref[pl.ds(65 + 2 * K * j, K, stride=2), :] = we
    tt_ref[...] = flip_ref[...].T


TILES = (slice(0, 128), slice(128, 256))


def chunk(c):
    return slice(8 * c, 8 * c + 8)


def both(ref, c, *lead):
    return [ref[(*lead, chunk(c), t)] for t in TILES]


def lanes():
    return lax.broadcasted_iota(jnp.int32, (8, 128), 1)


def subs():
    return lax.broadcasted_iota(jnp.int32, (8, 128), 0)


def east_of(x):
    moved = [pltpu.roll(v, 127, 1) for v in x]
    return [jnp.where(lanes() == 127, moved[1], moved[0]), moved[1]]


def west_of(x):
    moved = [pltpu.roll(v, 1, 1) for v in x]
    return [moved[0], jnp.where(lanes() == 0, moved[0], moved[1])]


def up_rolled(x):
    return [pltpu.roll(v, 7, 0) for v in x]


def down_rolled(x):
    return [pltpu.roll(v, 1, 0) for v in x]


def pick(mask, x, y):
    return [jnp.where(mask, a, b) for a, b in zip(x, y)]


def tendency(x, x_n, x_s, m):
    x_e, x_w = east_of(x), west_of(x)
    return [
        (m[0][i] * x[i] + m[1][i] * x_e[i]) + (m[2][i] * x_w[i] + m[3][i] * x_n[i]) + m[4][i] * x_s[i]
        for i in range(2)
    ]


def apply(load, m_ref, k, chunks, write):
    x = load(0)
    up = up_rolled(x)
    below = x
    for c in range(chunks):
        x_next = load(c + 1) if c + 1 < chunks else x
        up_next, down = up_rolled(x_next), down_rolled(x)
        x_n, x_s = pick(subs() == 7, up_next, up), pick(subs() == 0, below, down)
        tend = tendency(x, x_n, x_s, [both(m_ref, c, j, k) for j in range(5)])
        for i, t in enumerate(TILES):
            write(c, i, t, x[i], tend[i])
        x, up, below = x_next, up_next, down


def prep_kernel(
    t_ref, u_ref, v_ref, th_ref, sea_ref, dx_ref, dy_ref, w_ref, e_ref, m_ref, geo, acc0, acc1, flip0, flip1
):
    rows = dx_ref.shape[0]
    chunks = rows // 8

    def columns(c, carry):
        at = pl.ds(pl.multiple_of(8 * c, 8), 8)
        lane = lanes()

        def put(acc, slot, left, right):
            moved = pltpu.roll(jnp.where(lane < 64, left, right), (4 * slot + 2) % 128, 1)
            return moved if acc is None else jnp.where(lane >> 2 == slot, moved, acc)

        def ends(ref, *lead):
            return ref[(*lead, at, TILES[0])], ref[(*lead, at, TILES[-1])]

        one = two = None
        for k in range(K):
            th = ends(th_ref, k)
            wet = [a * b.astype(f32) for a, b in zip(th, ends(sea_ref, k))]
            for q, value in enumerate((ends(t_ref, 0, k), ends(t_ref, 1, k), wet, ends(u_ref, k))):
                one = put(one, q * K + k, *value)
            for q, value in enumerate((ends(v_ref, k), th)):
                two = put(two, q * K + k, *value)
        two = put(two, 2 * K, *ends(dx_ref))
        two = put(two, 2 * K + 1, *ends(dy_ref))
        acc0[at, :] = one
        acc1[at, :] = two
        return carry

    lax.fori_loop(0, chunks, columns, 0, unroll=8)
    flip0[...] = acc0[...].T
    flip1[...] = acc1[...].T
    places = {C0: (flip0, 0), C1: (flip0, 1), WET: (flip0, 2), U: (flip0, 3), V: (flip1, 0), TH: (flip1, 1)}
    for out, near, far in ((w_ref, 2, 3), (e_ref, 1, 0)):

        def get(s, at):
            ref, q = places[s]
            return ref[pl.ds(4 * K * q + at, K, stride=4), :]

        d1 = flip1[pl.ds(8 * K + near, 2, stride=4), :]
        d2 = flip1[pl.ds(8 * K + far, 2, stride=4), :]
        low, high = min(near, far), max(near, far)
        da, db = (d1, d2) if near < far else (d2, d1)
        p, q = coefs(get(U, low), get(WET, low), get(WET, high), da[1:2], db[1:2], da[0:1], db[0:1])
        for s in (C0, C1, WET, U, V, TH):
            out[s * K : (s + 1) * K, :] = get(s, near)
        out[D * K : (D + 1) * K, :] = join(d1, jnp.zeros((6, rows), f32))
        for n in range(2):
            out[(F0 + n) * K : (F0 + n + 1) * K, :] = p * get(n, low) + q * get(n, high)
        mine = p if near < far else -q
        r = (-0.5 * STEP) / (d2[0:1] * d2[1:2] * get(TH, far))
        out[SELF * K : (SELF + 1) * K, :] = mine
        out[BESIDE * K : (BESIDE + 1) * K, :] = jnp.where(get(WET, far) > 0, -r * mine, 0.0)

    for c in range(chunks):
        n = min(c + 1, chunks - 1)
        dx, dy = both(dx_ref, c), both(dy_ref, c)
        dx_e, dy_e = east_of(dx), east_of(dy)
        dx_n, dy_n = (pick(subs() == 7, up_rolled(both(r, n)), up_rolled(x)) for r, x in ((dx_ref, dx), (dy_ref, dy)))
        for i, t in enumerate(TILES):
            geo[0, chunk(c), t] = 0.5 * (dy[i] + dy_e[i])
            geo[1, chunk(c), t] = 0.5 / (dx[i] + dx_e[i])
            geo[2, chunk(c), t] = 0.5 * (dx[i] + dx_n[i])
            geo[3, chunk(c), t] = 0.5 / (dy[i] + dy_n[i])
            geo[4, chunk(c), t] = (-0.5 * STEP) / (dx[i] * dy[i])

    def level(k, carry):
        def wet(c):
            return [a * b.astype(f32) for a, b in zip(both(th_ref, c, k), both(sea_ref, c, k))]

        w = wet(0)
        up = up_rolled(w)
        zero = jnp.zeros((8, 128), f32)
        p_below, q_below = [zero, zero], [zero, zero]
        for c in range(chunks):
            w_next = wet(c + 1) if c + 1 < chunks else w
            up_next = up_rolled(w_next)
            w_e, w_n = east_of(w), pick(subs() == 7, up_next, up)
            u, v, th = both(u_ref, c, k), both(v_ref, c, k), both(th_ref, c, k)
            gx, ex, gy, ey, dd = [both(geo, c, j) for j in range(5)]
            a, b, p, q = [], [], [], []
            for i in range(2):
                g, h = gx[i] * jnp.minimum(w[i], w_e[i]), 0.5 * u[i]
                if i == 1:
                    g = jnp.where(lanes() == 127, 0.0, g)
                a.append(g * (h + ex[i]))
                b.append(g * (h - ex[i]))
                g, h = gy[i] * jnp.minimum(w[i], w_n[i]), 0.5 * v[i]
                if c == chunks - 1:
                    g = jnp.where(subs() == 7, 0.0, g)
                p.append(g * (h + ey[i]))
                q.append(g * (h - ey[i]))
            a_w, b_w = west_of(a), west_of(b)
            a_w[0], b_w[0] = (jnp.where(lanes() == 0, 0.0, y[0]) for y in (a_w, b_w))
            p_down, q_down = down_rolled(p), down_rolled(q)
            p_s, q_s = pick(subs() == 0, p_below, p_down), pick(subs() == 0, q_below, q_down)
            for i, t in enumerate(TILES):
                r = dd[i] / th[i]
                m_ref[0, k, chunk(c), t] = r * ((a[i] - b_w[i]) + (p[i] - q_s[i]))
                m_ref[1, k, chunk(c), t] = r * b[i]
                m_ref[2, k, chunk(c), t] = -r * a_w[i]
                m_ref[3, k, chunk(c), t] = r * q[i]
                m_ref[4, k, chunk(c), t] = -r * p_s[i]
                m_ref[5, k, chunk(c), t] = r
            w, up, p_below, q_below = w_next, up_next, p_down, q_down
        return carry

    lax.fori_loop(0, K, level, 0)


def stages_kernel(partner, yr, t_ref, sea_ref, m_ref, sec_ref, res_ref, win_ref):
    @pl.when(lax.axis_index("lat") == lax.axis_size("lat") - 1)
    def _():
        win_ref[...] = window(yr[...], partner, 0)

    chunks = sea_ref.shape[1] // 8

    def level(k, carry):
        for n in range(2):

            def write(c, i, t, x, tend):
                sec_ref[n, k, chunk(c), t] = x + 2.0 * tend

            apply(lambda c: both(t_ref, c, n, k), m_ref, k, chunks, write)
        for n in range(2):

            def write(c, i, t, x, tend):
                total = 0.5 * (t_ref[n, k, chunk(c), t] + x) + tend
                res_ref[n, k, chunk(c), t] = jnp.where(sea_ref[k, chunk(c), t] > 0, total, 0.0)

            apply(lambda c: both(sec_ref, c, n, k), m_ref, k, chunks, write)
        return carry

    lax.fori_loop(0, K, level, 0, unroll=4)


def final_kernel(
    partner, win_ref, t_ref, sea_ref, m_ref, sec_ref, res_ref, xs, ys, xr, yr, own_w, own_e, pr, qr,
    out_ref, fy_ref, tt_ref, flip_ref, ghost_ref, done, sems,
):
    rows = sea_ref.shape[1]
    chunks = rows // 8
    boundary(xs, ys, xr, yr, own_w, own_e, pr, qr, partner, win_ref, fy_ref, tt_ref, flip_ref, ghost_ref)
    lane, sub = lanes(), subs()

    def edges(n, s, k, c):
        def row(i):
            r = fy_ref[pl.ds((4 * i + 2 * s + n) * K + k, 1), :]
            return [jnp.broadcast_to(r[:, t], (8, 128)) for t in TILES]

        ends = pltpu.roll(tt_ref[chunk(c), :], 63 - 2 * ((2 * s + n) * K + k), 1)
        out = [jnp.where(lane == 0, -ends, 0.0), jnp.where(lane == 127, ends, 0.0)]
        if c == 0:
            out = [o - jnp.where(sub == 0, f, 0.0) for o, f in zip(out, row(0))]
        if c == chunks - 1:
            out = [o + jnp.where(sub == 7, f, 0.0) for o, f in zip(out, row(1))]
        return out

    def copy(k):
        return pltpu.make_async_copy(done.at[:, pl.ds(k, 1)], out_ref.at[:, pl.ds(k, 1)], sems.at[k])

    def level(k, carry):
        for n in range(2):

            def section(c):
                r, x, add = both(m_ref, c, 5, k), both(sec_ref, c, n, k), edges(n, 0, k, c)
                return [x[i] + 2.0 * (r[i] * add[i]) for i in range(2)]

            for c, beside in ((0, 1), (chunks - 1, chunks - 2)):
                x, y = section(c), section(beside)
                x_n, x_s = up_rolled(x), down_rolled(x)
                if c == 0:
                    x_n = pick(sub == 7, up_rolled(y), x_n)
                else:
                    x_s = pick(sub == 0, down_rolled(y), x_s)
                tend = tendency(x, x_n, x_s, [both(m_ref, c, j, k) for j in range(5)])
                add, r = edges(n, 1, k, c), both(m_ref, c, 5, k)
                for i, t in enumerate(TILES):
                    total = 0.5 * (t_ref[n, k, chunk(c), t] + x[i]) + (tend[i] + r[i] * add[i])
                    done[n, k, chunk(c), t] = jnp.where(sea_ref[k, chunk(c), t] > 0, total, 0.0)
            for c in range(1, chunks - 1):
                ends = pltpu.roll(tt_ref[chunk(c), :], 126 - 4 * (n * K + k), 1)
                left, right = TILES
                done[n, k, chunk(c), left] = res_ref[n, k, chunk(c), left] + jnp.where(lane < 2, ends, 0.0)
                done[n, k, chunk(c), right] = res_ref[n, k, chunk(c), right] + jnp.where(lane > 125, ends, 0.0)
        copy(k).start()
        return carry

    lax.fori_loop(0, K, level, 0, unroll=2)
    for k in range(K):
        copy(k).wait()


def pairs(count_lon, count_lat, partner):
    out = []
    for o in range(count_lon):
        for a in range(count_lat):
            to = partner(o, a)
            if to is not None:
                source, target = o * count_lat + a, (to[0] % count_lon) * count_lat + to[1]
                if source != target:
                    out.append((source, target))
    return out


def shards(nlon, nlat, tracers, zonal_vel, merid_vel, thickness, land_sea, cell_dx, cell_dy, fold_partner):
    rows, cols = cell_dx.shape
    axes = ("lon", "lat")
    end = nlat - 1

    def swap(x, partner):
        return lax.ppermute(x, axes, pairs(nlon, nlat, partner))

    def y_partner(o, a):
        if a == 0:
            return None
        if a == end:
            return (nlon - 1 - o, a)
        return (o, a + 1) if a % 2 else (o, a - 1)

    fields = (tracers, zonal_vel, merid_vel, thickness, land_sea, cell_dx, cell_dy)
    n = SLABS * K

    vmem = pl.BlockSpec(memory_space=pltpu.VMEM)

    def edge(r):
        return [
            pl.BlockSpec((2, K, 8, cols), lambda i: (0, 0, r, 0)),
            *[pl.BlockSpec((K, 8, cols), lambda i: (0, r, 0))] * 4,
            *[pl.BlockSpec((8, cols), lambda i: (r, 0))] * 2,
        ]

    whole = pl.BlockSpec((n, cols), lambda i: (0, 0))
    line = jax.ShapeDtypeStruct((n, cols), f32)
    xs, ys = pl.pallas_call(
        rows_kernel,
        grid=(1,),
        in_specs=[*edge(0), *edge(rows // 8 - 1)],
        out_specs=[vmem] * 2,
        out_shape=[line] * 2,
        compiler_params=pltpu.CompilerParams(vmem_limit_bytes=8 << 20),
        name="edge_rows",
    )(*[pltpu.with_memory_space_constraint(x, pltpu.HBM) for x in (*fields, *fields)])
    xr = swap(xs, lambda o, a: (o, a ^ 1))
    yr = swap(ys, y_partner)

    whole_field = (K, rows, cols)
    side = jax.ShapeDtypeStruct((n + 2 * K, rows), f32)
    own_w, own_e, m = pl.pallas_call(
        prep_kernel,
        in_specs=[vmem] * 7,
        out_specs=[vmem] * 3,
        out_shape=[side, side, jax.ShapeDtypeStruct((6, *whole_field), f32)],
        scratch_shapes=[pltpu.VMEM((5, rows, cols), f32)] + [pltpu.VMEM((rows, 128), f32)] * 2 + [pltpu.VMEM((128, rows), f32)] * 2,
        cost_estimate=pl.CostEstimate(flops=10_000_000, bytes_accessed=10_000_000, transcendentals=0),
        compiler_params=pltpu.CompilerParams(vmem_limit_bytes=18 << 20),
        name="prep",
    )(*fields)
    message = jax.ShapeDtypeStruct((n + K + 2 * (n - K), 128), f32)
    ps, qs = pl.pallas_call(
        corners_kernel,
        out_shape=[message, message],
        compiler_params=pltpu.CompilerParams(vmem_limit_bytes=8 << 20),
        name="corners",
    )(xr, yr, own_w, own_e)
    qr = swap(qs, lambda o, a: (o + 1, a) if o % 2 else (o - 1, a))
    pr = swap(ps, lambda o, a: (o ^ 1, a))

    field = jax.ShapeDtypeStruct((2, *whole_field), f32)
    partner = fold_partner.reshape(1, cols)
    sec, res, win = pl.pallas_call(
        stages_kernel,
        in_specs=[vmem] * 5,
        out_specs=[vmem] * 3,
        out_shape=[field, field, jax.ShapeDtypeStruct((n, cols + 128), f32)],
        cost_estimate=pl.CostEstimate(flops=20_000_000, bytes_accessed=14_000_000, transcendentals=0),
        compiler_params=pltpu.CompilerParams(vmem_limit_bytes=18 << 20),
        name="stages",
    )(partner, yr, tracers, land_sea, m)
    return pl.pallas_call(
        final_kernel,
        in_specs=[vmem] * 15,
        out_specs=pl.BlockSpec(memory_space=pl.ANY),
        out_shape=jax.ShapeDtypeStruct(tracers.shape, f32),
        scratch_shapes=[
            pltpu.VMEM((8 * K, cols), f32),
            pltpu.VMEM((rows, 128), f32),
            pltpu.VMEM((128, rows), f32),
            pltpu.VMEM((n + K, cols + 128), f32),
            pltpu.VMEM((2, *whole_field), f32),
            pltpu.SemaphoreType.DMA((K,)),
        ],
        cost_estimate=pl.CostEstimate(flops=20_000_000, bytes_accessed=14_000_000, transcendentals=0),
        compiler_params=pltpu.CompilerParams(vmem_limit_bytes=18 << 20),
        name="final",
    )(partner, win, tracers, land_sea, m, sec, res, xs, ys, xr, yr, own_w, own_e, pr, qr)


def solution(mesh):
    return jax.shard_map(
        functools.partial(shards, mesh.shape["lon"], mesh.shape["lat"]),
        mesh=mesh,
        in_specs=(
            P(None, None, "lat", "lon"),
            P(None, "lat", "lon"),
            P(None, "lat", "lon"),
            P(None, "lat", "lon"),
            P(None, "lat", "lon"),
            P("lat", "lon"),
            P("lat", "lon"),
            P("lon"),
        ),
        out_specs=P(None, None, "lat", "lon"),
        check_vma=False,
    )
```
